256 devices in a mesh: mp: 16 (over y, x_hi, core), shard: 16 (over z, x_lo).
Axes of the slice: x: 4 (x_hi: 2, x_lo: 2; x = x_hi * 2 + x_lo), y: 4, z: 8, core: 2. Of those that a mesh axis runs over, the one named last changes fastest.
Arguments:
- bank: bfloat16 [4096, 8192], P('shard'), may hold values from -6 to 6
- calib_ids: int32 [16, 1024], P('mp', 'shard'), may hold values from 0 to 4095, as said below
- norm_gains: float32 [16, 8192], P('mp'), may hold values from 0.5 to 1.5
- proj_slabs: bfloat16 [16, 8192, 512], P('mp', 'shard'), may hold values from -0.0625 to 0.0625
Outputs:
- merged_gram: float32 [8192, 8192], P('mp', 'shard')
- numer: float32 [8192, 512], P('shard')
The draws below stay inside these ranges and needn't reach their ends.
Inputs may be any that keep to these rules, and one draw needn't show every extreme that they name: `calib_ids`: token t of every model names a bank row in block t // 64, rows (t // 64) * 256 to (t // 64) * 256 + 255.
All inputs are finite; a program needn't handle non-finite values.
Results may differ from the reference program's by a relative error of at most 0.0048.
Values may be sent and summed in bfloat16 or wider, within the bound.
No kernel may reach another device: no remote copies, remote signals or barrier semaphores. Data moves between devices by JAX's collectives and lax.ppermute only.
A program may use at most 128 MiB of HBM per device.

```python
import jax
import jax.numpy as jnp
from jax import lax

D = 8192
S = 512
TOK_DEV = 64
BANK_DEV = 256
MODELS = 16
TOKENS = 1024
BANK = 4096


def draw_calib_ids(key, part):
    offsets = jax.random.randint(key, (MODELS, TOKENS), 0, BANK_DEV, dtype=jnp.int32)
    token_pos = jnp.arange(TOKENS, dtype=jnp.int32)[None, :]
    model_pos = jnp.arange(MODELS, dtype=jnp.int32)[:, None]
    within = token_pos % TOK_DEV
    offsets = jnp.where((model_pos == 0) & (within == 0), 0, offsets)
    offsets = jnp.where((model_pos == 0) & (within == TOK_DEV - 1), BANK_DEV - 1, offsets)
    return token_pos // TOK_DEV * BANK_DEV + offsets


def block_levels(key, dims, cuts, least, high):
    gain = 1.0
    for axis_at, parts in cuts:
        draws = jax.random.uniform(jax.random.fold_in(jax.random.fold_in(key, 6), axis_at), (parts,), jnp.float32, least / len(cuts), high / len(cuts))
        gain = gain * jnp.repeat(jnp.exp(draws), dims[axis_at] // parts).reshape((-1,) + (1,) * (len(dims) - 1 - axis_at))
    return gain


def normal_values(key, extent, width, reach, split=(), held_as=jnp.bfloat16):
    drawn = jax.random.normal(key, extent, jnp.float32) * width
    if len(split) > 0:
        drawn = block_levels(key, extent, split, -0.22, 0.18) * drawn
    return jnp.clip(drawn, min=-reach, max=reach).astype(held_as)


def setup_inputs(seed: int = 0) -> dict:
    key_list = jax.random.split(jax.random.key(seed), 5)
    bank = normal_values(key_list[0], (BANK, D), 1.0, 6.0, ((0, 16),))
    calib_ids = draw_calib_ids(jax.random.fold_in(key_list[4], 71), 0)
    norm_gains = jnp.clip(1.0 + 0.1 * jax.random.normal(key_list[2], (MODELS, D), jnp.float32), 0.5, 1.5)
    proj_slabs = normal_values(key_list[3], (MODELS, D, S), D ** -0.5, 0.0625, ((0, 16), (1, 16)))
    return dict(bank=bank, calib_ids=calib_ids, norm_gains=norm_gains, proj_slabs=proj_slabs)


ALPHA = 0.9
EPSILON = 1e-05

def features(bank, ids_model, gain_model):
    bank_rows = bank[ids_model].astype(jnp.float32)
    mean_square = lax.optimization_barrier(jnp.mean(bank_rows * bank_rows, axis=-1, keepdims=True))
    normed = bank_rows * lax.rsqrt(mean_square + EPSILON) * gain_model.astype(jnp.float32)[None, :]
    return normed.astype(jnp.bfloat16)

def reference(bank, calib_ids, norm_gains, proj_slabs):
    merged_gram = jnp.zeros((D, D), jnp.float32)
    numer = jnp.zeros((D, S), jnp.float32)
    for model in range(MODELS):
        calib = features(bank, calib_ids[model], norm_gains[model]).astype(jnp.float32)
        gram_model = jnp.dot(calib.T, calib, precision=lax.Precision.HIGHEST) / TOKENS
        diag_part = jnp.diagonal(gram_model)
        merged_gram = merged_gram + ALPHA * gram_model + (1.0 - ALPHA) * jnp.diag(diag_part)
        weight_slab = proj_slabs[model].astype(jnp.float32)
        model_out = jnp.dot(calib, weight_slab, precision=lax.Precision.HIGHEST).astype(jnp.bfloat16).astype(jnp.float32)
        numer = numer + ALPHA * jnp.dot(calib.T, model_out, precision=lax.Precision.HIGHEST) / TOKENS
        numer = numer + (1.0 - ALPHA) * diag_part[:, None] * weight_slab
    return (merged_gram, numer)
```

```python
import jax
import jax.numpy as jnp
from jax import lax
from jax.sharding import PartitionSpec as P

ALPHA = 0.9
EPSILON = 1e-05
BF = jnp.bfloat16
F4 = jnp.float32
AXES = ("mp", "shard")
Z_GROUPS = [[z * 2 + xl for z in range(8)] for xl in range(2)]
CORE_GROUPS = [[q * 2 + c for q in range(8)] for c in range(2)]


def shift(x, y=0, xh=0, c=0, z=0, xl=0):
    pairs = []
    for p in range(16):
        for s in range(16):
            py, pxh, pc = p // 4, p // 2 % 2, p % 2
            sz, sxl = s // 2, s % 2
            tp = (py + y) % 4 * 4 + (pxh ^ xh) * 2 + (pc ^ c)
            ts = (sz + z) % 8 * 2 + (sxl ^ xl)
            pairs.append((p * 16 + s, tp * 16 + ts))
    return lax.ppermute(x, AXES, pairs)


def swap_z(x):
    return lax.all_to_all(x, "shard", 0, 0, tiled=True, axis_index_groups=Z_GROUPS)


def dot(a, b):
    return jnp.dot(a, b, preferred_element_type=F4)


def split3(v):
    hi = lax.reduce_precision(v, 8, 7)
    mid = lax.reduce_precision(v - hi, 8, 7)
    return hi.astype(BF), mid.astype(BF), (v - hi - mid).astype(BF)


def gather_mp(x):
    half = x.shape[0] // 2
    h = shift(x, xh=1)
    u = shift(x, y=1)
    d = shift(x, y=-1)
    hu = shift(h, y=1)
    hd = shift(h, y=-1)
    t = jnp.concatenate([shift(u[:half], y=1), shift(d[half:], y=-1)], 0)
    ht = shift(t, xh=1)
    own = jnp.stack([x, h, d, hd, t, ht, u, hu], 0)
    return own, shift(own, c=1)


def gather_z(x):
    u, d = [x], [x]
    for _ in range(3):
        u.append(shift(u[-1], z=1))
        d.append(shift(d[-1], z=-1))
    far = jnp.concatenate([shift(u[3][:128], z=1), shift(d[3][128:], z=-1)], 0)
    return jnp.stack([x, d[1], d[2], d[3], far, u[3], u[2], u[1]], 0)


def local(bank, calib_ids, norm_gains, proj_slabs):
    p = lax.axis_index("mp")
    s = lax.axis_index("shard")
    y, xh, c = p // 4, p // 2 % 2, p % 2
    z, xl = s // 2, s % 2
    weights = proj_slabs[0]
    ids = calib_ids[0] - s * 256
    gains = norm_gains[0]

    def order_cols(x):
        n = x.shape[0]
        x = x.reshape(n, 8, 2, 512)
        x = jnp.where(xl == 0, x, x[:, :, ::-1])
        return x.reshape(n, 8, 1024).transpose(1, 0, 2)

    lane = lax.broadcasted_iota(jnp.int32, (64, 256), 1)
    pick = (ids[:, None] == lane).astype(BF)
    rows = dot(pick, bank)
    mean_square = jnp.mean(rows * rows, axis=-1, keepdims=True)
    calib_own = (rows * lax.rsqrt(mean_square + EPSILON) * gains[None, :]).astype(BF)
    cols = swap_z(order_cols(calib_own)).reshape(512, 1024)

    packed = jnp.concatenate([gains, ids.astype(F4), jnp.zeros((960,), F4)]).reshape(72, 128)
    packed = lax.all_to_all(jnp.broadcast_to(packed[None], (16, 72, 128)), "mp", 0, 0, tiled=True)
    gains_all = packed[:, :64].reshape(16, 8192)
    ids_all = packed[:, 64, :64].astype(jnp.int32)

    piece = lax.dynamic_slice_in_dim(bank, p * 16, 16, 0)
    piece = swap_z(order_cols(piece))
    piece = lax.dynamic_slice_in_dim(jnp.concatenate([piece, piece], 0), z, 8, 0)
    own_s, other_s = gather_mp(piece)
    bank_s = jnp.concatenate([own_s, other_s], 0).transpose(1, 0, 2, 3).reshape(8, 256, 1024)

    bank_f = bank.astype(F4)
    row_scale = lax.rsqrt(jnp.mean(bank_f * bank_f, axis=-1) + EPSILON)
    lane3 = lax.broadcasted_iota(jnp.int32, (16, 64, 256), 2)
    hit = ids_all[:, :, None] == lane3
    scale_all = jnp.sum(jnp.where(hit, row_scale[None, None, :], 0.0), -1)

    def relative(row):
        q = row // 16
        return ((q % 2) ^ c) * 128 + ((q // 4 - y) % 4) * 32 + ((q // 2 % 2) ^ xh) * 16 + row % 16

    sub = lax.broadcasted_iota(jnp.int32, (256, 256), 0)
    src = lax.broadcasted_iota(jnp.int32, (256, 256), 1)
    reorder = (relative(src) == sub).astype(BF)
    bank_p = dot(reorder, lax.dynamic_slice_in_dim(bank, p * 512, 512, 1)).astype(BF)
    hi, mid, lo = split3(scale_all)
    extra = jnp.stack([relative(ids_all).astype(BF), hi, mid, lo], 0).reshape(8, 512)
    block = jnp.concatenate([bank_p, extra, jnp.zeros((8, 512), BF)], 0)
    blocks = gather_z(block)
    bank_pz = blocks[:, :256]
    ids_z = blocks[:, 256:258].reshape(8, 1024).astype(jnp.int32)
    scale_z = blocks[:, 258:264].astype(F4).reshape(8, 3, 1024)
    scale_z = (scale_z[:, 0] + scale_z[:, 1] + scale_z[:, 2]).reshape(8, 16, 64, 1)
    gains_p = lax.dynamic_slice_in_dim(gains_all, p * 512, 512, 1)
    gains_s = lax.dynamic_slice_in_dim(gains_all, z * 1024, 1024, 1).reshape(16, 2, 512)
    gains_s = jnp.where(xl == 0, gains_s, gains_s[:, ::-1]).reshape(16, 1024)
    pick_z = (ids_z[:, :, None] == lax.broadcasted_iota(jnp.int32, (8, 1024, 256), 2)).astype(BF)

    def build(table, g):
        sel = lax.dot_general(pick_z, table, (((2,), (1,)), ((0,), (0,))), preferred_element_type=F4)
        n = g.shape[1]
        out = sel.reshape(8, 16, 64, n) * scale_z * g[None, :, None, :]
        return out.astype(BF).reshape(8192, n)

    calib_p = build(bank_pz, gains_p)
    calib_s = build(bank_s, gains_s)
    gram = lax.dot_general(calib_p, calib_s, (((0,), (0,)), ((), ())), preferred_element_type=F4)
    gram = gram[:, :512] + shift(gram[:, 512:], xl=1)
    on_diag = (p == s) & (
        lax.broadcasted_iota(jnp.int32, (512, 512), 0) == lax.broadcasted_iota(jnp.int32, (512, 512), 1)
    )
    merged_gram = gram * jnp.where(on_diag, 1.0 / 1024, ALPHA / 1024)

    weights_other = shift(weights, xl=1)
    partial_out = dot(cols[:, :512], weights) + dot(cols[:, 512:], weights_other)
    partial_out = swap_z(partial_out.astype(BF).reshape(8, 64, 512))
    model_out = jnp.sum(partial_out.astype(F4), 0).astype(BF)
    out_t = lax.all_to_all(model_out.T.reshape(16, 32, 64), "mp", 0, 0, tiled=True)
    out_t = out_t.transpose(1, 0, 2).reshape(32, 1024)

    cols_f = cols.astype(F4)
    diag = jnp.sum(cols_f * cols_f, 0).reshape(8, 128)
    diag = (diag[:4] + shift(diag[4:], xl=1)).reshape(512)
    diag_term = ((1.0 - ALPHA) / 1024 * diag)[None, :] * weights.T.astype(F4)
    diag_term = lax.all_to_all(diag_term.astype(BF).reshape(16, 32, 512), "mp", 0, 0, tiled=True)
    diag_term = jnp.sum(diag_term.astype(F4), 0)

    sel = dot(hit.astype(BF).reshape(1024, 256), bank).reshape(16, 64, 8192)
    calib_all = (sel * scale_all[:, :, None] * gains_all[:, None, :]).astype(BF).reshape(1024, 8192)
    numer_t = dot(out_t, calib_all) * (ALPHA / 1024)
    numer_t = numer_t.astype(BF).reshape(32, 16, 512).transpose(1, 0, 2)
    numer_t = lax.all_to_all(numer_t, "shard", 0, 0, tiled=True)
    numer_t = jnp.sum(numer_t.astype(F4), 0) + diag_term
    mine = lax.all_to_all(
        jnp.broadcast_to(numer_t[None], (8, 32, 512)), "mp", 0, 0, tiled=True, axis_index_groups=CORE_GROUPS
    )
    theirs = shift(mine, c=1)
    both = jnp.where(c == 0, jnp.stack([mine, theirs], 1), jnp.stack([theirs, mine], 1))
    numer = both.reshape(512, 512).T
    return (merged_gram, numer)


def solution(mesh):
    placed = (P("shard", None), P("mp", "shard"), P("mp", None), P("mp", "shard", None))
    return jax.shard_map(
        local,
        mesh=mesh,
        in_specs=placed,
        out_specs=(P("mp", "shard"), P("shard", None)),
        check_vma=False,
    )
```

```python
import jax
import jax.numpy as jnp
from jax import lax
from jax.experimental import pallas as pl
from jax.experimental.pallas import tpu as pltpu
from jax.sharding import PartitionSpec as P

ALPHA = 0.9
EPSILON = 1e-05
BF = jnp.bfloat16
F4 = jnp.float32
AXES = ("mp", "shard")
Z_GROUPS = [[z * 2 + xl for z in range(8)] for xl in range(2)]
CORE_GROUPS = [[q * 2 + c for q in range(8)] for c in range(2)]


def shift(x, y=0, xh=0, c=0, z=0, xl=0):
    pairs = []
    for p in range(16):
        for s in range(16):
            py, pxh, pc = p // 4, p // 2 % 2, p % 2
            sz, sxl = s // 2, s % 2
            tp = (py + y) % 4 * 4 + (pxh ^ xh) * 2 + (pc ^ c)
            ts = (sz + z) % 8 * 2 + (sxl ^ xl)
            pairs.append((p * 16 + s, tp * 16 + ts))
    return lax.ppermute(x, AXES, pairs)


def swap_z(x):
    return lax.all_to_all(x, "shard", 0, 0, tiled=True, axis_index_groups=Z_GROUPS)


def dot(a, b):
    return jnp.dot(a, b, preferred_element_type=F4)


def contract_rows(a, b):
    return lax.dot_general(a, b, (((0,), (0,)), ((), ())), preferred_element_type=F4)


def gather_mp(x):
    half = x.shape[0] // 2
    h = shift(x, xh=1)
    u = shift(x, y=1)
    d = shift(x, y=-1)
    hu = shift(h, y=1)
    hd = shift(h, y=-1)
    t = jnp.concatenate([shift(u[:half], y=1), shift(d[half:], y=-1)], 0)
    ht = shift(t, xh=1)
    own = jnp.stack([x, h, d, hd, t, ht, u, hu], 0)
    return own, shift(own, c=1)


def gather_z(x):
    u, d = [x], [x]
    for _ in range(3):
        u.append(shift(u[-1], z=1))
        d.append(shift(d[-1], z=-1))
    far = [shift(u[3][:128], z=1), shift(d[3][128:], z=-1)]
    return [x, d[1], d[2], d[3]] + far + [u[3], u[2], u[1]]


def prepare_kernel(info, bank, ids, gains, calib_out, piece_out, rows):
    p, xl = info[0], info[1]
    pick = (ids[...] == lax.broadcasted_iota(jnp.int32, (64, 256), 1)).astype(BF)

    def take(b, total):
        at = pl.multiple_of(b * 512, 512)
        got = dot(pick, bank[:, pl.ds(at, 512)])
        rows[b] = got
        return total + jnp.sum(got * got, axis=1, keepdims=True)

    total = lax.fori_loop(0, 16, take, jnp.zeros((64, 1), F4))
    scale = lax.rsqrt(total / 8192 + EPSILON)
    hi = scale.astype(BF).astype(F4)
    mid = (scale - hi).astype(BF).astype(F4)
    low = scale - hi - mid
    lane = lax.broadcasted_iota(jnp.int32, (16, 128), 1)
    extra = jnp.zeros((16, 128), F4)
    for q in range(4):
        part = slice(q * 16, q * 16 + 16)
        for j, v in enumerate((ids[...].astype(F4), hi, mid, low)):
            extra = jnp.where(lane == q * 32 + j, v[part], extra)
    extra = extra.astype(BF)
    own_row = pl.multiple_of(p * 16, 16)

    def emit(zz, carry):
        for j in range(2):
            b = zz * 2 + (xl ^ j)
            g = gains[pl.ds(b, 1), :]
            calib_out[zz, :, j * 512 : j * 512 + 512] = (rows[b] * scale * g).astype(BF)
            piece_out[zz, :, j * 512 : j * 512 + 512] = bank[
                pl.ds(own_row, 16), pl.ds(pl.multiple_of(b * 512, 512), 512)
            ]
        piece_out[zz, :, 1024:] = extra
        return carry

    lax.fori_loop(0, 8, emit, 0)


def prepare(info, bank, ids, gains):
    return pl.pallas_call(
        prepare_kernel,
        in_specs=[
            pl.BlockSpec(memory_space=pltpu.SMEM),
            pl.BlockSpec(memory_space=pltpu.VMEM),
            pl.BlockSpec(memory_space=pltpu.VMEM),
            pl.BlockSpec(memory_space=pltpu.VMEM),
        ],
        out_specs=[pl.BlockSpec(memory_space=pltpu.VMEM)] * 2,
        out_shape=[
            jax.ShapeDtypeStruct((8, 64, 1024), BF),
            jax.ShapeDtypeStruct((8, 16, 1152), BF),
        ],
        scratch_shapes=[pltpu.VMEM((16, 64, 512), F4)],
        compiler_params=pltpu.CompilerParams(vmem_limit_bytes=32 * 2**20),
        cost_estimate=pl.CostEstimate(flops=2**28, bytes_accessed=6 * 2**20, transcendentals=64),
        name="prepare",
    )(info, bank, ids, gains)


def gram_kernel(
    info, b0, b1, b2, b3, b4a, b4b, b5, b6, b7, own_s, other_s, gains, near, far, acc, table, pick, scale, calib
):
    k = pl.program_id(0)
    y, xh, c = info[2], info[3], info[4]

    @pl.when(k == 0)
    def _():
        acc[...] = jnp.zeros_like(acc)

    for i, b in enumerate((b0, b1, b2, b3, None, b5, b6, b7)):

        @pl.when(k == i)
        def _(b=b):
            if b is None:
                table[0:128, 0:512] = b4a[...]
                table[128:256, 0:512] = b4b[...]
            else:
                table[:, 0:512] = b[...]

    lane = lax.broadcasted_iota(jnp.int32, (16, 256), 1).astype(F4)
    models = []
    for core in range(2):
        src = own_s if core == 0 else other_s
        for slot in range(8):
            dy, dxh = slot // 2, slot % 2
            q = lax.rem(y + dy, 4) * 4 + (xh ^ dxh) * 2 + (c ^ core)
            models.append(q)
            table[pl.ds(pl.multiple_of(q * 16, 16), 16), 512:1536] = src[slot, 0, :, 0:1024]
            extra = src[slot, 0, :, 1024:1152].astype(F4)
            for t in range(4):
                row = (core * 8 + slot) * 64 + t * 16
                at = t * 32
                hit = extra[:, at : at + 1] == lane
                pick[row : row + 16, :] = jnp.where(hit, 1.0, 0.0).astype(BF)
                value = extra[:, at + 1 : at + 2] + extra[:, at + 2 : at + 3] + extra[:, at + 3 : at + 4]
                scale[row : row + 16, :] = jnp.broadcast_to(value, (16, 128))

    for n in range(6):
        cols = slice(n * 256, n * 256 + 256)
        got = dot(pick[...], table[:, cols])
        for m in range(16):
            part = slice(m * 64, m * 64 + 64)
            r = scale[part, :]
            r = jnp.concatenate([r, r], 1)
            g = gains[pl.ds(models[m], 1), cols]
            calib[part, cols] = (got[part] * r * g).astype(BF)
    for n in range(4):
        cols = slice(n * 256, n * 256 + 256)
        rhs = calib[:, 512 + n * 256 : 512 + n * 256 + 256]
        acc[:, cols] += contract_rows(calib[:, 0:512], rhs)

    @pl.when(k == 7)
    def _():
        near[...] = acc[:, 0:512]
        far[...] = acc[:, 512:1024].astype(BF)


def gram_call(info, blocks, own_s, other_s, gains):
    whole = lambda shape: pl.BlockSpec(shape, lambda k, info: (0,) * len(shape))
    by_z = pl.BlockSpec((8, 1, 16, 1152), lambda k, info: (0, (info[5] + k) % 8, 0, 0))
    return pl.pallas_call(
        gram_kernel,
        grid_spec=pltpu.PrefetchScalarGridSpec(
            num_scalar_prefetch=1,
            grid=(8,),
            in_specs=[whole(b.shape) for b in blocks] + [by_z, by_z, whole((16, 1536))],
            out_specs=[whole((512, 512)), whole((512, 512))],
            scratch_shapes=[
                pltpu.VMEM((512, 1024), F4),
                pltpu.VMEM((256, 1536), BF),
                pltpu.VMEM((1024, 256), BF),
                pltpu.VMEM((1024, 128), F4),
                pltpu.VMEM((1024, 1536), BF),
            ],
        ),
        out_shape=[
            jax.ShapeDtypeStruct((512, 512), F4),
            jax.ShapeDtypeStruct((512, 512), BF),
        ],
        compiler_params=pltpu.CompilerParams(
            dimension_semantics=("arbitrary",), vmem_limit_bytes=44 * 2**20
        ),
        cost_estimate=pl.CostEstimate(flops=15 * 2**30, bytes_accessed=9 * 2**20, transcendentals=0),
        name="gram",
    )(info, *blocks, own_s, other_s, gains)


def local(bank, calib_ids, norm_gains, proj_slabs):
    p = lax.axis_index("mp")
    s = lax.axis_index("shard")
    y, xh, c = p // 4, p // 2 % 2, p % 2
    z, xl = s // 2, s % 2
    info = jnp.stack([p, xl, y, xh, c, z]).astype(jnp.int32)
    weights = proj_slabs[0]
    ids = (calib_ids[0] - s * 256).reshape(64, 1)
    gain_blocks = norm_gains.reshape(16, 512)

    mine = lax.dynamic_slice_in_dim(gain_blocks, z * 2, 2, 0)
    mine = jnp.where(xl == 0, mine, mine[::-1]).reshape(1, 1024)
    sent = jnp.concatenate([gain_blocks, jnp.broadcast_to(mine, (16, 1024))], 1)
    gains_all = lax.all_to_all(sent.reshape(16, 12, 128), "mp", 0, 0, tiled=True).reshape(16, 1536)

    calib_own, piece = prepare(info, bank, ids, gain_blocks)
    piece = swap_z(piece)
    cols = swap_z(calib_own).reshape(512, 1024)

    blocks = gather_z(lax.dynamic_slice_in_dim(bank, p * 512, 512, 1))
    own_s, other_s = gather_mp(piece)
    near, far = gram_call(info, blocks, own_s, other_s, gains_all)
    gram = near + shift(far, xl=1).astype(F4)
    on_diag = (p == s) & (
        lax.broadcasted_iota(jnp.int32, (512, 512), 0) == lax.broadcasted_iota(jnp.int32, (512, 512), 1)
    )
    merged_gram = gram * jnp.where(on_diag, 1.0 / 1024, ALPHA / 1024)

    both = jnp.concatenate([weights, shift(weights, xl=1)], 0)
    partial_out = swap_z(dot(cols, both).astype(BF).reshape(8, 64, 512))
    model_out = jnp.sum(partial_out.astype(F4), 0).astype(BF)
    model_out = swap_z(jnp.broadcast_to(model_out[None], (8, 64, 512))).reshape(512, 512)

    cols_f = cols.astype(F4)
    diag = jnp.sum(cols_f * cols_f, 0)
    numer = contract_rows(cols, model_out) * (ALPHA / 1024)
    numer = numer + ((1.0 - ALPHA) / 1024 * diag)[:, None] * both.astype(F4)
    numer = numer[:512] + shift(numer[512:].astype(BF), xl=1).astype(F4)
    numer = lax.all_to_all(numer.astype(BF).reshape(16, 32, 512), "mp", 0, 0, tiled=True)
    numer = jnp.sum(numer.astype(F4), 0)
    mine = lax.all_to_all(
        jnp.broadcast_to(numer[None], (8, 32, 512)), "mp", 0, 0, tiled=True, axis_index_groups=CORE_GROUPS
    )
    theirs = shift(mine, c=1)
    numer = jnp.where(c == 0, jnp.stack([mine, theirs], 1), jnp.stack([theirs, mine], 1)).reshape(512, 512)
    return (merged_gram, numer)


def solution(mesh):
    placed = (P("shard", None), P("mp", "shard"), P("mp", None), P("mp", "shard", None))
    return jax.shard_map(
        local,
        mesh=mesh,
        in_specs=placed,
        out_specs=(P("mp", "shard"), P("shard", None)),
        check_vma=False,
    )
```

```python
import jax
import jax.numpy as jnp
from jax import lax
from jax.experimental import pallas as pl
from jax.experimental.pallas import tpu as pltpu
from jax.sharding import PartitionSpec as P

ALPHA = 0.9
EPSILON = 1e-05
BF = jnp.bfloat16
F4 = jnp.float32
AXES = ("mp", "shard")
Z_GROUPS = [[z * 2 + xl for z in range(8)] for xl in range(2)]
CORE_GROUPS = [[q * 2 + c for q in range(8)] for c in range(2)]


def shift(x, y=0, xh=0, c=0, z=0, xl=0):
    pairs = []
    for p in range(16):
        for s in range(16):
            py, pxh, pc = p // 4, p // 2 % 2, p % 2
            sz, sxl = s // 2, s % 2
            tp = (py + y) % 4 * 4 + (pxh ^ xh) * 2 + (pc ^ c)
            ts = (sz + z) % 8 * 2 + (sxl ^ xl)
            pairs.append((p * 16 + s, tp * 16 + ts))
    return lax.ppermute(x, AXES, pairs)


def swap_z(x):
    return lax.all_to_all(x, "shard", 0, 0, tiled=True, axis_index_groups=Z_GROUPS)


def dot(a, b):
    return jnp.dot(a, b, preferred_element_type=F4)


def contract_rows(a, b):
    return lax.dot_general(a, b, (((0,), (0,)), ((), ())), preferred_element_type=F4)


def gather_mp(x):
    half = x.shape[0] // 2
    h = shift(x, xh=1)
    u = shift(x, y=1)
    d = shift(x, y=-1)
    hu = shift(h, y=1)
    hd = shift(h, y=-1)
    t = jnp.concatenate([shift(u[:half], y=1), shift(d[half:], y=-1)], 0)
    ht = shift(t, xh=1)
    own = jnp.stack([x, h, d, hd, t, ht, u, hu], 0)
    return own, shift(own, c=1)


def gather_z(x):
    u, d = [x], [x]
    for _ in range(3):
        u.append(shift(u[-1], z=1))
        d.append(shift(d[-1], z=-1))
    far = [shift(u[3][:128], z=1), shift(d[3][128:], z=-1)]
    return [x, d[1], d[2], d[3]] + far + [u[3], u[2], u[1]]


def prepare_kernel(info, bank, ids, gains, calib_out, piece_out, cols_out, rows, total):
    zz = pl.program_id(0)
    p, s, xl = info[0], info[1], info[2]
    i0 = lax.broadcasted_iota(jnp.int32, (64, 64), 0)
    i1 = lax.broadcasted_iota(jnp.int32, (64, 64), 1)
    row_ids = (ids[...] - s * 256).astype(F4)
    row_ids = jnp.sum(jnp.where(i0 == i1, row_ids, 0.0), axis=1, keepdims=True)
    pick = jnp.where(row_ids == lax.broadcasted_iota(jnp.int32, (64, 256), 1).astype(F4), 1.0, 0.0).astype(BF)

    @pl.when(zz == 0)
    def _():
        total[...] = jnp.zeros_like(total)

    got = dot(pick, bank[...])
    total[...] += jnp.sum(got * got, axis=1, keepdims=True)
    own_row = pl.multiple_of(p * 16, 16)
    for j in range(2):
        at = pl.multiple_of((xl ^ j) * 512, 512)
        piece_out[zz, :, j * 512 : j * 512 + 512] = bank[pl.ds(own_row, 16), pl.ds(at, 512)]
        rows[zz, j] = got[:, j * 512 : j * 512 + 512]

    @pl.when(zz == p // 2)
    def _():
        cols_out[...] = bank[:, pl.ds(pl.multiple_of(p % 2 * 512, 512), 512)]

    @pl.when(zz == 7)
    def _():
        scale = lax.rsqrt(total[:, 0:1] / 8192 + EPSILON)
        hi = scale.astype(BF).astype(F4)
        mid = (scale - hi).astype(BF).astype(F4)
        low = scale - hi - mid
        lane = lax.broadcasted_iota(jnp.int32, (16, 128), 1)
        extra = jnp.zeros((16, 128), F4)
        for q in range(4):
            part = slice(q * 16, q * 16 + 16)
            for j, v in enumerate((row_ids, hi, mid, low)):
                extra = jnp.where(lane == q * 32 + j, v[part], extra)
        extra = extra.astype(BF)
        own = [gains[pl.ds(s // 2 * 2 + i, 1), :] for i in range(2)]
        own = jnp.concatenate([g[:, i * 128 : i * 128 + 128] for g in own for i in range(4)], 0)
        own_hi = own.astype(BF).astype(F4)
        own = jnp.concatenate([own_hi, own - own_hi], 0).astype(BF)
        for to in range(8):
            piece_out[to, :, 1024:1152] = extra
            piece_out[to, :, 1152:1280] = own
            for j in range(2):
                g = gains[pl.ds(to * 2 + (xl ^ j), 1), :]
                calib_out[to, :, j * 512 : j * 512 + 512] = (rows[to, xl ^ j] * scale * g).astype(BF)


def prepare(info, bank, ids, gains):
    whole = lambda shape: pl.BlockSpec(shape, lambda i, info: (0,) * len(shape))
    return pl.pallas_call(
        prepare_kernel,
        grid_spec=pltpu.PrefetchScalarGridSpec(
            num_scalar_prefetch=1,
            grid=(8,),
            in_specs=[pl.BlockSpec((256, 1024), lambda i, info: (0, i)), whole((1, 64)), whole((16, 512))],
            out_specs=[whole((8, 64, 1024)), whole((8, 16, 1280)), whole((256, 512))],
            scratch_shapes=[pltpu.VMEM((8, 2, 64, 512), F4), pltpu.VMEM((64, 128), F4)],
        ),
        out_shape=[
            jax.ShapeDtypeStruct((8, 64, 1024), BF),
            jax.ShapeDtypeStruct((8, 16, 1280), BF),
            jax.ShapeDtypeStruct((256, 512), BF),
        ],
        compiler_params=pltpu.CompilerParams(
            dimension_semantics=("arbitrary",), vmem_limit_bytes=24 * 2**20
        ),
        cost_estimate=pl.CostEstimate(flops=2**28, bytes_accessed=6 * 2**20, transcendentals=64),
        name="prepare",
    )(info, bank, ids, gains)


ORDER = (0, 7, 1, 6, 2, 5, 3, 4)


def slot_model(info, core, slot):
    y, xh, c = info[3], info[4], info[5]
    return lax.rem(y + slot // 2, 4) * 4 + (xh ^ (slot % 2)) * 2 + (c ^ core)


def gram_kernel(first, last, info, *refs):
    refs = list(refs)
    blocks = [refs.pop(0) for _ in range(3 if last else 2)]
    own_s, other_s = refs.pop(0), refs.pop(0)
    if first:
        own_g, other_g = refs.pop(0), refs.pop(0)
    else:
        gains, before = refs.pop(0), refs.pop(0)
    if last:
        near, far = refs.pop(0), refs.pop(0)
    else:
        acc = refs.pop(0)
    if first:
        gains = refs.pop(0)
    if last:
        acc = refs.pop(0)
    table, pick, scale, calib = refs
    step = pl.program_id(0)
    p, xl, z = info[0], info[2], info[6]

    @pl.when(step == 0)
    def _():
        if not first:
            acc[...] = before[...]
        else:
            acc[...] = jnp.zeros_like(acc)
            for core in range(2):
                src = own_g if core == 0 else other_g
                for slot in range(8):
                    m = slot_model(info, core, slot)
                    row = []
                    for b in (p, z * 2 + xl, z * 2 + (1 - xl)):
                        tile = src[slot, b // 2].astype(F4)
                        tile = tile[0:8] + tile[8:16]
                        tile = jnp.where(b % 2 == 0, tile[0:4], tile[4:8])
                        row += [tile[i : i + 1] for i in range(4)]
                    gains[pl.ds(m, 1), :] = jnp.concatenate(row, 1)
        table[:, 0:512] = blocks[0][...]

    @pl.when(step == 1)
    def _():
        if last:
            table[0:128, 0:512] = blocks[1][...]
            table[128:256, 0:512] = blocks[2][...]
        else:
            table[:, 0:512] = blocks[1][...]

    lane = lax.broadcasted_iota(jnp.int32, (16, 256), 1).astype(F4)
    models = []
    for core in range(2):
        src = own_s if core == 0 else other_s
        for slot in range(8):
            m = slot_model(info, core, slot)
            models.append(m)
            table[pl.ds(pl.multiple_of(m * 16, 16), 16), 512:1536] = src[slot, 0, :, 0:1024]
            extra = src[slot, 0, :, 1024:1152].astype(F4)
            for t in range(4):
                row = (core * 8 + slot) * 64 + t * 16
                at = t * 32
                hit = extra[:, at : at + 1] == lane
                pick[row : row + 16, :] = jnp.where(hit, 1.0, 0.0).astype(BF)
                value = extra[:, at + 1 : at + 2] + extra[:, at + 2 : at + 3] + extra[:, at + 3 : at + 4]
                scale[row : row + 16, :] = jnp.broadcast_to(value, (16, 128))

    for n in range(6):
        cols = slice(n * 256, n * 256 + 256)
        got = dot(pick[...], table[:, cols])
        for m in range(16):
            part = slice(m * 64, m * 64 + 64)
            r = scale[part, :]
            r = jnp.concatenate([r, r], 1)
            g = gains[pl.ds(models[m], 1), cols]
            calib[part, cols] = (got[part] * r * g).astype(BF)
    acc[...] += contract_rows(calib[:, 0:512], calib[:, 512:1536])

    if last:

        @pl.when(step == 1)
        def _():
            near[...] = acc[:, 0:512]
            far[...] = acc[:, 512:1024].astype(BF)


def gram_call(i, info, blocks, own_s, other_s, gains, before):
    first, last = i == 0, i == 3
    k0, k1 = ORDER[2 * i], ORDER[2 * i + 1]
    whole = lambda shape: pl.BlockSpec(shape, lambda j, info: (0,) * len(shape))
    by_z = pl.BlockSpec((8, 1, 16, 1280), lambda j, info: (0, (info[6] + k0 + j * (k1 - k0) + 8) % 8, 0, 0))
    gain_view = pl.BlockSpec((8, 8, 16, 128), lambda j, info: (0, 0, 0, 9))
    shapes = [jax.ShapeDtypeStruct((512, 1024), F4)]
    if last:
        shapes = [jax.ShapeDtypeStruct((512, 512), F4), jax.ShapeDtypeStruct((512, 512), BF)]
    if first:
        shapes.append(jax.ShapeDtypeStruct((16, 1536), F4))
    extra = [own_s, other_s] if first else [gains, before]
    extra_specs = [gain_view, gain_view] if first else [whole((16, 1536)), whole((512, 1024))]
    operands = [info, *blocks, own_s, other_s, *extra]
    return pl.pallas_call(
        lambda *refs: gram_kernel(first, last, *refs),
        grid_spec=pltpu.PrefetchScalarGridSpec(
            num_scalar_prefetch=1,
            grid=(2,),
            in_specs=[whole(b.shape) for b in blocks] + [by_z, by_z] + extra_specs,
            out_specs=[whole(o.shape) for o in shapes],
            scratch_shapes=([pltpu.VMEM((512, 1024), F4)] if last else [])
            + [
                pltpu.VMEM((256, 1536), BF),
                pltpu.VMEM((1024, 256), BF),
                pltpu.VMEM((1024, 128), F4),
                pltpu.VMEM((1024, 1536), BF),
            ],
        ),
        out_shape=shapes,
        input_output_aliases={} if first or last else {len(operands) - 1: 0},
        compiler_params=pltpu.CompilerParams(
            dimension_semantics=("arbitrary",), vmem_limit_bytes=44 * 2**20
        ),
        cost_estimate=pl.CostEstimate(flops=4 * 2**30, bytes_accessed=6 * 2**20, transcendentals=0),
        name="gram" + str(i),
    )(*operands)


def local(bank, calib_ids, norm_gains, proj_slabs):
    p = lax.axis_index("mp")
    s = lax.axis_index("shard")
    y, xh, c = p // 4, p // 2 % 2, p % 2
    z, xl = s // 2, s % 2
    info = jnp.stack([p, s, xl, y, xh, c, z]).astype(jnp.int32)
    weights = proj_slabs[0]

    calib_own, piece, bank_cols = prepare(info, bank, calib_ids, norm_gains.reshape(16, 512))
    piece = swap_z(piece)
    cols = swap_z(calib_own).reshape(512, 1024)

    b = gather_z(bank_cols)
    own_s, other_s = gather_mp(piece)
    both = jnp.concatenate([weights, shift(weights, xl=1)], 0)
    cols, b[1], b[8] = lax.optimization_barrier((cols, b[1], b[8]))
    partial_out = swap_z(dot(cols, both).astype(BF).reshape(8, 64, 512))
    partial_out, b[2], b[7] = lax.optimization_barrier((partial_out, b[2], b[7]))
    model_out = jnp.sum(partial_out.astype(F4), 0).astype(BF)
    model_out = swap_z(jnp.broadcast_to(model_out[None], (8, 64, 512))).reshape(512, 512)

    cols_f = cols.astype(F4)
    diag = jnp.sum(cols_f * cols_f, 0)
    numer = contract_rows(cols, model_out) * (ALPHA / 1024)
    numer = numer + ((1.0 - ALPHA) / 1024 * diag)[:, None] * both.astype(F4)
    numer = numer[:512] + shift(numer[512:].astype(BF), xl=1).astype(F4)
    numer = lax.all_to_all(numer.astype(BF).reshape(16, 32, 512), "mp", 0, 0, tiled=True)
    numer = jnp.sum(numer.astype(F4), 0)
    mine = lax.all_to_all(
        jnp.broadcast_to(numer[None], (8, 32, 512)), "mp", 0, 0, tiled=True, axis_index_groups=CORE_GROUPS
    )
    theirs = shift(mine, c=1)
    numer = jnp.where(c == 0, jnp.stack([mine, theirs], 1), jnp.stack([theirs, mine], 1)).reshape(512, 512)
    acc, gains = gram_call(0, info, [b[0], b[8]], own_s, other_s, None, None)
    (acc,) = gram_call(1, info, [b[1], b[7]], own_s, other_s, gains, acc)
    (acc,) = gram_call(2, info, [b[2], b[6]], own_s, other_s, gains, acc)
    near, far = gram_call(3, info, [b[3], b[4], b[5]], own_s, other_s, gains, acc)
    gram = near + shift(far, xl=1).astype(F4)
    on_diag = (p == s) & (
        lax.broadcasted_iota(jnp.int32, (512, 512), 0) == lax.broadcasted_iota(jnp.int32, (512, 512), 1)
    )
    merged_gram = gram * jnp.where(on_diag, 1.0 / 1024, ALPHA / 1024)

    return (merged_gram, numer)


def solution(mesh):
    placed = (P("shard", None), P("mp", "shard"), P("mp", None), P("mp", "shard", None))
    return jax.shard_map(
        local,
        mesh=mesh,
        in_specs=placed,
        out_specs=(P("mp", "shard"), P("shard", None)),
        check_vma=False,
    )
```

```python
import jax
import jax.numpy as jnp
from jax import lax
from jax.experimental import pallas as pl
from jax.experimental.pallas import tpu as pltpu
from jax.sharding import PartitionSpec as P

ALPHA = 0.9
EPSILON = 1e-05
BF = jnp.bfloat16
F4 = jnp.float32
VMEM = 60 * 2**20
AXES = ("mp", "shard")
Z_GROUPS = [[z * 2 + xl for z in range(8)] for xl in range(2)]
CORE_GROUPS = [[q * 2 + c for q in range(8)] for c in range(2)]


def shift(x, y=0, xh=0, c=0, z=0, xl=0):
    pairs = []
    for p in range(16):
        for s in range(16):
            py, pxh, pc = p // 4, p // 2 % 2, p % 2
            sz, sxl = s // 2, s % 2
            tp = (py + y) % 4 * 4 + (pxh ^ xh) * 2 + (pc ^ c)
            ts = (sz + z) % 8 * 2 + (sxl ^ xl)
            pairs.append((p * 16 + s, tp * 16 + ts))
    return lax.ppermute(x, AXES, pairs)


def swap_z(x):
    return lax.all_to_all(x, "shard", 0, 0, tiled=True, axis_index_groups=Z_GROUPS)


def dot(a, b):
    return jnp.dot(a, b, preferred_element_type=F4)


def contract_rows(a, b):
    return lax.dot_general(a, b, (((0,), (0,)), ((), ())), preferred_element_type=F4)


def gather_both(piece, x, w):
    tie = lax.optimization_barrier
    z = [x]
    zu, zd = shift(x, z=1), shift(x, z=-1)
    piece, zu, zd, w = tie((swap_z(piece), zu, zd, shift(w, xl=1)))
    z += [zu, zd]
    h, u, d = shift(piece, xh=1), shift(piece, y=1), shift(piece, y=-1)
    zu, zd = shift(zu, z=1), shift(zd, z=-1)
    h, u, d, zu, zd = tie((h, u, d, zu, zd))
    z += [zu, zd]
    half = piece.shape[0] // 2
    t0, t1 = shift(u[:half], y=1), shift(d[half:], y=-1)
    hu, hd = shift(h, y=1), shift(h, y=-1)
    zu, zd = shift(zu, z=1), shift(zd, z=-1)
    hu, hd, t0, t1, zu, zd = tie((hu, hd, t0, t1, zu, zd))
    z += [zu, zd]
    t = jnp.concatenate([t0, t1], 0)
    ht = shift(t, xh=1)
    zu, zd = shift(zu[:128], z=1), shift(zd[128:], z=-1)
    ht, zu, zd = tie((ht, zu, zd))
    own = jnp.stack([piece, h, d, hd, t, ht, u, hu], 0)
    return own, shift(own, c=1), w, [x, z[2], z[4], z[6], zu, zd, z[5], z[3], z[1]]


def prepare_kernel(info, bank, ids, gains, piece_out, cols_out, total):
    zz = pl.program_id(0)
    p, s, xl = info[0], info[1], info[2]
    i0 = lax.broadcasted_iota(jnp.int32, (64, 64), 0)
    i1 = lax.broadcasted_iota(jnp.int32, (64, 64), 1)
    row_ids = (ids[...] - s * 256).astype(F4)
    row_ids = jnp.sum(jnp.where(i0 == i1, row_ids, 0.0), axis=1, keepdims=True)
    pick = jnp.where(row_ids == lax.broadcasted_iota(jnp.int32, (64, 256), 1).astype(F4), 1.0, 0.0).astype(BF)

    @pl.when(zz == 0)
    def _():
        total[...] = jnp.zeros_like(total)

    got = dot(pick, bank[...])
    total[...] += jnp.sum(got * got, axis=1, keepdims=True)
    own_row = pl.multiple_of(p * 16, 16)
    for j in range(2):
        at = pl.multiple_of((xl ^ j) * 512, 512)
        piece_out[zz, :, j * 512 : j * 512 + 512] = bank[pl.ds(own_row, 16), pl.ds(at, 512)]

    @pl.when(zz == p // 2)
    def _():
        cols_out[...] = bank[:, pl.ds(pl.multiple_of(p % 2 * 512, 512), 512)]

    @pl.when(zz == 7)
    def _():
        scale = lax.rsqrt(total[:, 0:1] / 8192 + EPSILON)
        hi = scale.astype(BF).astype(F4)
        mid = (scale - hi).astype(BF).astype(F4)
        low = scale - hi - mid
        lane = lax.broadcasted_iota(jnp.int32, (16, 128), 1)
        extra = jnp.zeros((16, 128), F4)
        for q in range(4):
            part = slice(q * 16, q * 16 + 16)
            for j, v in enumerate((row_ids, hi, mid, low)):
                extra = jnp.where(lane == q * 32 + j, v[part], extra)
        extra = extra.astype(BF)
        own = gains[:, pl.ds(pl.multiple_of(s // 2 * 1024, 1024), 1024)]
        own = jnp.concatenate([own[:, i * 128 : i * 128 + 128] for i in range(8)], 0)
        own_hi = own.astype(BF).astype(F4)
        own = jnp.concatenate([own_hi, own - own_hi], 0).astype(BF)
        for to in range(8):
            piece_out[to, :, 1024:1152] = extra
            piece_out[to, :, 1152:1280] = own


def prepare(info, bank, ids, gains):
    whole = lambda shape: pl.BlockSpec(shape, lambda i, info: (0,) * len(shape))
    return pl.pallas_call(
        prepare_kernel,
        grid_spec=pltpu.PrefetchScalarGridSpec(
            num_scalar_prefetch=1,
            grid=(8,),
            in_specs=[pl.BlockSpec((256, 1024), lambda i, info: (0, i)), whole((1, 64)), whole((1, 8192))],
            out_specs=[whole((8, 16, 1280)), whole((256, 512))],
            scratch_shapes=[pltpu.VMEM((64, 128), F4)],
        ),
        out_shape=[jax.ShapeDtypeStruct((8, 16, 1280), BF), jax.ShapeDtypeStruct((256, 512), BF)],
        compiler_params=pltpu.CompilerParams(dimension_semantics=("arbitrary",), vmem_limit_bytes=VMEM),
        cost_estimate=pl.CostEstimate(flops=2**28, bytes_accessed=5 * 2**20, transcendentals=64),
        name="prepare",
    )(info, bank, ids, gains)


def project_kernel(info, own_s, other_s, gains, weights, part_out, calib_out, diag_out, table, calib):
    zz = pl.program_id(0)
    xl, z = info[2], info[6]
    for core in range(2):
        src = own_s if core == 0 else other_s
        for slot in range(8):
            m = slot_model(info, core, slot)
            table[pl.ds(pl.multiple_of(m * 16, 16), 16), :] = src[slot, 0, :, 0:1024]
    extra = own_s[0, 0, :, 1024:1152].astype(F4)
    lane = lax.broadcasted_iota(jnp.int32, (16, 256), 1).astype(F4)
    pick, scale = [], []
    for t in range(4):
        at = t * 32
        pick.append(jnp.where(extra[:, at : at + 1] == lane, 1.0, 0.0))
        scale.append(extra[:, at + 1 : at + 2] + extra[:, at + 2 : at + 3] + extra[:, at + 3 : at + 4])
    pick = jnp.concatenate(pick, 0).astype(BF)
    scale = jnp.concatenate(scale, 0)
    rows = pl.ds(pl.multiple_of(zz * 64, 64), 64)
    for j in range(2):
        cols = slice(j * 512, j * 512 + 512)
        g = gains[:, pl.ds(pl.multiple_of((z * 2 + (xl ^ j)) * 512, 512), 512)]
        calib[rows, cols] = (dot(pick, table[:, cols]) * scale * g).astype(BF)

    @pl.when(zz == 7)
    def _():
        calib_out[...] = calib[...]
        part = dot(calib[...], weights[...]).astype(BF)
        for to in range(8):
            part_out[to] = part[to * 64 : to * 64 + 64]
        whole = calib[...].astype(F4)
        diag_out[...] = jnp.sum(whole * whole, axis=0, keepdims=True)


def project(info, own_s, other_s, gains, weights):
    whole = lambda shape: pl.BlockSpec(shape, lambda i, info: (0,) * len(shape))
    by_z = pl.BlockSpec((8, 1, 16, 1280), lambda i, info: (0, i, 0, 0))
    return pl.pallas_call(
        project_kernel,
        grid_spec=pltpu.PrefetchScalarGridSpec(
            num_scalar_prefetch=1,
            grid=(8,),
            in_specs=[by_z, by_z, whole((1, 8192)), whole((1024, 512))],
            out_specs=[whole((8, 64, 512)), whole((512, 1024)), whole((1, 1024))],
            scratch_shapes=[pltpu.VMEM((256, 1024), BF), pltpu.VMEM((512, 1024), BF)],
        ),
        out_shape=[
            jax.ShapeDtypeStruct((8, 64, 512), BF),
            jax.ShapeDtypeStruct((512, 1024), BF),
            jax.ShapeDtypeStruct((1, 1024), F4),
        ],
        compiler_params=pltpu.CompilerParams(dimension_semantics=("arbitrary",), vmem_limit_bytes=VMEM),
        cost_estimate=pl.CostEstimate(flops=2**30, bytes_accessed=8 * 2**20, transcendentals=0),
        name="project",
    )(info, own_s, other_s, gains, weights)


def numer_kernel(calib, model_out, diag, weights, near, far):
    ratio = lax.broadcasted_iota(jnp.int32, (512, 512), 0) == lax.broadcasted_iota(jnp.int32, (512, 512), 1)
    for j in range(2):
        cols = slice(j * 512, j * 512 + 512)
        d = diag[:, cols] * ((1.0 - ALPHA) / 1024)
        d = jnp.sum(jnp.where(ratio, d, 0.0), axis=1, keepdims=True)
        got = contract_rows(calib[:, cols], model_out[...]) * (ALPHA / 1024)
        got = got + d * weights[cols, :].astype(F4)
        if j == 0:
            near[...] = got
        else:
            far[...] = got.astype(BF)


def numer_call(calib, model_out, diag, weights):
    return pl.pallas_call(
        numer_kernel,
        in_specs=[pl.BlockSpec(memory_space=pltpu.VMEM)] * 4,
        out_specs=[pl.BlockSpec(memory_space=pltpu.VMEM)] * 2,
        out_shape=[jax.ShapeDtypeStruct((512, 512), F4), jax.ShapeDtypeStruct((512, 512), BF)],
        compiler_params=pltpu.CompilerParams(vmem_limit_bytes=VMEM),
        cost_estimate=pl.CostEstimate(flops=2**29, bytes_accessed=4 * 2**20, transcendentals=0),
        name="numer",
    )(calib, model_out, diag, weights)


ORDER = (0, 7, 1, 6, 2, 5, 3, 4)


def slot_model(info, core, slot):
    y, xh, c = info[3], info[4], info[5]
    return lax.rem(y + slot // 2, 4) * 4 + (xh ^ (slot % 2)) * 2 + (c ^ core)


def gram_kernel(first, last, info, *refs):
    refs = list(refs)
    blocks = [refs.pop(0) for _ in range(3 if last else 2)]
    own_s, other_s = refs.pop(0), refs.pop(0)
    if first:
        own_g, other_g = refs.pop(0), refs.pop(0)
    else:
        gains, before = refs.pop(0), refs.pop(0)
    if last:
        near, far = refs.pop(0), refs.pop(0)
    else:
        acc = refs.pop(0)
    if first:
        gains = refs.pop(0)
    if last:
        acc = refs.pop(0)
    table, pick, scale, calib = refs
    step = pl.program_id(0)
    p, xl, z = info[0], info[2], info[6]

    @pl.when(step == 0)
    def _():
        if not first:
            acc[...] = before[...]
        else:
            acc[...] = jnp.zeros_like(acc)
            for core in range(2):
                src = own_g if core == 0 else other_g
                for slot in range(8):
                    m = slot_model(info, core, slot)
                    row = []
                    for b in (p, z * 2 + xl, z * 2 + (1 - xl)):
                        tile = src[slot, b // 2].astype(F4)
                        tile = tile[0:8] + tile[8:16]
                        tile = jnp.where(b % 2 == 0, tile[0:4], tile[4:8])
                        row += [tile[i : i + 1] for i in range(4)]
                    gains[pl.ds(m, 1), :] = jnp.concatenate(row, 1)
        table[:, 0:512] = blocks[0][...]

    @pl.when(step == 1)
    def _():
        if last:
            table[0:128, 0:512] = blocks[1][...]
            table[128:256, 0:512] = blocks[2][...]
        else:
            table[:, 0:512] = blocks[1][...]

    lane = lax.broadcasted_iota(jnp.int32, (16, 256), 1).astype(F4)
    models = []
    for core in range(2):
        src = own_s if core == 0 else other_s
        for slot in range(8):
            m = slot_model(info, core, slot)
            models.append(m)
            table[pl.ds(pl.multiple_of(m * 16, 16), 16), 512:1536] = src[slot, 0, :, 0:1024]
            extra = src[slot, 0, :, 1024:1152].astype(F4)
            for t in range(4):
                row = (core * 8 + slot) * 64 + t * 16
                at = t * 32
                hit = extra[:, at : at + 1] == lane
                pick[row : row + 16, :] = jnp.where(hit, 1.0, 0.0).astype(BF)
                value = extra[:, at + 1 : at + 2] + extra[:, at + 2 : at + 3] + extra[:, at + 3 : at + 4]
                scale[row : row + 16, :] = jnp.broadcast_to(value, (16, 128))

    for n in range(6):
        cols = slice(n * 256, n * 256 + 256)
        got = dot(pick[...], table[:, cols])
        for m in range(16):
            part = slice(m * 64, m * 64 + 64)
            r = scale[part, :]
            r = jnp.concatenate([r, r], 1)
            g = gains[pl.ds(models[m], 1), cols]
            calib[part, cols] = (got[part] * r * g).astype(BF)
    acc[...] += contract_rows(calib[:, 0:512], calib[:, 512:1536])

    if last:

        @pl.when(step == 1)
        def _():
            near[...] = acc[:, 0:512]
            far[...] = acc[:, 512:1024].astype(BF)


def gram_call(i, info, blocks, own_s, other_s, gains, before):
    first, last = i == 0, i == 3
    k0, k1 = ORDER[2 * i], ORDER[2 * i + 1]
    whole = lambda shape: pl.BlockSpec(shape, lambda j, info: (0,) * len(shape))
    by_z = pl.BlockSpec((8, 1, 16, 1280), lambda j, info: (0, (info[6] + k0 + j * (k1 - k0) + 8) % 8, 0, 0))
    gain_view = pl.BlockSpec((8, 8, 16, 128), lambda j, info: (0, 0, 0, 9))
    shapes = [jax.ShapeDtypeStruct((512, 1024), F4)]
    if last:
        shapes = [jax.ShapeDtypeStruct((512, 512), F4), jax.ShapeDtypeStruct((512, 512), BF)]
    if first:
        shapes.append(jax.ShapeDtypeStruct((16, 1536), F4))
    extra = [own_s, other_s] if first else [gains, before]
    extra_specs = [gain_view, gain_view] if first else [whole((16, 1536)), whole((512, 1024))]
    operands = [info, *blocks, own_s, other_s, *extra]
    return pl.pallas_call(
        lambda *refs: gram_kernel(first, last, *refs),
        grid_spec=pltpu.PrefetchScalarGridSpec(
            num_scalar_prefetch=1,
            grid=(2,),
            in_specs=[whole(b.shape) for b in blocks] + [by_z, by_z] + extra_specs,
            out_specs=[whole(o.shape) for o in shapes],
            scratch_shapes=([pltpu.VMEM((512, 1024), F4)] if last else [])
            + [
                pltpu.VMEM((256, 1536), BF),
                pltpu.VMEM((1024, 256), BF),
                pltpu.VMEM((1024, 128), F4),
                pltpu.VMEM((1024, 1536), BF),
            ],
        ),
        out_shape=shapes,
        input_output_aliases={} if first or last else {len(operands) - 1: 0},
        compiler_params=pltpu.CompilerParams(dimension_semantics=("arbitrary",), vmem_limit_bytes=VMEM),
        cost_estimate=pl.CostEstimate(flops=4 * 2**30, bytes_accessed=6 * 2**20, transcendentals=0),
        name="gram" + str(i),
    )(*operands)


def local(bank, calib_ids, norm_gains, proj_slabs):
    p = lax.axis_index("mp")
    s = lax.axis_index("shard")
    y, xh, c = p // 4, p // 2 % 2, p % 2
    z, xl = s // 2, s % 2
    info = jnp.stack([p, s, xl, y, xh, c, z]).astype(jnp.int32)
    weights = proj_slabs[0]

    piece, bank_cols = prepare(info, bank, calib_ids, norm_gains)
    own_s, other_s, weights_other, b = gather_both(piece, bank_cols, weights)
    both = jnp.concatenate([weights, weights_other], 0)

    partial_out, calib, diag = project(info, own_s, other_s, norm_gains, both)
    tie = lax.optimization_barrier
    partial_out, info = tie((partial_out, info))
    acc, gains = gram_call(0, info, [b[0], b[8]], own_s, other_s, None, None)
    partial_out, gains = tie((swap_z(partial_out), gains))
    model_out = jnp.sum(partial_out.astype(F4), 0).astype(BF)
    model_out, info = tie((jnp.broadcast_to(model_out[None], (8, 64, 512)), info))
    (acc,) = gram_call(1, info, [b[1], b[7]], own_s, other_s, gains, acc)
    model_out, acc = tie((swap_z(model_out), acc))

    near, far = numer_call(calib, model_out.reshape(512, 512), diag, both)
    far, info = tie((far, info))
    (acc,) = gram_call(2, info, [b[2], b[6]], own_s, other_s, gains, acc)
    far, acc = tie((shift(far, xl=1), acc))
    numer = (near + far.astype(F4)).astype(BF).reshape(16, 32, 512)
    numer, info = tie((numer, info))
    near, far = gram_call(3, info, [b[3], b[4], b[5]], own_s, other_s, gains, acc)
    numer, far = tie((lax.all_to_all(numer, "mp", 0, 0, tiled=True), far))
    numer = jnp.sum(numer.astype(F4), 0)
    mine = lax.all_to_all(
        jnp.broadcast_to(numer[None], (8, 32, 512)), "mp", 0, 0, tiled=True, axis_index_groups=CORE_GROUPS
    )
    theirs = shift(mine, c=1)
    numer = jnp.where(c == 0, jnp.stack([mine, theirs], 1), jnp.stack([theirs, mine], 1)).reshape(512, 512)

    gram = near + shift(far, xl=1).astype(F4)
    on_diag = (p == s) & (
        lax.broadcasted_iota(jnp.int32, (512, 512), 0) == lax.broadcasted_iota(jnp.int32, (512, 512), 1)
    )
    merged_gram = gram * jnp.where(on_diag, 1.0 / 1024, ALPHA / 1024)

    return (merged_gram, numer)


def solution(mesh):
    placed = (P("shard", None), P("mp", "shard"), P("mp", None), P("mp", "shard", None))
    return jax.shard_map(
        local,
        mesh=mesh,
        in_specs=placed,
        out_specs=(P("mp", "shard"), P("shard", None)),
        check_vma=False,
    )
```

```python
import jax
import jax.numpy as jnp
from jax import lax
from jax.experimental import pallas as pl
from jax.experimental.pallas import tpu as pltpu
from jax.sharding import PartitionSpec as P

ALPHA = 0.9
EPSILON = 1e-05
BF = jnp.bfloat16
F4 = jnp.float32
VMEM = 60 * 2**20
AXES = ("mp", "shard")
Z_GROUPS = [[z * 2 + xl for z in range(8)] for xl in range(2)]
XLO_GROUPS = [[p * 16 + z * 2 + xl for p in range(16) for xl in range(2)] for z in range(8)]


def shift(x, y=0, xh=0, c=0, z=0, xl=0):
    pairs = []
    for p in range(16):
        for s in range(16):
            py, pxh, pc = p // 4, p // 2 % 2, p % 2
            sz, sxl = s // 2, s % 2
            tp = (py + y) % 4 * 4 + (pxh ^ xh) * 2 + (pc ^ c)
            ts = (sz + z) % 8 * 2 + (sxl ^ xl)
            pairs.append((p * 16 + s, tp * 16 + ts))
    return lax.ppermute(x, AXES, pairs)


def swap_z(x):
    return lax.all_to_all(x, "shard", 0, 0, tiled=True, axis_index_groups=Z_GROUPS)


def dot(a, b):
    return jnp.dot(a, b, preferred_element_type=F4)


def contract_rows(a, b):
    return lax.dot_general(a, b, (((0,), (0,)), ((), ())), preferred_element_type=F4)


def gather_both(piece, x, w):
    tie = lax.optimization_barrier
    zu, zd = shift(x, z=1), shift(x, z=-1)
    piece, w = tie((swap_z(piece), shift(w, xl=1)))
    h, u, d = shift(piece, xh=1), shift(piece, y=1), shift(piece, y=-1)
    h, u, d, zu, zd = tie((h, u, d, zu, zd))
    z = [zu, zd]
    half = piece.shape[0] // 2
    t0, t1 = shift(u[:half], y=1), shift(d[half:], y=-1)
    hu, hd = shift(h, y=1), shift(h, y=-1)
    zu, zd = shift(zu, z=1), shift(zd, z=-1)
    hu, hd, t0, t1, zu, zd = tie((hu, hd, t0, t1, zu, zd))
    z += [zu, zd]
    t = jnp.concatenate([t0, t1], 0)
    ht = shift(t, xh=1)
    zu, zd = shift(zu, z=1), shift(zd, z=-1)
    ht, zu, zd = tie((ht, zu, zd))
    z += [zu, zd]
    zu, zd = shift(zu[:128], z=1), shift(zd[128:], z=-1)
    own = jnp.stack([piece, h, d, hd, t, ht, u, hu], 0)
    own, other, zu, zd = tie((own, shift(own, c=1), zu, zd))
    return own, other, w, [x, z[1], z[3], z[5], zu, zd, z[4], z[2], z[0]]


def prepare_kernel(info, bank, ids, gains, piece_out, cols_out, total, column, pick):
    zz = pl.program_id(0)
    p, s, xl = info[0], info[1], info[2]

    @pl.when(zz == 0)
    def _():
        i0 = lax.broadcasted_iota(jnp.int32, (64, 64), 0)
        i1 = lax.broadcasted_iota(jnp.int32, (64, 64), 1)
        row_ids = (ids[...] - s * 256).astype(F4)
        row_ids = jnp.sum(jnp.where(i0 == i1, row_ids, 0.0), axis=1, keepdims=True)
        lane = lax.broadcasted_iota(jnp.int32, (64, 256), 1).astype(F4)
        column[...] = jnp.broadcast_to(row_ids, (64, 128))
        pick[...] = jnp.where(row_ids == lane, 1.0, 0.0).astype(BF)
        total[...] = jnp.zeros_like(total)

    own_row = pl.multiple_of(p * 16, 16)
    for half in range(2):
        got = dot(pick[...], bank[:, half * 1024 : half * 1024 + 1024])
        got = got * got
        total[...] += sum(got[:, i * 128 : i * 128 + 128] for i in range(8))
        for j in range(2):
            at = pl.multiple_of(half * 1024 + (xl ^ j) * 512, 512)
            piece_out[zz * 2 + half, :, j * 512 : j * 512 + 512] = bank[pl.ds(own_row, 16), pl.ds(at, 512)]

    @pl.when(zz == p // 4)
    def _():
        cols_out[...] = bank[:, pl.ds(pl.multiple_of(p % 4 * 512, 512), 512)]

    @pl.when(zz == 3)
    def _():
        row_ids = column[:, 0:1]
        scale = lax.rsqrt(jnp.sum(total[...], axis=1, keepdims=True) / 8192 + EPSILON)
        hi = scale.astype(BF).astype(F4)
        mid = (scale - hi).astype(BF).astype(F4)
        low = scale - hi - mid
        lane = lax.broadcasted_iota(jnp.int32, (16, 128), 1)
        extra = jnp.zeros((16, 128), F4)
        for q in range(4):
            part = slice(q * 16, q * 16 + 16)
            for j, v in enumerate((row_ids, hi, mid, low)):
                extra = jnp.where(lane == q * 32 + j, v[part], extra)
        extra = extra.astype(BF)
        own = gains[:, pl.ds(pl.multiple_of(s // 2 * 1024, 1024), 1024)]
        own = jnp.concatenate([own[:, i * 128 : i * 128 + 128] for i in range(8)], 0)
        own_hi = own.astype(BF).astype(F4)
        own = jnp.concatenate([own_hi, own - own_hi], 0).astype(BF)
        for to in range(8):
            piece_out[to, :, 1024:1152] = extra
            piece_out[to, :, 1152:1280] = own


def prepare(info, bank, ids, gains):
    whole = lambda shape: pl.BlockSpec(shape, lambda i, info: (0,) * len(shape))
    return pl.pallas_call(
        prepare_kernel,
        grid_spec=pltpu.PrefetchScalarGridSpec(
            num_scalar_prefetch=1,
            grid=(4,),
            in_specs=[pl.BlockSpec((256, 2048), lambda i, info: (0, i)), whole((1, 64)), whole((1, 8192))],
            out_specs=[whole((8, 16, 1280)), whole((256, 512))],
            scratch_shapes=[pltpu.VMEM((64, 128), F4), pltpu.VMEM((64, 128), F4), pltpu.VMEM((64, 256), BF)],
        ),
        out_shape=[jax.ShapeDtypeStruct((8, 16, 1280), BF), jax.ShapeDtypeStruct((256, 512), BF)],
        compiler_params=pltpu.CompilerParams(dimension_semantics=("arbitrary",), vmem_limit_bytes=VMEM),
        cost_estimate=pl.CostEstimate(flops=2**28, bytes_accessed=5 * 2**20, transcendentals=64),
        name="prepare",
    )(info, bank, ids, gains)


def project_kernel(info, own_s, other_s, gains, weights, part_out, calib_out, diag_out, table, calib):
    zz = pl.program_id(0)
    xl, z = info[2], info[6]
    lane = lax.broadcasted_iota(jnp.int32, (16, 256), 1).astype(F4)
    for i in range(2):
        for core in range(2):
            src = own_s if core == 0 else other_s
            for slot in range(8):
                m = slot_model(info, core, slot)
                table[i, pl.ds(pl.multiple_of(m * 16, 16), 16), :] = src[slot, i, :, 0:1024]
        extra = own_s[0, i, :, 1024:1152].astype(F4)
        pick, scale = [], []
        for t in range(4):
            at = t * 32
            pick.append(jnp.where(extra[:, at : at + 1] == lane, 1.0, 0.0))
            scale.append(extra[:, at + 1 : at + 2] + extra[:, at + 2 : at + 3] + extra[:, at + 3 : at + 4])
        pick = jnp.concatenate(pick, 0).astype(BF)
        scale = jnp.concatenate(scale, 0)
        rows = pl.ds(pl.multiple_of(zz * 128 + i * 64, 64), 64)
        for j in range(2):
            cols = slice(j * 512, j * 512 + 512)
            g = gains[:, pl.ds(pl.multiple_of((z * 2 + (xl ^ j)) * 512, 512), 512)]
            calib[rows, cols] = (dot(pick, table[i, :, cols]) * scale * g).astype(BF)

    @pl.when(zz == 3)
    def _():
        calib_out[...] = calib[...]
        part = dot(calib[...], weights[...]).astype(BF)
        for to in range(8):
            part_out[to] = part[to * 64 : to * 64 + 64]
        whole = calib[...].astype(F4)
        diag_out[...] = jnp.sum(whole * whole, axis=0, keepdims=True)


def project(info, own_s, other_s, gains, weights):
    whole = lambda shape: pl.BlockSpec(shape, lambda i, info: (0,) * len(shape))
    by_z = pl.BlockSpec((8, 2, 16, 1280), lambda i, info: (0, i, 0, 0))
    return pl.pallas_call(
        project_kernel,
        grid_spec=pltpu.PrefetchScalarGridSpec(
            num_scalar_prefetch=1,
            grid=(4,),
            in_specs=[by_z, by_z, whole((1, 8192)), whole((1024, 512))],
            out_specs=[whole((8, 64, 512)), whole((512, 1024)), whole((1, 1024))],
            scratch_shapes=[pltpu.VMEM((2, 256, 1024), BF), pltpu.VMEM((512, 1024), BF)],
        ),
        out_shape=[
            jax.ShapeDtypeStruct((8, 64, 512), BF),
            jax.ShapeDtypeStruct((512, 1024), BF),
            jax.ShapeDtypeStruct((1, 1024), F4),
        ],
        compiler_params=pltpu.CompilerParams(dimension_semantics=("arbitrary",), vmem_limit_bytes=VMEM),
        cost_estimate=pl.CostEstimate(flops=2**30, bytes_accessed=8 * 2**20, transcendentals=0),
        name="project",
    )(info, own_s, other_s, gains, weights)


def numer_kernel(info, calib, model_out, diag, weights, out):
    xl = info[2]
    ratio = lax.broadcasted_iota(jnp.int32, (512, 512), 0) == lax.broadcasted_iota(jnp.int32, (512, 512), 1)
    for j in range(2):
        cols = slice(j * 512, j * 512 + 512)
        d = diag[:, cols] * ((1.0 - ALPHA) / 1024)
        d = jnp.sum(jnp.where(ratio, d, 0.0), axis=1, keepdims=True)
        got = contract_rows(calib[:, cols], model_out[...]) * (ALPHA / 1024)
        got = got + d * weights[cols, :].astype(F4)
        got = got.astype(BF)
        for q in range(16):
            out[q * 2 + (xl ^ j)] = got[q * 32 : q * 32 + 32]


def numer_call(info, calib, model_out, diag, weights):
    return pl.pallas_call(
        numer_kernel,
        in_specs=[pl.BlockSpec(memory_space=pltpu.SMEM)] + [pl.BlockSpec(memory_space=pltpu.VMEM)] * 4,
        out_specs=pl.BlockSpec(memory_space=pltpu.VMEM),
        out_shape=jax.ShapeDtypeStruct((32, 32, 512), BF),
        compiler_params=pltpu.CompilerParams(vmem_limit_bytes=VMEM),
        cost_estimate=pl.CostEstimate(flops=2**29, bytes_accessed=4 * 2**20, transcendentals=0),
        name="numer",
    )(info, calib, model_out, diag, weights)


ORDER = (0, 7, 1, 6, 2, 5, 3, 4)


def slot_model(info, core, slot):
    y, xh, c = info[3], info[4], info[5]
    return lax.rem(y + slot // 2, 4) * 4 + (xh ^ (slot % 2)) * 2 + (c ^ core)


def gram_kernel(first, last, info, *refs):
    refs = list(refs)
    blocks = [refs.pop(0) for _ in range(3 if last else 2)]
    own_s, other_s = refs.pop(0), refs.pop(0)
    if first:
        own_g, other_g = refs.pop(0), refs.pop(0)
    else:
        gains, before = refs.pop(0), refs.pop(0)
    if last:
        near, far = refs.pop(0), refs.pop(0)
    else:
        acc = refs.pop(0)
    if first:
        gains = refs.pop(0)
    if last:
        acc = refs.pop(0)
    table, pick, scale, calib = refs
    step = pl.program_id(0)
    p, xl, z = info[0], info[2], info[6]

    @pl.when(step == 0)
    def _():
        if not first:
            acc[...] = before[...]
        else:
            acc[...] = jnp.zeros_like(acc)
            for core in range(2):
                src = own_g if core == 0 else other_g
                for slot in range(8):
                    m = slot_model(info, core, slot)
                    row = []
                    for b in (p, z * 2 + xl, z * 2 + (1 - xl)):
                        tile = src[slot, b // 2].astype(F4)
                        tile = tile[0:8] + tile[8:16]
                        tile = jnp.where(b % 2 == 0, tile[0:4], tile[4:8])
                        row += [tile[i : i + 1] for i in range(4)]
                    gains[pl.ds(m, 1), :] = jnp.concatenate(row, 1)
        table[:, 0:512] = blocks[0][...]

    @pl.when(step == 1)
    def _():
        if last:
            table[0:128, 0:512] = blocks[1][...]
            table[128:256, 0:512] = blocks[2][...]
        else:
            table[:, 0:512] = blocks[1][...]

    lane = lax.broadcasted_iota(jnp.int32, (16, 256), 1).astype(F4)
    models = []
    for core in range(2):
        src = own_s if core == 0 else other_s
        for slot in range(8):
            m = slot_model(info, core, slot)
            models.append(m)
            table[pl.ds(pl.multiple_of(m * 16, 16), 16), 512:1536] = src[slot, 0, :, 0:1024]
            extra = src[slot, 0, :, 1024:1152].astype(F4)
            for t in range(4):
                row = (core * 8 + slot) * 64 + t * 16
                at = t * 32
                hit = extra[:, at : at + 1] == lane
                pick[row : row + 16, :] = jnp.where(hit, 1.0, 0.0).astype(BF)
                value = extra[:, at + 1 : at + 2] + extra[:, at + 2 : at + 3] + extra[:, at + 3 : at + 4]
                scale[row : row + 16, :] = jnp.broadcast_to(value, (16, 128))

    for n in range(6):
        cols = slice(n * 256, n * 256 + 256)
        got = dot(pick[...], table[:, cols])
        for m in range(16):
            part = slice(m * 64, m * 64 + 64)
            r = scale[part, :]
            r = jnp.concatenate([r, r], 1)
            g = gains[pl.ds(models[m], 1), cols]
            calib[part, cols] = (got[part] * r * g).astype(BF)
    acc[...] += contract_rows(calib[:, 0:512], calib[:, 512:1536])

    if last:

        @pl.when(step == 1)
        def _():
            near[...] = acc[:, 0:512]
            far[...] = acc[:, 512:1024].astype(BF)


def gram_call(i, info, blocks, own_s, other_s, gains, before):
    first, last = i == 0, i == 3
    k0, k1 = ORDER[2 * i], ORDER[2 * i + 1]
    whole = lambda shape: pl.BlockSpec(shape, lambda j, info: (0,) * len(shape))
    by_z = pl.BlockSpec((8, 1, 16, 1280), lambda j, info: (0, (info[6] + k0 + j * (k1 - k0) + 8) % 8, 0, 0))
    gain_view = pl.BlockSpec((8, 8, 16, 128), lambda j, info: (0, 0, 0, 9))
    shapes = [jax.ShapeDtypeStruct((512, 1024), F4)]
    if last:
        shapes = [jax.ShapeDtypeStruct((512, 512), F4), jax.ShapeDtypeStruct((512, 512), BF)]
    if first:
        shapes.append(jax.ShapeDtypeStruct((16, 1536), F4))
    extra = [own_s, other_s] if first else [gains, before]
    extra_specs = [gain_view, gain_view] if first else [whole((16, 1536)), whole((512, 1024))]
    operands = [info, *blocks, own_s, other_s, *extra]
    return pl.pallas_call(
        lambda *refs: gram_kernel(first, last, *refs),
        grid_spec=pltpu.PrefetchScalarGridSpec(
            num_scalar_prefetch=1,
            grid=(2,),
            in_specs=[whole(b.shape) for b in blocks] + [by_z, by_z] + extra_specs,
            out_specs=[whole(o.shape) for o in shapes],
            scratch_shapes=([pltpu.VMEM((512, 1024), F4)] if last else [])
            + [
                pltpu.VMEM((256, 1536), BF),
                pltpu.VMEM((1024, 256), BF),
                pltpu.VMEM((1024, 128), F4),
                pltpu.VMEM((1024, 1536), BF),
            ],
        ),
        out_shape=shapes,
        input_output_aliases={} if first or last else {len(operands) - 1: 0},
        compiler_params=pltpu.CompilerParams(dimension_semantics=("arbitrary",), vmem_limit_bytes=VMEM),
        cost_estimate=pl.CostEstimate(flops=4 * 2**30, bytes_accessed=6 * 2**20, transcendentals=0),
        name="gram" + str(i),
    )(*operands)


def local(bank, calib_ids, norm_gains, proj_slabs):
    p = lax.axis_index("mp")
    s = lax.axis_index("shard")
    y, xh, c = p // 4, p // 2 % 2, p % 2
    z, xl = s // 2, s % 2
    info = jnp.stack([p, s, xl, y, xh, c, z]).astype(jnp.int32)
    weights = proj_slabs[0]

    piece, bank_cols = prepare(info, bank, calib_ids, norm_gains)
    own_s, other_s, weights_other, b = gather_both(piece, bank_cols, weights)
    both = jnp.concatenate([weights, weights_other], 0)

    partial_out, calib, diag = project(info, own_s, other_s, norm_gains, both)
    tie = lax.optimization_barrier
    partial_out, info = tie((partial_out, info))
    acc, gains = gram_call(0, info, [b[0], b[8]], own_s, other_s, None, None)
    partial_out, gains = tie((swap_z(partial_out), gains))
    model_out = jnp.sum(partial_out.astype(F4), 0).astype(BF)
    model_out, info = tie((jnp.broadcast_to(model_out[None], (8, 64, 512)), info))
    (acc,) = gram_call(1, info, [b[1], b[7]], own_s, other_s, gains, acc)
    model_out, acc = tie((swap_z(model_out), acc))

    numer = numer_call(info, calib, model_out.reshape(512, 512), diag, both)
    numer, info = tie((numer, info))
    (acc,) = gram_call(2, info, [b[2], b[6]], own_s, other_s, gains, acc)
    near, far = gram_call(3, info, [b[3], b[4], b[5]], own_s, other_s, gains, acc)
    numer, near = tie((lax.all_to_all(numer, AXES, 0, 0, tiled=True, axis_index_groups=XLO_GROUPS), near))
    numer = jnp.sum(numer.astype(F4), 0).astype(BF)
    numer = lax.all_to_all(jnp.broadcast_to(numer[None], (16, 32, 512)), "mp", 0, 0, tiled=True)
    numer = numer.reshape(512, 512).astype(F4)

    gram = near + shift(far, xl=1).astype(F4)
    on_diag = (p == s) & (
        lax.broadcasted_iota(jnp.int32, (512, 512), 0) == lax.broadcasted_iota(jnp.int32, (512, 512), 1)
    )
    merged_gram = gram * jnp.where(on_diag, 1.0 / 1024, ALPHA / 1024)

    return (merged_gram, numer)


def solution(mesh):
    placed = (P("shard", None), P("mp", "shard"), P("mp", None), P("mp", "shard", None))
    return jax.shard_map(
        local,
        mesh=mesh,
        in_specs=placed,
        out_specs=(P("mp", "shard"), P("shard", None)),
        check_vma=False,
    )
```

```python
import jax
import jax.numpy as jnp
from jax import lax
from jax.experimental import pallas as pl
from jax.experimental.pallas import tpu as pltpu
from jax.sharding import PartitionSpec as P

ALPHA = 0.9
EPSILON = 1e-05
BF = jnp.bfloat16
F4 = jnp.float32
VMEM = 60 * 2**20
AXES = ("mp", "shard")
Z_GROUPS = [[z * 2 + xl for z in range(8)] for xl in range(2)]
CORE_GROUPS = [[q * 2 + c for q in range(8)] for c in range(2)]
XLO_GROUPS = [[p * 16 + z * 2 + xl for p in range(16) for xl in range(2)] for z in range(8)]


def shift(x, y=0, xh=0, c=0, z=0, xl=0):
    pairs = []
    for p in range(16):
        for s in range(16):
            py, pxh, pc = p // 4, p // 2 % 2, p % 2
            sz, sxl = s // 2, s % 2
            tp = (py + y) % 4 * 4 + (pxh ^ xh) * 2 + (pc ^ c)
            ts = (sz + z) % 8 * 2 + (sxl ^ xl)
            pairs.append((p * 16 + s, tp * 16 + ts))
    return lax.ppermute(x, AXES, pairs)


def swap_z(x):
    return lax.all_to_all(x, "shard", 0, 0, tiled=True, axis_index_groups=Z_GROUPS)


def dot(a, b):
    return jnp.dot(a, b, preferred_element_type=F4)


def contract_rows(a, b):
    return lax.dot_general(a, b, (((0,), (0,)), ((), ())), preferred_element_type=F4)


def gather_mp(piece, w):
    n = len(CORE_GROUPS[0])
    sent = jnp.broadcast_to(piece[None], (n, *piece.shape)).reshape(n * piece.shape[0], *piece.shape[1:])
    own = lax.all_to_all(sent, "mp", 0, 0, tiled=True, axis_index_groups=CORE_GROUPS)
    own, w = lax.optimization_barrier((own.reshape(n, *piece.shape), shift(w, xl=1)))
    return own, shift(own, c=1), w


def prepare_kernel(info, bank, ids, gains, piece_out, cols_out, total, column, pick):
    zz = pl.program_id(0)
    p, s, xl = info[0], info[1], info[2]

    @pl.when(zz == 0)
    def _():
        i0 = lax.broadcasted_iota(jnp.int32, (64, 64), 0)
        i1 = lax.broadcasted_iota(jnp.int32, (64, 64), 1)
        row_ids = (ids[...] - s * 256).astype(F4)
        row_ids = jnp.sum(jnp.where(i0 == i1, row_ids, 0.0), axis=1, keepdims=True)
        lane = lax.broadcasted_iota(jnp.int32, (64, 256), 1).astype(F4)
        column[...] = jnp.broadcast_to(row_ids, (64, 128))
        pick[...] = jnp.where(row_ids == lane, 1.0, 0.0).astype(BF)
        total[...] = jnp.zeros_like(total)

    own_row = pl.multiple_of(p * 16, 16)
    for half in range(2):
        got = dot(pick[...], bank[:, half * 1024 : half * 1024 + 1024])
        got = got * got
        total[...] += sum(got[:, i * 128 : i * 128 + 128] for i in range(8))
        for j in range(2):
            at = pl.multiple_of(half * 1024 + (xl ^ j) * 512, 512)
            piece_out[zz * 2 + half, :, j * 512 : j * 512 + 512] = bank[pl.ds(own_row, 16), pl.ds(at, 512)]

    @pl.when(zz == p // 4)
    def _():
        cols_out[...] = bank[:, pl.ds(pl.multiple_of(p % 4 * 512, 512), 512)]

    @pl.when(zz == 3)
    def _():
        row_ids = column[:, 0:1]
        scale = lax.rsqrt(jnp.sum(total[...], axis=1, keepdims=True) / 8192 + EPSILON)
        hi = scale.astype(BF).astype(F4)
        mid = (scale - hi).astype(BF).astype(F4)
        low = scale - hi - mid
        lane = lax.broadcasted_iota(jnp.int32, (16, 128), 1)
        extra = jnp.zeros((16, 128), F4)
        for q in range(4):
            part = slice(q * 16, q * 16 + 16)
            for j, v in enumerate((row_ids, hi, mid, low)):
                extra = jnp.where(lane == q * 32 + j, v[part], extra)
        extra = extra.astype(BF)
        own = gains[:, pl.ds(pl.multiple_of(s // 2 * 1024, 1024), 1024)]
        own = jnp.concatenate([own[:, i * 128 : i * 128 + 128] for i in range(8)], 0)
        own_hi = own.astype(BF).astype(F4)
        own = jnp.concatenate([own_hi, own - own_hi], 0).astype(BF)
        for to in range(8):
            piece_out[to, :, 1024:1152] = extra
            piece_out[to, :, 1152:1280] = own


def prepare(info, bank, ids, gains):
    whole = lambda shape: pl.BlockSpec(shape, lambda i, info: (0,) * len(shape))
    return pl.pallas_call(
        prepare_kernel,
        grid_spec=pltpu.PrefetchScalarGridSpec(
            num_scalar_prefetch=1,
            grid=(4,),
            in_specs=[pl.BlockSpec((256, 2048), lambda i, info: (0, i)), whole((1, 64)), whole((1, 8192))],
            out_specs=[whole((8, 16, 1280)), whole((256, 512))],
            scratch_shapes=[pltpu.VMEM((64, 128), F4), pltpu.VMEM((64, 128), F4), pltpu.VMEM((64, 256), BF)],
        ),
        out_shape=[jax.ShapeDtypeStruct((8, 16, 1280), BF), jax.ShapeDtypeStruct((256, 512), BF)],
        compiler_params=pltpu.CompilerParams(dimension_semantics=("arbitrary",), vmem_limit_bytes=VMEM),
        cost_estimate=pl.CostEstimate(flops=2**28, bytes_accessed=5 * 2**20, transcendentals=64),
        name="prepare",
    )(info, bank, ids, gains)


def project_kernel(info, own_s, other_s, gains, weights, part_out, calib_out, diag_out, table, calib):
    zz = pl.program_id(0)
    xl, z = info[2], info[6]
    lane = lax.broadcasted_iota(jnp.int32, (16, 256), 1).astype(F4)
    for i in range(2):
        for core in range(2):
            src = own_s if core == 0 else other_s
            for slot in range(8):
                m = slot_model(info, core, slot)
                table[i, pl.ds(pl.multiple_of(m * 16, 16), 16), :] = src[slot, i, :, 0:1024]
        extra = own_s[info[3] * 2 + info[4], i, :, 1024:1152].astype(F4)
        pick, scale = [], []
        for t in range(4):
            at = t * 32
            pick.append(jnp.where(extra[:, at : at + 1] == lane, 1.0, 0.0))
            scale.append(extra[:, at + 1 : at + 2] + extra[:, at + 2 : at + 3] + extra[:, at + 3 : at + 4])
        pick = jnp.concatenate(pick, 0).astype(BF)
        scale = jnp.concatenate(scale, 0)
        rows = pl.ds(pl.multiple_of(zz * 128 + i * 64, 64), 64)
        for j in range(2):
            cols = slice(j * 512, j * 512 + 512)
            g = gains[:, pl.ds(pl.multiple_of((z * 2 + (xl ^ j)) * 512, 512), 512)]
            calib[rows, cols] = (dot(pick, table[i, :, cols]) * scale * g).astype(BF)

    @pl.when(zz == 3)
    def _():
        calib_out[...] = calib[...]
        part = dot(calib[...], weights[...]).astype(BF)
        for to in range(8):
            part_out[to] = part[to * 64 : to * 64 + 64]
        whole = calib[...].astype(F4)
        diag_out[...] = jnp.sum(whole * whole, axis=0, keepdims=True)


def project(info, own_s, other_s, gains, weights):
    whole = lambda shape: pl.BlockSpec(shape, lambda i, info: (0,) * len(shape))
    by_z = pl.BlockSpec((8, 2, 16, 1280), lambda i, info: (0, i, 0, 0))
    return pl.pallas_call(
        project_kernel,
        grid_spec=pltpu.PrefetchScalarGridSpec(
            num_scalar_prefetch=1,
            grid=(4,),
            in_specs=[by_z, by_z, whole((1, 8192)), whole((1024, 512))],
            out_specs=[whole((8, 64, 512)), whole((512, 1024)), whole((1, 1024))],
            scratch_shapes=[pltpu.VMEM((2, 256, 1024), BF), pltpu.VMEM((512, 1024), BF)],
        ),
        out_shape=[
            jax.ShapeDtypeStruct((8, 64, 512), BF),
            jax.ShapeDtypeStruct((512, 1024), BF),
            jax.ShapeDtypeStruct((1, 1024), F4),
        ],
        compiler_params=pltpu.CompilerParams(dimension_semantics=("arbitrary",), vmem_limit_bytes=VMEM),
        cost_estimate=pl.CostEstimate(flops=2**30, bytes_accessed=8 * 2**20, transcendentals=0),
        name="project",
    )(info, own_s, other_s, gains, weights)


def numer_kernel(info, calib, model_out, diag, weights, out):
    xl = info[2]
    ratio = lax.broadcasted_iota(jnp.int32, (512, 512), 0) == lax.broadcasted_iota(jnp.int32, (512, 512), 1)
    for j in range(2):
        cols = slice(j * 512, j * 512 + 512)
        d = diag[:, cols] * ((1.0 - ALPHA) / 1024)
        d = jnp.sum(jnp.where(ratio, d, 0.0), axis=1, keepdims=True)
        got = contract_rows(calib[:, cols], model_out[...]) * (ALPHA / 1024)
        got = got + d * weights[cols, :].astype(F4)
        got = got.astype(BF)
        for q in range(16):
            out[q * 2 + (xl ^ j)] = got[q * 32 : q * 32 + 32]


def numer_call(info, calib, model_out, diag, weights):
    return pl.pallas_call(
        numer_kernel,
        in_specs=[pl.BlockSpec(memory_space=pltpu.SMEM)] + [pl.BlockSpec(memory_space=pltpu.VMEM)] * 4,
        out_specs=pl.BlockSpec(memory_space=pltpu.VMEM),
        out_shape=jax.ShapeDtypeStruct((32, 32, 512), BF),
        compiler_params=pltpu.CompilerParams(vmem_limit_bytes=VMEM),
        cost_estimate=pl.CostEstimate(flops=2**29, bytes_accessed=4 * 2**20, transcendentals=0),
        name="numer",
    )(info, calib, model_out, diag, weights)


def slot_model(info, core, slot):
    return slot * 2 + (info[5] ^ core)


def gram_kernel(first, last, info, *refs):
    refs = list(refs)
    block, own_s, other_s = refs.pop(0), refs.pop(0), refs.pop(0)
    if first:
        own_g, other_g = refs.pop(0), refs.pop(0)
    else:
        gains, before = refs.pop(0), refs.pop(0)
    if last:
        near, far = refs.pop(0), refs.pop(0)
    else:
        acc = refs.pop(0)
    if first:
        gains = refs.pop(0)
    if last:
        acc = refs.pop(0)
    table, pick, scale, calib = refs
    step = pl.program_id(0)
    p, xl, z = info[0], info[2], info[6]

    @pl.when(step == 0)
    def _():
        if not first:
            acc[...] = before[...]
        else:
            acc[...] = jnp.zeros_like(acc)
            for core in range(2):
                src = own_g if core == 0 else other_g
                for slot in range(8):
                    m = slot_model(info, core, slot)
                    row = []
                    for b in (p, z * 2 + xl, z * 2 + (1 - xl)):
                        tile = src[slot, b // 2].astype(F4)
                        tile = tile[0:8] + tile[8:16]
                        tile = jnp.where(b % 2 == 0, tile[0:4], tile[4:8])
                        row += [tile[i : i + 1] for i in range(4)]
                    gains[pl.ds(m, 1), :] = jnp.concatenate(row, 1)

    table[:, 0:512] = block[0]
    lane = lax.broadcasted_iota(jnp.int32, (16, 256), 1).astype(F4)
    models = []
    for core in range(2):
        src = own_s if core == 0 else other_s
        for slot in range(8):
            m = slot_model(info, core, slot)
            models.append(m)
            table[pl.ds(pl.multiple_of(m * 16, 16), 16), 512:1536] = src[slot, 0, :, 0:1024]
            extra = src[slot, 0, :, 1024:1152].astype(F4)
            for t in range(4):
                row = (core * 8 + slot) * 64 + t * 16
                at = t * 32
                hit = extra[:, at : at + 1] == lane
                pick[row : row + 16, :] = jnp.where(hit, 1.0, 0.0).astype(BF)
                value = extra[:, at + 1 : at + 2] + extra[:, at + 2 : at + 3] + extra[:, at + 3 : at + 4]
                scale[row : row + 16, :] = jnp.broadcast_to(value, (16, 128))

    for n in range(6):
        cols = slice(n * 256, n * 256 + 256)
        got = dot(pick[...], table[:, cols])
        for m in range(16):
            part = slice(m * 64, m * 64 + 64)
            r = scale[part, :]
            r = jnp.concatenate([r, r], 1)
            g = gains[pl.ds(models[m], 1), cols]
            calib[part, cols] = (got[part] * r * g).astype(BF)
    acc[...] += contract_rows(calib[:, 0:512], calib[:, 512:1536])

    if last:

        @pl.when(step == 1)
        def _():
            near[...] = acc[:, 0:512]
            far[...] = acc[:, 512:1024].astype(BF)


def gram_call(i, info, blocks, own_s, other_s, gains, before):
    first, last = i == 0, i == 3
    whole = lambda shape: pl.BlockSpec(shape, lambda j, info: (0,) * len(shape))
    by_z = pl.BlockSpec((8, 1, 16, 1280), lambda j, info: (0, 2 * i + j, 0, 0))
    block = pl.BlockSpec((1, 256, 512), lambda j, info: (2 * i + j, 0, 0))
    gain_view = pl.BlockSpec((8, 8, 16, 128), lambda j, info: (0, 0, 0, 9))
    shapes = [jax.ShapeDtypeStruct((512, 1024), F4)]
    if last:
        shapes = [jax.ShapeDtypeStruct((512, 512), F4), jax.ShapeDtypeStruct((512, 512), BF)]
    if first:
        shapes.append(jax.ShapeDtypeStruct((16, 1536), F4))
    extra = [own_s, other_s] if first else [gains, before]
    extra_specs = [gain_view, gain_view] if first else [whole((16, 1536)), whole((512, 1024))]
    operands = [info, blocks, own_s, other_s, *extra]
    return pl.pallas_call(
        lambda *refs: gram_kernel(first, last, *refs),
        grid_spec=pltpu.PrefetchScalarGridSpec(
            num_scalar_prefetch=1,
            grid=(2,),
            in_specs=[block, by_z, by_z] + extra_specs,
            out_specs=[whole(o.shape) for o in shapes],
            scratch_shapes=([pltpu.VMEM((512, 1024), F4)] if last else [])
            + [
                pltpu.VMEM((256, 1536), BF),
                pltpu.VMEM((1024, 256), BF),
                pltpu.VMEM((1024, 128), F4),
                pltpu.VMEM((1024, 1536), BF),
            ],
        ),
        out_shape=shapes,
        input_output_aliases={} if first or last else {len(operands) - 1: 0},
        compiler_params=pltpu.CompilerParams(dimension_semantics=("arbitrary",), vmem_limit_bytes=VMEM),
        cost_estimate=pl.CostEstimate(flops=4 * 2**30, bytes_accessed=6 * 2**20, transcendentals=0),
        name="gram" + str(i),
    )(*operands)


def local(bank, calib_ids, norm_gains, proj_slabs):
    p = lax.axis_index("mp")
    s = lax.axis_index("shard")
    y, xh, c = p // 4, p // 2 % 2, p % 2
    z, xl = s // 2, s % 2
    info = jnp.stack([p, s, xl, y, xh, c, z]).astype(jnp.int32)
    weights = proj_slabs[0]

    piece, bank_cols = prepare(info, bank, calib_ids, norm_gains)
    blocks = lax.all_gather(bank_cols, "shard", axis=0, axis_index_groups=Z_GROUPS)
    own_s, other_s, weights_other = gather_mp(swap_z(piece), weights)
    both = jnp.concatenate([weights, weights_other], 0)

    partial_out, calib, diag = project(info, own_s, other_s, norm_gains, both)
    tie = lax.optimization_barrier
    partial_out, info = tie((partial_out, info))
    acc, gains = gram_call(0, info, blocks, own_s, other_s, None, None)
    partial_out, gains = tie((swap_z(partial_out), gains))
    model_out = jnp.sum(partial_out.astype(F4), 0).astype(BF)
    model_out, info = tie((jnp.broadcast_to(model_out[None], (8, 64, 512)), info))
    (acc,) = gram_call(1, info, blocks, own_s, other_s, gains, acc)
    model_out, acc = tie((swap_z(model_out), acc))

    numer = numer_call(info, calib, model_out.reshape(512, 512), diag, both)
    numer, info = tie((numer, info))
    (acc,) = gram_call(2, info, blocks, own_s, other_s, gains, acc)
    near, far = gram_call(3, info, blocks, own_s, other_s, gains, acc)
    numer, near = tie((lax.all_to_all(numer, AXES, 0, 0, tiled=True, axis_index_groups=XLO_GROUPS), near))
    numer = jnp.sum(numer.astype(F4), 0).astype(BF)
    numer = lax.all_to_all(jnp.broadcast_to(numer[None], (16, 32, 512)), "mp", 0, 0, tiled=True)
    numer = numer.reshape(512, 512).astype(F4)

    gram = near + shift(far, xl=1).astype(F4)
    on_diag = (p == s) & (
        lax.broadcasted_iota(jnp.int32, (512, 512), 0) == lax.broadcasted_iota(jnp.int32, (512, 512), 1)
    )
    merged_gram = gram * jnp.where(on_diag, 1.0 / 1024, ALPHA / 1024)

    return (merged_gram, numer)


def solution(mesh):
    placed = (P("shard", None), P("mp", "shard"), P("mp", None), P("mp", "shard", None))
    return jax.shard_map(
        local,
        mesh=mesh,
        in_specs=placed,
        out_specs=(P("mp", "shard"), P("shard", None)),
        check_vma=False,
    )
```

```python
import jax
import jax.numpy as jnp
from jax import lax
from jax.experimental import pallas as pl
from jax.experimental.pallas import tpu as pltpu
from jax.sharding import PartitionSpec as P

ALPHA = 0.9
EPSILON = 1e-05
BF = jnp.bfloat16
F4 = jnp.float32
VMEM = 60 * 2**20
AXES = ("mp", "shard")
Z_GROUPS = [[z * 2 + xl for z in range(8)] for xl in range(2)]
CORE_GROUPS = [[q * 2 + c for q in range(8)] for c in range(2)]
XLO_GROUPS = [[p * 16 + z * 2 + xl for p in range(16) for xl in range(2)] for z in range(8)]


def shift(x, y=0, xh=0, c=0, z=0, xl=0):
    pairs = []
    for p in range(16):
        for s in range(16):
            py, pxh, pc = p // 4, p // 2 % 2, p % 2
            sz, sxl = s // 2, s % 2
            tp = (py + y) % 4 * 4 + (pxh ^ xh) * 2 + (pc ^ c)
            ts = (sz + z) % 8 * 2 + (sxl ^ xl)
            pairs.append((p * 16 + s, tp * 16 + ts))
    return lax.ppermute(x, AXES, pairs)


def swap_z(x):
    return lax.all_to_all(x, "shard", 0, 0, tiled=True, axis_index_groups=Z_GROUPS)


def dot(a, b):
    return jnp.dot(a, b, preferred_element_type=F4)


def contract_rows(a, b):
    return lax.dot_general(a, b, (((0,), (0,)), ((), ())), preferred_element_type=F4)


def gather_mp(sent, w):
    own = lax.all_to_all(sent, "mp", 0, 0, tiled=True, axis_index_groups=CORE_GROUPS)
    own, w = lax.optimization_barrier((own.reshape(8, 8, 16, 1152), shift(w, xl=1)))
    return own, shift(own, c=1), w


def prepare_kernel(info, bank, ids, piece_out, cols_out, total, pick):
    zz = pl.program_id(0)
    p, s, xl = info[0], info[1], info[2]

    @pl.when(zz == 0)
    def _():
        i0 = lax.broadcasted_iota(jnp.int32, (64, 64), 0)
        i1 = lax.broadcasted_iota(jnp.int32, (64, 64), 1)
        row_ids = (ids[...] - s * 256).astype(F4)
        row_ids = jnp.sum(jnp.where(i0 == i1, row_ids, 0.0), axis=1, keepdims=True)
        lane = lax.broadcasted_iota(jnp.int32, (64, 256), 1).astype(F4)
        pick[...] = jnp.where(row_ids == lane, 1.0, 0.0).astype(BF)
        total[...] = jnp.zeros_like(total)

    own_row = pl.multiple_of(p * 16, 16)
    for half in range(2):
        got = dot(pick[...], bank[:, half * 1024 : half * 1024 + 1024])
        got = got * got
        total[...] += sum(got[:, i * 128 : i * 128 + 128] for i in range(8))
        for j in range(2):
            at = pl.multiple_of(half * 1024 + (xl ^ j) * 512, 512)
            piece_out[zz * 2 + half, :, j * 512 : j * 512 + 512] = bank[pl.ds(own_row, 16), pl.ds(at, 512)]

    @pl.when(zz == p // 4)
    def _():
        cols_out[...] = bank[:, pl.ds(pl.multiple_of(p % 4 * 512, 512), 512)]

    @pl.when(zz == 3)
    def _():
        scale = lax.rsqrt(jnp.sum(total[...], axis=1, keepdims=True) / 8192 + EPSILON)
        i0 = lax.broadcasted_iota(jnp.int32, (64, 64), 0)
        i1 = lax.broadcasted_iota(jnp.int32, (64, 64), 1)
        scale = jnp.sum(jnp.where(i0 == i1, scale, 0.0), axis=0, keepdims=True)
        hi = scale.astype(BF).astype(F4)
        mid = (scale - hi).astype(BF).astype(F4)
        low = scale - hi - mid
        first = jnp.concatenate([(ids[...] - s * 256).astype(F4), hi], 1)
        second = jnp.concatenate([mid, low], 1)
        row = lax.broadcasted_iota(jnp.int32, (16, 128), 0)
        extra = jnp.where(row == 0, first, jnp.where(row == 1, second, 0.0)).astype(BF)
        for to in range(8):
            piece_out[to, :, 1024:1152] = extra


def prepare(info, bank, ids):
    whole = lambda shape: pl.BlockSpec(shape, lambda i, info: (0,) * len(shape))
    return pl.pallas_call(
        prepare_kernel,
        grid_spec=pltpu.PrefetchScalarGridSpec(
            num_scalar_prefetch=1,
            grid=(4,),
            in_specs=[pl.BlockSpec((256, 2048), lambda i, info: (0, i)), whole((1, 64))],
            out_specs=[whole((8, 16, 1152)), whole((256, 512))],
            scratch_shapes=[pltpu.VMEM((64, 128), F4), pltpu.VMEM((64, 256), BF)],
        ),
        out_shape=[jax.ShapeDtypeStruct((8, 16, 1152), BF), jax.ShapeDtypeStruct((256, 512), BF)],
        compiler_params=pltpu.CompilerParams(dimension_semantics=("arbitrary",), vmem_limit_bytes=VMEM),
        cost_estimate=pl.CostEstimate(flops=2**28, bytes_accessed=5 * 2**20, transcendentals=64),
        name="prepare",
    )(info, bank, ids)


def address_kernel(info, piece, gains, out):
    z, xl = info[6], info[2]
    for q in range(8):
        out[q * 8 : q * 8 + 8] = piece[...]
        for i, b in enumerate((2 * q, 2 * q + 1, z * 2 + xl, z * 2 + (1 - xl))):
            at = b * 512 if i < 2 else pl.multiple_of(b * 512, 512)
            g = gains[:, pl.ds(at, 512)]
            g = jnp.concatenate([g[:, j * 128 : j * 128 + 128] for j in range(4)], 0)
            hi = g.astype(BF).astype(F4)
            top = piece[i, :, 1024:1152].astype(F4)[0:8]
            out[q * 8 + i, :, 1024:1152] = jnp.concatenate([top, hi, g - hi], 0).astype(BF)


def address(info, piece, gains):
    return pl.pallas_call(
        address_kernel,
        in_specs=[pl.BlockSpec(memory_space=pltpu.SMEM)] + [pl.BlockSpec(memory_space=pltpu.VMEM)] * 2,
        out_specs=pl.BlockSpec(memory_space=pltpu.VMEM),
        out_shape=jax.ShapeDtypeStruct((64, 16, 1152), BF),
        compiler_params=pltpu.CompilerParams(vmem_limit_bytes=VMEM),
        cost_estimate=pl.CostEstimate(flops=2**20, bytes_accessed=3 * 2**20, transcendentals=0),
        name="address",
    )(info, piece, gains)


def token_columns(tiles):
    stacked = jnp.concatenate([t.astype(F4)[0:8] for t in tiles], 0).T
    out = []
    for m in range(16):
        first, second = stacked[:, m * 8 : m * 8 + 1], stacked[:, m * 8 + 1 : m * 8 + 2]
        out.append((first[0:64], first[64:128] + second[0:64] + second[64:128]))
    return out


def project_kernel(info, own_s, other_s, gains, weights, part_out, calib_out, diag_out, table, calib):
    zz = pl.program_id(0)
    xl, z = info[2], info[6]
    lane = lax.broadcasted_iota(jnp.int32, (64, 256), 1).astype(F4)
    for i in range(2):
        for core in range(2):
            src = own_s if core == 0 else other_s
            for slot in range(8):
                m = slot_model(info, core, slot)
                table[i, pl.ds(pl.multiple_of(m * 16, 16), 16), :] = src[slot, i, :, 0:1024]
        extra = own_s[info[3] * 2 + info[4], i, :, 1024:1152]
        column, scale = token_columns([extra] * 16)[0]
        pick = jnp.where(column == lane, 1.0, 0.0).astype(BF)
        rows = pl.ds(pl.multiple_of(zz * 128 + i * 64, 64), 64)
        for j in range(2):
            cols = slice(j * 512, j * 512 + 512)
            g = gains[:, pl.ds(pl.multiple_of((z * 2 + (xl ^ j)) * 512, 512), 512)]
            calib[rows, cols] = (dot(pick, table[i, :, cols]) * scale * g).astype(BF)

    @pl.when(zz == 3)
    def _():
        calib_out[...] = calib[...]
        part = dot(calib[...], weights[...]).astype(BF)
        for to in range(8):
            part_out[to] = part[to * 64 : to * 64 + 64]
        whole = calib[...].astype(F4)
        diag_out[...] = jnp.sum(whole * whole, axis=0, keepdims=True)


def project(info, own_s, other_s, gains, weights):
    whole = lambda shape: pl.BlockSpec(shape, lambda i, info: (0,) * len(shape))
    by_z = pl.BlockSpec((8, 2, 16, 1152), lambda i, info: (0, i, 0, 0))
    return pl.pallas_call(
        project_kernel,
        grid_spec=pltpu.PrefetchScalarGridSpec(
            num_scalar_prefetch=1,
            grid=(4,),
            in_specs=[by_z, by_z, whole((1, 8192)), whole((1024, 512))],
            out_specs=[whole((8, 64, 512)), whole((512, 1024)), whole((1, 1024))],
            scratch_shapes=[pltpu.VMEM((2, 256, 1024), BF), pltpu.VMEM((512, 1024), BF)],
        ),
        out_shape=[
            jax.ShapeDtypeStruct((8, 64, 512), BF),
            jax.ShapeDtypeStruct((512, 1024), BF),
            jax.ShapeDtypeStruct((1, 1024), F4),
        ],
        compiler_params=pltpu.CompilerParams(dimension_semantics=("arbitrary",), vmem_limit_bytes=VMEM),
        cost_estimate=pl.CostEstimate(flops=2**30, bytes_accessed=8 * 2**20, transcendentals=0),
        name="project",
    )(info, own_s, other_s, gains, weights)


def numer_kernel(info, calib, model_out, diag, weights, out):
    xl = info[2]
    ratio = lax.broadcasted_iota(jnp.int32, (512, 512), 0) == lax.broadcasted_iota(jnp.int32, (512, 512), 1)
    for j in range(2):
        cols = slice(j * 512, j * 512 + 512)
        d = diag[:, cols] * ((1.0 - ALPHA) / 1024)
        d = jnp.sum(jnp.where(ratio, d, 0.0), axis=1, keepdims=True)
        got = contract_rows(calib[:, cols], model_out[...]) * (ALPHA / 1024)
        got = got + d * weights[cols, :].astype(F4)
        got = got.astype(BF)
        for q in range(16):
            out[q * 2 + (xl ^ j)] = got[q * 32 : q * 32 + 32]


def numer_call(info, calib, model_out, diag, weights):
    return pl.pallas_call(
        numer_kernel,
        in_specs=[pl.BlockSpec(memory_space=pltpu.SMEM)] + [pl.BlockSpec(memory_space=pltpu.VMEM)] * 4,
        out_specs=pl.BlockSpec(memory_space=pltpu.VMEM),
        out_shape=jax.ShapeDtypeStruct((32, 32, 512), BF),
        compiler_params=pltpu.CompilerParams(vmem_limit_bytes=VMEM),
        cost_estimate=pl.CostEstimate(flops=2**29, bytes_accessed=4 * 2**20, transcendentals=0),
        name="numer",
    )(info, calib, model_out, diag, weights)


STEPS = (3, 3, 2)


def slot_model(info, core, slot):
    return slot * 2 + (info[5] ^ core)


def gram_kernel(first, last, info, *refs):
    refs = list(refs)
    block, own_s, other_s = refs.pop(0), refs.pop(0), refs.pop(0)
    if first:
        own_g, other_g = refs.pop(0), refs.pop(0)
    else:
        gains, before = refs.pop(0), refs.pop(0)
    if last:
        near, far = refs.pop(0), refs.pop(0)
    else:
        acc = refs.pop(0)
    if first:
        gains = refs.pop(0)
    if last:
        acc = refs.pop(0)
    table, pick, scale, calib = refs
    step = pl.program_id(0)

    @pl.when(step == 0)
    def _():
        if not first:
            acc[...] = before[...]
        else:
            acc[...] = jnp.zeros_like(acc)
            for core in range(2):
                src = own_g if core == 0 else other_g
                for slot in range(8):
                    m = slot_model(info, core, slot)
                    row = []
                    for b in (info[5], 2, 3):
                        tile = src[slot, b].astype(F4)
                        tile = tile[8:12] + tile[12:16]
                        row += [tile[i : i + 1] for i in range(4)]
                    gains[pl.ds(m, 1), :] = jnp.concatenate(row, 1)

    table[:, 0:512] = block[0]
    lane = lax.broadcasted_iota(jnp.int32, (64, 256), 1).astype(F4)
    models, tiles = [], []
    for core in range(2):
        src = own_s if core == 0 else other_s
        for slot in range(8):
            m = slot_model(info, core, slot)
            models.append(m)
            table[pl.ds(pl.multiple_of(m * 16, 16), 16), 512:1536] = src[slot, 0, :, 0:1024]
            tiles.append(src[slot, 0, :, 1024:1152])
    for m, (column, value) in enumerate(token_columns(tiles)):
        part = slice(m * 64, m * 64 + 64)
        pick[part, :] = jnp.where(column == lane, 1.0, 0.0).astype(BF)
        scale[part, :] = jnp.broadcast_to(value, (64, 128))

    for n in range(6):
        cols = slice(n * 256, n * 256 + 256)
        got = dot(pick[...], table[:, cols])
        for m in range(16):
            part = slice(m * 64, m * 64 + 64)
            r = scale[part, :]
            r = jnp.concatenate([r, r], 1)
            g = gains[pl.ds(models[m], 1), cols]
            calib[part, cols] = (got[part] * r * g).astype(BF)
    acc[...] += contract_rows(calib[:, 0:512], calib[:, 512:1536])

    if last:

        @pl.when(step == STEPS[-1] - 1)
        def _():
            near[...] = acc[:, 0:512]
            far[...] = acc[:, 512:1024].astype(BF)


def gram_call(i, info, blocks, own_s, other_s, gains, before):
    first, last = i == 0, i == len(STEPS) - 1
    start, steps = sum(STEPS[:i]), STEPS[i]
    whole = lambda shape: pl.BlockSpec(shape, lambda j, info: (0,) * len(shape))
    by_z = pl.BlockSpec((8, 1, 16, 1152), lambda j, info: (0, start + j, 0, 0))
    block = pl.BlockSpec((1, 256, 512), lambda j, info: (start + j, 0, 0))
    gain_view = pl.BlockSpec((8, 8, 16, 128), lambda j, info: (0, 0, 0, 8))
    shapes = [jax.ShapeDtypeStruct((512, 1024), F4)]
    if last:
        shapes = [jax.ShapeDtypeStruct((512, 512), F4), jax.ShapeDtypeStruct((512, 512), BF)]
    if first:
        shapes.append(jax.ShapeDtypeStruct((16, 1536), F4))
    extra = [own_s, other_s] if first else [gains, before]
    extra_specs = [gain_view, gain_view] if first else [whole((16, 1536)), whole((512, 1024))]
    operands = [info, blocks, own_s, other_s, *extra]
    return pl.pallas_call(
        lambda *refs: gram_kernel(first, last, *refs),
        grid_spec=pltpu.PrefetchScalarGridSpec(
            num_scalar_prefetch=1,
            grid=(steps,),
            in_specs=[block, by_z, by_z] + extra_specs,
            out_specs=[whole(o.shape) for o in shapes],
            scratch_shapes=([pltpu.VMEM((512, 1024), F4)] if last else [])
            + [
                pltpu.VMEM((256, 1536), BF),
                pltpu.VMEM((1024, 256), BF),
                pltpu.VMEM((1024, 128), F4),
                pltpu.VMEM((1024, 1536), BF),
            ],
        ),
        out_shape=shapes,
        input_output_aliases={} if first or last else {len(operands) - 1: 0},
        compiler_params=pltpu.CompilerParams(dimension_semantics=("arbitrary",), vmem_limit_bytes=VMEM),
        cost_estimate=pl.CostEstimate(flops=steps * 2**31, bytes_accessed=6 * 2**20, transcendentals=0),
        name="gram" + str(i),
    )(*operands)


def local(bank, calib_ids, norm_gains, proj_slabs):
    p = lax.axis_index("mp")
    s = lax.axis_index("shard")
    y, xh, c = p // 4, p // 2 % 2, p % 2
    z, xl = s // 2, s % 2
    info = jnp.stack([p, s, xl, y, xh, c, z]).astype(jnp.int32)
    weights = proj_slabs[0]

    piece, bank_cols = prepare(info, bank, calib_ids)
    blocks = lax.all_gather(bank_cols, "shard", axis=0, axis_index_groups=Z_GROUPS)
    own_s, other_s, weights_other = gather_mp(address(info, swap_z(piece), norm_gains), weights)
    both = jnp.concatenate([weights, weights_other], 0)

    partial_out, calib, diag = project(info, own_s, other_s, norm_gains, both)
    tie = lax.optimization_barrier
    partial_out, info = tie((partial_out, info))
    acc, gains = gram_call(0, info, blocks, own_s, other_s, None, None)
    partial_out, gains = tie((swap_z(partial_out), gains))
    model_out = jnp.sum(partial_out.astype(F4), 0).astype(BF)
    model_out, info = tie((jnp.broadcast_to(model_out[None], (8, 64, 512)), info))
    (acc,) = gram_call(1, info, blocks, own_s, other_s, gains, acc)
    model_out, acc = tie((swap_z(model_out), acc))

    numer = numer_call(info, calib, model_out.reshape(512, 512), diag, both)
    numer, info = tie((numer, info))
    near, far = gram_call(2, info, blocks, own_s, other_s, gains, acc)
    numer, near = tie((lax.all_to_all(numer, AXES, 0, 0, tiled=True, axis_index_groups=XLO_GROUPS), near))
    numer = jnp.sum(numer.astype(F4), 0).astype(BF)
    numer = lax.all_to_all(jnp.broadcast_to(numer[None], (16, 32, 512)), "mp", 0, 0, tiled=True)
    numer = numer.reshape(512, 512).astype(F4)

    gram = near + shift(far, xl=1).astype(F4)
    on_diag = (p == s) & (
        lax.broadcasted_iota(jnp.int32, (512, 512), 0) == lax.broadcasted_iota(jnp.int32, (512, 512), 1)
    )
    merged_gram = gram * jnp.where(on_diag, 1.0 / 1024, ALPHA / 1024)

    return (merged_gram, numer)


def solution(mesh):
    placed = (P("shard", None), P("mp", "shard"), P("mp", None), P("mp", "shard", None))
    return jax.shard_map(
        local,
        mesh=mesh,
        in_specs=placed,
        out_specs=(P("mp", "shard"), P("shard", None)),
        check_vma=False,
    )
```

```python
import jax
import jax.numpy as jnp
from jax import lax
from jax.experimental import pallas as pl
from jax.experimental.pallas import tpu as pltpu
from jax.sharding import PartitionSpec as P

ALPHA = 0.9
EPSILON = 1e-05
BF = jnp.bfloat16
F4 = jnp.float32
VMEM = 60 * 2**20
AXES = ("mp", "shard")
Z_GROUPS = [[z * 2 + xl for z in range(8)] for xl in range(2)]
CORE_GROUPS = [[q * 2 + c for q in range(8)] for c in range(2)]
XLO_GROUPS = [[p * 16 + z * 2 + xl for p in range(16) for xl in range(2)] for z in range(8)]


def shift(x, y=0, xh=0, c=0, z=0, xl=0):
    pairs = []
    for p in range(16):
        for s in range(16):
            py, pxh, pc = p // 4, p // 2 % 2, p % 2
            sz, sxl = s // 2, s % 2
            tp = (py + y) % 4 * 4 + (pxh ^ xh) * 2 + (pc ^ c)
            ts = (sz + z) % 8 * 2 + (sxl ^ xl)
            pairs.append((p * 16 + s, tp * 16 + ts))
    return lax.ppermute(x, AXES, pairs)


def swap_z(x):
    return lax.all_to_all(x, "shard", 0, 0, tiled=True, axis_index_groups=Z_GROUPS)


def dot(a, b):
    return jnp.dot(a, b, preferred_element_type=F4)


def contract_rows(a, b):
    return lax.dot_general(a, b, (((0,), (0,)), ((), ())), preferred_element_type=F4)


def gather(sent, w, x):
    own = lax.all_to_all(sent, "mp", 0, 0, tiled=True, axis_index_groups=CORE_GROUPS)
    z = [x]
    u = d = x
    for _ in range(3):
        u, d = shift(u, z=1), shift(d, z=-1)
        z += [u, d]
    z += [shift(u[:128], z=1), shift(d[128:], z=-1)]
    own, w, *z = lax.optimization_barrier((own.reshape(8, 8, 16, 1152), shift(w, xl=1), *z))
    return own, shift(own, c=1), w, z


def prepare_kernel(info, bank, ids, piece_out, cols_out, total, pick):
    zz = pl.program_id(0)
    p, s, xl = info[0], info[1], info[2]

    @pl.when(zz == 0)
    def _():
        i0 = lax.broadcasted_iota(jnp.int32, (64, 64), 0)
        i1 = lax.broadcasted_iota(jnp.int32, (64, 64), 1)
        row_ids = (ids[...] - s * 256).astype(F4)
        row_ids = jnp.sum(jnp.where(i0 == i1, row_ids, 0.0), axis=1, keepdims=True)
        lane = lax.broadcasted_iota(jnp.int32, (64, 256), 1).astype(F4)
        pick[...] = jnp.where(row_ids == lane, 1.0, 0.0).astype(BF)
        total[...] = jnp.zeros_like(total)

    own_row = pl.multiple_of(p * 16, 16)
    for half in range(2):
        got = dot(pick[...], bank[:, half * 1024 : half * 1024 + 1024])
        got = got * got
        total[...] += sum(got[:, i * 128 : i * 128 + 128] for i in range(8))
        for j in range(2):
            at = pl.multiple_of(half * 1024 + (xl ^ j) * 512, 512)
            piece_out[zz * 2 + half, :, j * 512 : j * 512 + 512] = bank[pl.ds(own_row, 16), pl.ds(at, 512)]

    @pl.when(zz == p // 4)
    def _():
        cols_out[...] = bank[:, pl.ds(pl.multiple_of(p % 4 * 512, 512), 512)]

    @pl.when(zz == 3)
    def _():
        scale = lax.rsqrt(jnp.sum(total[...], axis=1, keepdims=True) / 8192 + EPSILON)
        i0 = lax.broadcasted_iota(jnp.int32, (64, 64), 0)
        i1 = lax.broadcasted_iota(jnp.int32, (64, 64), 1)
        scale = jnp.sum(jnp.where(i0 == i1, scale, 0.0), axis=0, keepdims=True)
        hi = scale.astype(BF).astype(F4)
        mid = (scale - hi).astype(BF).astype(F4)
        low = scale - hi - mid
        first = jnp.concatenate([(ids[...] - s * 256).astype(F4), hi], 1)
        second = jnp.concatenate([mid, low], 1)
        row = lax.broadcasted_iota(jnp.int32, (16, 128), 0)
        extra = jnp.where(row == 0, first, jnp.where(row == 1, second, 0.0)).astype(BF)
        for to in range(8):
            piece_out[to, :, 1024:1152] = extra


def prepare(info, bank, ids):
    whole = lambda shape: pl.BlockSpec(shape, lambda i, info: (0,) * len(shape))
    return pl.pallas_call(
        prepare_kernel,
        grid_spec=pltpu.PrefetchScalarGridSpec(
            num_scalar_prefetch=1,
            grid=(4,),
            in_specs=[pl.BlockSpec((256, 2048), lambda i, info: (0, i)), whole((1, 64))],
            out_specs=[whole((8, 16, 1152)), whole((256, 512))],
            scratch_shapes=[pltpu.VMEM((64, 128), F4), pltpu.VMEM((64, 256), BF)],
        ),
        out_shape=[jax.ShapeDtypeStruct((8, 16, 1152), BF), jax.ShapeDtypeStruct((256, 512), BF)],
        compiler_params=pltpu.CompilerParams(dimension_semantics=("arbitrary",), vmem_limit_bytes=VMEM),
        cost_estimate=pl.CostEstimate(flops=2**28, bytes_accessed=5 * 2**20, transcendentals=64),
        name="prepare",
    )(info, bank, ids)


def address_kernel(info, piece, gains, out):
    z, xl = info[6], info[2]
    for q in range(8):
        out[q * 8 : q * 8 + 8] = piece[...]
        for i, b in enumerate((2 * q, 2 * q + 1, z * 2 + xl, z * 2 + (1 - xl))):
            at = b * 512 if i < 2 else pl.multiple_of(b * 512, 512)
            g = gains[:, pl.ds(at, 512)]
            g = jnp.concatenate([g[:, j * 128 : j * 128 + 128] for j in range(4)], 0)
            hi = g.astype(BF).astype(F4)
            top = piece[i, :, 1024:1152].astype(F4)[0:8]
            out[q * 8 + i, :, 1024:1152] = jnp.concatenate([top, hi, g - hi], 0).astype(BF)


def address(info, piece, gains):
    return pl.pallas_call(
        address_kernel,
        in_specs=[pl.BlockSpec(memory_space=pltpu.SMEM)] + [pl.BlockSpec(memory_space=pltpu.VMEM)] * 2,
        out_specs=pl.BlockSpec(memory_space=pltpu.VMEM),
        out_shape=jax.ShapeDtypeStruct((64, 16, 1152), BF),
        compiler_params=pltpu.CompilerParams(vmem_limit_bytes=VMEM),
        cost_estimate=pl.CostEstimate(flops=2**20, bytes_accessed=3 * 2**20, transcendentals=0),
        name="address",
    )(info, piece, gains)


def token_columns(tiles):
    stacked = jnp.concatenate([t.astype(F4)[0:8] for t in tiles], 0).T
    out = []
    for m in range(16):
        first, second = stacked[:, m * 8 : m * 8 + 1], stacked[:, m * 8 + 1 : m * 8 + 2]
        out.append((first[0:64], first[64:128] + second[0:64] + second[64:128]))
    return out


def project_kernel(info, own_s, other_s, gains, weights, part_out, calib_out, diag_out, table, calib):
    zz = pl.program_id(0)
    xl, z = info[2], info[6]
    lane = lax.broadcasted_iota(jnp.int32, (64, 256), 1).astype(F4)
    for i in range(2):
        for core in range(2):
            src = own_s if core == 0 else other_s
            for slot in range(8):
                m = slot_model(info, core, slot)
                table[i, pl.ds(pl.multiple_of(m * 16, 16), 16), :] = src[slot, i, :, 0:1024]
        extra = own_s[info[3] * 2 + info[4], i, :, 1024:1152]
        column, scale = token_columns([extra] * 16)[0]
        pick = jnp.where(column == lane, 1.0, 0.0).astype(BF)
        rows = pl.ds(pl.multiple_of(zz * 128 + i * 64, 64), 64)
        for j in range(2):
            cols = slice(j * 512, j * 512 + 512)
            g = gains[:, pl.ds(pl.multiple_of((z * 2 + (xl ^ j)) * 512, 512), 512)]
            calib[rows, cols] = (dot(pick, table[i, :, cols]) * scale * g).astype(BF)

    @pl.when(zz == 3)
    def _():
        calib_out[...] = calib[...]
        part = dot(calib[...], weights[...]).astype(BF)
        for to in range(8):
            part_out[to] = part[to * 64 : to * 64 + 64]
        whole = calib[...].astype(F4)
        diag_out[...] = jnp.sum(whole * whole, axis=0, keepdims=True)


def project(info, own_s, other_s, gains, weights):
    whole = lambda shape: pl.BlockSpec(shape, lambda i, info: (0,) * len(shape))
    by_z = pl.BlockSpec((8, 2, 16, 1152), lambda i, info: (0, i, 0, 0))
    return pl.pallas_call(
        project_kernel,
        grid_spec=pltpu.PrefetchScalarGridSpec(
            num_scalar_prefetch=1,
            grid=(4,),
            in_specs=[by_z, by_z, whole((1, 8192)), whole((1024, 512))],
            out_specs=[whole((8, 64, 512)), whole((512, 1024)), whole((1, 1024))],
            scratch_shapes=[pltpu.VMEM((2, 256, 1024), BF), pltpu.VMEM((512, 1024), BF)],
        ),
        out_shape=[
            jax.ShapeDtypeStruct((8, 64, 512), BF),
            jax.ShapeDtypeStruct((512, 1024), BF),
            jax.ShapeDtypeStruct((1, 1024), F4),
        ],
        compiler_params=pltpu.CompilerParams(dimension_semantics=("arbitrary",), vmem_limit_bytes=VMEM),
        cost_estimate=pl.CostEstimate(flops=2**30, bytes_accessed=8 * 2**20, transcendentals=0),
        name="project",
    )(info, own_s, other_s, gains, weights)


def numer_kernel(info, calib, model_out, diag, weights, out):
    xl = info[2]
    ratio = lax.broadcasted_iota(jnp.int32, (512, 512), 0) == lax.broadcasted_iota(jnp.int32, (512, 512), 1)
    for j in range(2):
        cols = slice(j * 512, j * 512 + 512)
        d = diag[:, cols] * ((1.0 - ALPHA) / 1024)
        d = jnp.sum(jnp.where(ratio, d, 0.0), axis=1, keepdims=True)
        got = contract_rows(calib[:, cols], model_out[...]) * (ALPHA / 1024)
        got = got + d * weights[cols, :].astype(F4)
        got = got.astype(BF)
        for q in range(16):
            out[q * 2 + (xl ^ j)] = got[q * 32 : q * 32 + 32]


def numer_call(info, calib, model_out, diag, weights):
    return pl.pallas_call(
        numer_kernel,
        in_specs=[pl.BlockSpec(memory_space=pltpu.SMEM)] + [pl.BlockSpec(memory_space=pltpu.VMEM)] * 4,
        out_specs=pl.BlockSpec(memory_space=pltpu.VMEM),
        out_shape=jax.ShapeDtypeStruct((32, 32, 512), BF),
        compiler_params=pltpu.CompilerParams(vmem_limit_bytes=VMEM),
        cost_estimate=pl.CostEstimate(flops=2**29, bytes_accessed=4 * 2**20, transcendentals=0),
        name="numer",
    )(info, calib, model_out, diag, weights)


ORDER = (0, 7, 1, 6, 2, 5, 3, 4)
STEPS = (3, 3, 2)


def slot_model(info, core, slot):
    return slot * 2 + (info[5] ^ core)


def gram_kernel(first, last, info, *refs):
    refs = list(refs)
    blocks = [refs.pop(0) for _ in range(3)]
    own_s, other_s = refs.pop(0), refs.pop(0)
    if first:
        own_g, other_g = refs.pop(0), refs.pop(0)
    else:
        gains, before = refs.pop(0), refs.pop(0)
    if last:
        near, far = refs.pop(0), refs.pop(0)
    else:
        acc = refs.pop(0)
    if first:
        gains = refs.pop(0)
    if last:
        acc = refs.pop(0)
    table, pick, scale, calib = refs
    step = pl.program_id(0)

    @pl.when(step == 0)
    def _():
        if not first:
            acc[...] = before[...]
        else:
            acc[...] = jnp.zeros_like(acc)
            for core in range(2):
                src = own_g if core == 0 else other_g
                for slot in range(8):
                    m = slot_model(info, core, slot)
                    row = []
                    for b in (info[5], 2, 3):
                        tile = src[slot, b].astype(F4)
                        tile = tile[8:12] + tile[12:16]
                        row += [tile[i : i + 1] for i in range(4)]
                    gains[pl.ds(m, 1), :] = jnp.concatenate(row, 1)

    for i in range(2 if last else 3):

        @pl.when(step == i)
        def _(i=i):
            if last and i == 1:
                table[0:128, 0:512] = blocks[1][...]
                table[128:256, 0:512] = blocks[2][...]
            else:
                table[:, 0:512] = blocks[i][...]

    lane = lax.broadcasted_iota(jnp.int32, (64, 256), 1).astype(F4)
    models, tiles = [], []
    for core in range(2):
        src = own_s if core == 0 else other_s
        for slot in range(8):
            m = slot_model(info, core, slot)
            models.append(m)
            table[pl.ds(pl.multiple_of(m * 16, 16), 16), 512:1536] = src[slot, 0, :, 0:1024]
            tiles.append(src[slot, 0, :, 1024:1152])
    for m, (column, value) in enumerate(token_columns(tiles)):
        part = slice(m * 64, m * 64 + 64)
        pick[part, :] = jnp.where(column == lane, 1.0, 0.0).astype(BF)
        scale[part, :] = jnp.broadcast_to(value, (64, 128))

    for n in range(6):
        cols = slice(n * 256, n * 256 + 256)
        got = dot(pick[...], table[:, cols])
        for m in range(16):
            part = slice(m * 64, m * 64 + 64)
            r = scale[part, :]
            r = jnp.concatenate([r, r], 1)
            g = gains[pl.ds(models[m], 1), cols]
            calib[part, cols] = (got[part] * r * g).astype(BF)
    acc[...] += contract_rows(calib[:, 0:512], calib[:, 512:1536])

    if last:

        @pl.when(step == STEPS[-1] - 1)
        def _():
            near[...] = acc[:, 0:512]
            far[...] = acc[:, 512:1024].astype(BF)


def gram_call(i, info, blocks, own_s, other_s, gains, before):
    first, last = i == 0, i == len(STEPS) - 1
    start, steps = sum(STEPS[:i]), STEPS[i]
    whole = lambda shape: pl.BlockSpec(shape, lambda j, info: (0,) * len(shape))
    by_z = pl.BlockSpec((8, 1, 16, 1152), lambda j, info: (0, info[7 + start + j], 0, 0))
    gain_view = pl.BlockSpec((8, 8, 16, 128), lambda j, info: (0, 0, 0, 8))
    shapes = [jax.ShapeDtypeStruct((512, 1024), F4)]
    if last:
        shapes = [jax.ShapeDtypeStruct((512, 512), F4), jax.ShapeDtypeStruct((512, 512), BF)]
    if first:
        shapes.append(jax.ShapeDtypeStruct((16, 1536), F4))
    extra = [own_s, other_s] if first else [gains, before]
    extra_specs = [gain_view, gain_view] if first else [whole((16, 1536)), whole((512, 1024))]
    blocks = blocks[start : start + 3]
    operands = [info, *blocks, own_s, other_s, *extra]
    return pl.pallas_call(
        lambda *refs: gram_kernel(first, last, *refs),
        grid_spec=pltpu.PrefetchScalarGridSpec(
            num_scalar_prefetch=1,
            grid=(steps,),
            in_specs=[whole(b.shape) for b in blocks] + [by_z, by_z] + extra_specs,
            out_specs=[whole(o.shape) for o in shapes],
            scratch_shapes=([pltpu.VMEM((512, 1024), F4)] if last else [])
            + [
                pltpu.VMEM((256, 1536), BF),
                pltpu.VMEM((1024, 256), BF),
                pltpu.VMEM((1024, 128), F4),
                pltpu.VMEM((1024, 1536), BF),
            ],
        ),
        out_shape=shapes,
        input_output_aliases={} if first or last else {len(operands) - 1: 0},
        compiler_params=pltpu.CompilerParams(dimension_semantics=("arbitrary",), vmem_limit_bytes=VMEM),
        cost_estimate=pl.CostEstimate(flops=steps * 2**31, bytes_accessed=6 * 2**20, transcendentals=0),
        name="gram" + str(i),
    )(*operands)


def local(bank, calib_ids, norm_gains, proj_slabs):
    p = lax.axis_index("mp")
    s = lax.axis_index("shard")
    y, xh, c = p // 4, p // 2 % 2, p % 2
    z, xl = s // 2, s % 2
    info = jnp.stack([p, s, xl, y, xh, c, z] + [(z + k) % 8 for k in ORDER]).astype(jnp.int32)
    weights = proj_slabs[0]

    piece, bank_cols = prepare(info, bank, calib_ids)
    sent = address(info, swap_z(piece), norm_gains)
    own_s, other_s, weights_other, blocks = gather(sent, weights, bank_cols)
    both = jnp.concatenate([weights, weights_other], 0)

    partial_out, calib, diag = project(info, own_s, other_s, norm_gains, both)
    tie = lax.optimization_barrier
    partial_out, info = tie((partial_out, info))
    acc, gains = gram_call(0, info, blocks, own_s, other_s, None, None)
    partial_out, gains = tie((swap_z(partial_out), gains))
    model_out = jnp.sum(partial_out.astype(F4), 0).astype(BF)
    model_out, info = tie((jnp.broadcast_to(model_out[None], (8, 64, 512)), info))
    (acc,) = gram_call(1, info, blocks, own_s, other_s, gains, acc)
    model_out, acc = tie((swap_z(model_out), acc))

    numer = numer_call(info, calib, model_out.reshape(512, 512), diag, both)
    numer, info = tie((numer, info))
    near, far = gram_call(2, info, blocks, own_s, other_s, gains, acc)
    numer, near = tie((lax.all_to_all(numer, AXES, 0, 0, tiled=True, axis_index_groups=XLO_GROUPS), near))
    numer = jnp.sum(numer.astype(F4), 0).astype(BF)
    numer = lax.all_to_all(jnp.broadcast_to(numer[None], (16, 32, 512)), "mp", 0, 0, tiled=True)
    numer = numer.reshape(512, 512).astype(F4)

    gram = near + shift(far, xl=1).astype(F4)
    on_diag = (p == s) & (
        lax.broadcasted_iota(jnp.int32, (512, 512), 0) == lax.broadcasted_iota(jnp.int32, (512, 512), 1)
    )
    merged_gram = gram * jnp.where(on_diag, 1.0 / 1024, ALPHA / 1024)

    return (merged_gram, numer)


def solution(mesh):
    placed = (P("shard", None), P("mp", "shard"), P("mp", None), P("mp", "shard", None))
    return jax.shard_map(
        local,
        mesh=mesh,
        in_specs=placed,
        out_specs=(P("mp", "shard"), P("shard", None)),
        check_vma=False,
    )
```

```python
import jax
import jax.numpy as jnp
from jax import lax
from jax.experimental import pallas as pl
from jax.experimental.pallas import tpu as pltpu
from jax.sharding import PartitionSpec as P

ALPHA = 0.9
EPSILON = 1e-05
BF = jnp.bfloat16
F4 = jnp.float32
VMEM = 60 * 2**20
AXES = ("mp", "shard")
Z_GROUPS = [[z * 2 + xl for z in range(8)] for xl in range(2)]
XLO_GROUPS = [[p * 16 + z * 2 + xl for p in range(16) for xl in range(2)] for z in range(8)]


def shift(x, yp=0, xh=0, c=0, z=0, xl=0):
    pairs = []
    for p in range(16):
        for s in range(16):
            py, pxh, pc = p // 4, p // 2 % 2, p % 2
            sz, sxl = s // 2, s % 2
            tp = (py ^ yp) * 4 + (pxh ^ xh) * 2 + (pc ^ c)
            ts = (sz + z) % 8 * 2 + (sxl ^ xl)
            pairs.append((p * 16 + s, tp * 16 + ts))
    return lax.ppermute(x, AXES, pairs)


def swap_z(x):
    return lax.all_to_all(x, "shard", 0, 0, tiled=True, axis_index_groups=Z_GROUPS)


def dot(a, b):
    return jnp.dot(a, b, preferred_element_type=F4)


def contract_rows(a, b):
    return lax.dot_general(a, b, (((0,), (0,)), ((), ())), preferred_element_type=F4)


def ring(x):
    z = [x]
    u = d = x
    for _ in range(3):
        u, d = shift(u, z=1), shift(d, z=-1)
        z += [u, d]
    return z + [shift(u[:128], z=1), shift(d[128:], z=-1)]


def quarter(info, other_core, other_pair, high):
    y, xh, c = info[3], info[4], info[5]
    pair = y % 2 if high else xh
    return pl.multiple_of((c ^ other_core) * 64 + (pair ^ other_pair) * 128, 64)


def prepare_kernel(info, bank, ids, piece_out, cols_out, total, pick):
    zz = pl.program_id(0)
    p, s, xl = info[0], info[1], info[2]

    @pl.when(zz == 0)
    def _():
        i0 = lax.broadcasted_iota(jnp.int32, (64, 64), 0)
        i1 = lax.broadcasted_iota(jnp.int32, (64, 64), 1)
        row_ids = (ids[...] - s * 256).astype(F4)
        row_ids = jnp.sum(jnp.where(i0 == i1, row_ids, 0.0), axis=1, keepdims=True)
        lane = lax.broadcasted_iota(jnp.int32, (64, 256), 1).astype(F4)
        pick[...] = jnp.where(row_ids == lane, 1.0, 0.0).astype(BF)
        total[...] = jnp.zeros_like(total)

    own_row = jnp.where(info[6] < 4, quarter(info, 0, 0, False), quarter(info, 0, 0, True))
    own_row = pl.multiple_of(own_row, 64)
    for half in range(2):
        got = dot(pick[...], bank[:, half * 1024 : half * 1024 + 1024])
        got = got * got
        total[...] += sum(got[:, i * 128 : i * 128 + 128] for i in range(8))
        for j in range(2):
            at = pl.multiple_of(half * 1024 + (xl ^ j) * 512, 512)
            piece_out[zz * 2 + half, :, j * 512 : j * 512 + 512] = bank[pl.ds(own_row, 64), pl.ds(at, 512)]

    @pl.when(zz == p // 4)
    def _():
        cols_out[...] = bank[:, pl.ds(pl.multiple_of(p % 4 * 512, 512), 512)]

    @pl.when(zz == 3)
    def _():
        scale = lax.rsqrt(jnp.sum(total[...], axis=1, keepdims=True) / 8192 + EPSILON)
        i0 = lax.broadcasted_iota(jnp.int32, (64, 64), 0)
        i1 = lax.broadcasted_iota(jnp.int32, (64, 64), 1)
        scale = jnp.sum(jnp.where(i0 == i1, scale, 0.0), axis=0, keepdims=True)
        hi = scale.astype(BF).astype(F4)
        mid = (scale - hi).astype(BF).astype(F4)
        low = scale - hi - mid
        first = jnp.concatenate([(ids[...] - s * 256).astype(F4), hi], 1)
        second = jnp.concatenate([mid, low], 1)
        row = lax.broadcasted_iota(jnp.int32, (64, 128), 0)
        extra = jnp.where(row == 0, first, jnp.where(row == 1, second, 0.0)).astype(BF)
        for to in range(8):
            piece_out[to, :, 1024:1152] = extra


def prepare(info, bank, ids):
    whole = lambda shape: pl.BlockSpec(shape, lambda i, info: (0,) * len(shape))
    return pl.pallas_call(
        prepare_kernel,
        grid_spec=pltpu.PrefetchScalarGridSpec(
            num_scalar_prefetch=1,
            grid=(4,),
            in_specs=[pl.BlockSpec((256, 2048), lambda i, info: (0, i)), whole((1, 64))],
            out_specs=[whole((8, 64, 1152)), whole((256, 512))],
            scratch_shapes=[pltpu.VMEM((64, 128), F4), pltpu.VMEM((64, 256), BF)],
        ),
        out_shape=[jax.ShapeDtypeStruct((8, 64, 1152), BF), jax.ShapeDtypeStruct((256, 512), BF)],
        compiler_params=pltpu.CompilerParams(dimension_semantics=("arbitrary",), vmem_limit_bytes=VMEM),
        cost_estimate=pl.CostEstimate(flops=2**28, bytes_accessed=5 * 2**20, transcendentals=64),
        name="prepare",
    )(info, bank, ids)


def address_kernel(info, extra, gains, out):
    z, xl = info[6], info[2]
    tokens = []
    for i in range(8):
        e = extra[i].astype(F4)
        scale = e[0:1, 64:128] + e[1:2, 0:64] + e[1:2, 64:128]
        tokens.append(jnp.concatenate([e[0:1, 0:64], scale], 1))
    tokens = jnp.concatenate(tokens, 0)

    def rows(b):
        g = gains[:, pl.ds(b, 512)]
        return [g[:, j * 128 : j * 128 + 128] for j in range(4)]

    mine = rows(pl.multiple_of((z * 2 + xl) * 512, 512)) + rows(pl.multiple_of((z * 2 + 1 - xl) * 512, 512))
    mine = jnp.concatenate(mine, 0)
    for q in range(16):
        out[q, 0:8] = tokens
        out[q, 8:16] = mine
        out[q, 16:24] = jnp.concatenate(rows(q * 512) * 2, 0)


def address(info, pieces, gains):
    whole = lambda shape: pl.BlockSpec(shape, lambda i, info: (0,) * len(shape))
    return pl.pallas_call(
        address_kernel,
        grid_spec=pltpu.PrefetchScalarGridSpec(
            num_scalar_prefetch=1,
            grid=(1,),
            in_specs=[pl.BlockSpec((8, 16, 128), lambda i, info: (0, 0, 8)), whole((1, 8192))],
            out_specs=whole((16, 24, 128)),
        ),
        out_shape=jax.ShapeDtypeStruct((16, 24, 128), F4),
        cost_estimate=pl.CostEstimate(flops=2**20, bytes_accessed=2**18, transcendentals=0),
        name="address",
    )(info, pieces, gains)


def fill(info, table, i, cols, high, own, core, pair, both):
    for j, src in enumerate((own, core, pair, both)):
        table[pl.ds(quarter(info, j % 2, j // 2, high), 64), cols] = src[i, :, 0:1024]


def project_kernel(
    info, own, core, xp, yp, xc, yc, gains, weights, part_out, calib_out, diag_out, table, calib
):
    zz = pl.program_id(0)
    xl, z = info[2], info[6]
    lane = lax.broadcasted_iota(jnp.int32, (64, 256), 1).astype(F4)
    for i in range(2):

        @pl.when(zz < 2)
        def _():
            fill(info, table.at[i], i, slice(0, 1024), False, own, core, xp, xc)

        @pl.when(zz >= 2)
        def _():
            fill(info, table.at[i], i, slice(0, 1024), True, own, core, yp, yc)

        extra = own[i, 0:16, 1024:1152].astype(F4)[0:8]
        extra = jnp.concatenate([extra] * 16, 0).T
        column = extra[0:64, 0:1]
        scale = extra[64:128, 0:1] + extra[0:64, 1:2] + extra[64:128, 1:2]
        pick = jnp.where(column == lane, 1.0, 0.0).astype(BF)
        rows = pl.ds(pl.multiple_of(zz * 128 + i * 64, 64), 64)
        for j in range(2):
            cols = slice(j * 512, j * 512 + 512)
            g = gains[:, pl.ds(pl.multiple_of((z * 2 + (xl ^ j)) * 512, 512), 512)]
            calib[rows, cols] = (dot(pick, table[i, :, cols]) * scale * g).astype(BF)

    @pl.when(zz == 3)
    def _():
        calib_out[...] = calib[...]
        part = dot(calib[...], weights[...]).astype(BF)
        for to in range(8):
            part_out[to] = part[to * 64 : to * 64 + 64]
        whole = calib[...].astype(F4)
        diag_out[...] = jnp.sum(whole * whole, axis=0, keepdims=True)


def project(info, pieces, gains, weights):
    whole = lambda shape: pl.BlockSpec(shape, lambda i, info: (0,) * len(shape))
    by_z = pl.BlockSpec((2, 64, 1152), lambda i, info: (i, 0, 0))
    low = pl.BlockSpec((2, 64, 1152), lambda i, info: (jnp.minimum(i, 1), 0, 0))
    high = pl.BlockSpec((2, 64, 1152), lambda i, info: (jnp.maximum(i - 2, 0), 0, 0))
    return pl.pallas_call(
        project_kernel,
        grid_spec=pltpu.PrefetchScalarGridSpec(
            num_scalar_prefetch=1,
            grid=(4,),
            in_specs=[by_z, by_z, low, high, low, high, whole((1, 8192)), whole((1024, 512))],
            out_specs=[whole((8, 64, 512)), whole((512, 1024)), whole((1, 1024))],
            scratch_shapes=[pltpu.VMEM((2, 256, 1024), BF), pltpu.VMEM((512, 1024), BF)],
        ),
        out_shape=[
            jax.ShapeDtypeStruct((8, 64, 512), BF),
            jax.ShapeDtypeStruct((512, 1024), BF),
            jax.ShapeDtypeStruct((1, 1024), F4),
        ],
        compiler_params=pltpu.CompilerParams(dimension_semantics=("arbitrary",), vmem_limit_bytes=VMEM),
        cost_estimate=pl.CostEstimate(flops=2**30, bytes_accessed=8 * 2**20, transcendentals=0),
        name="project",
    )(info, *pieces, gains, weights)


def numer_kernel(info, calib, model_out, diag, weights, out):
    xl = info[2]
    ratio = lax.broadcasted_iota(jnp.int32, (512, 512), 0) == lax.broadcasted_iota(jnp.int32, (512, 512), 1)
    for j in range(2):
        cols = slice(j * 512, j * 512 + 512)
        d = diag[:, cols] * ((1.0 - ALPHA) / 1024)
        d = jnp.sum(jnp.where(ratio, d, 0.0), axis=1, keepdims=True)
        got = contract_rows(calib[:, cols], model_out[...]) * (ALPHA / 1024)
        got = got + d * weights[cols, :].astype(F4)
        got = got.astype(BF)
        for q in range(16):
            out[q * 2 + (xl ^ j)] = got[q * 32 : q * 32 + 32]


def numer_call(info, calib, model_out, diag, weights):
    return pl.pallas_call(
        numer_kernel,
        in_specs=[pl.BlockSpec(memory_space=pltpu.SMEM)] + [pl.BlockSpec(memory_space=pltpu.VMEM)] * 4,
        out_specs=pl.BlockSpec(memory_space=pltpu.VMEM),
        out_shape=jax.ShapeDtypeStruct((32, 32, 512), BF),
        compiler_params=pltpu.CompilerParams(vmem_limit_bytes=VMEM),
        cost_estimate=pl.CostEstimate(flops=2**29, bytes_accessed=4 * 2**20, transcendentals=0),
        name="numer",
    )(info, calib, model_out, diag, weights)


ORDER = (0, 7, 1, 6, 2, 5, 3, 4)
STEPS = (3, 3, 2)


def gram_kernel(first, last, start, info, *refs):
    refs = list(refs)
    blocks = [refs.pop(0) for _ in range(3)]
    own, core, xp, yp, xc, yc, tokens, gains = [refs.pop(0) for _ in range(8)]
    if not first:
        before = refs.pop(0)
    if last:
        near, far = refs.pop(0), refs.pop(0)
    acc, table, pick, scale, calib = refs
    step = pl.program_id(0)
    at = info[7 + start + step]

    @pl.when(step == 0)
    def _():
        acc[...] = jnp.zeros_like(acc) if first else before[...]

    for i in range(2 if last else 3):

        @pl.when(step == i)
        def _(i=i):
            if last and i == 1:
                table[0:128, 0:512] = blocks[1][...]
                table[128:256, 0:512] = blocks[2][...]
            else:
                table[:, 0:512] = blocks[i][...]

    @pl.when(at < 4)
    def _():
        fill(info, table, 0, slice(512, 1536), False, own, core, xp, xc)

    @pl.when(at >= 4)
    def _():
        fill(info, table, 0, slice(512, 1536), True, own, core, yp, yc)

    lane = lax.broadcasted_iota(jnp.int32, (64, 256), 1).astype(F4)
    z_row = lax.broadcasted_iota(jnp.int32, (16, 8, 128), 1)
    token = jnp.sum(jnp.where(z_row == at, tokens[...], 0.0), axis=1)
    token = jnp.concatenate([token, jnp.zeros((112, 128), F4)], 0).T
    for m in range(16):
        part = slice(m * 64, m * 64 + 64)
        pick[part, :] = jnp.where(token[0:64, m : m + 1] == lane, 1.0, 0.0).astype(BF)
        scale[part, :] = jnp.broadcast_to(token[64:128, m : m + 1], (64, 128))

    for n in range(6):
        cols = slice(n * 256, n * 256 + 256)
        got = dot(pick[...], table[:, cols])
        for m in range(16):
            part = slice(m * 64, m * 64 + 64)
            r = scale[part, :]
            r = jnp.concatenate([r, r], 1)
            g = gains[m : m + 1, cols]
            calib[part, cols] = (got[part] * r * g).astype(BF)
    acc[...] += contract_rows(calib[:, 0:512], calib[:, 512:1536])

    if last:

        @pl.when(step == STEPS[-1] - 1)
        def _():
            near[...] = acc[:, 0:512]
            far[...] = acc[:, 512:1024].astype(BF)


def gram_call(i, info, blocks, pieces, tokens, gains, before):
    first, last = i == 0, i == len(STEPS) - 1
    start, steps = sum(STEPS[:i]), STEPS[i]
    whole = lambda shape: pl.BlockSpec(shape, lambda j, info: (0,) * len(shape))
    by_z = pl.BlockSpec((1, 64, 1152), lambda j, info: (info[7 + start + j], 0, 0))
    low = pl.BlockSpec((1, 64, 1152), lambda j, info: (jnp.minimum(info[7 + start + j], 3), 0, 0))
    high = pl.BlockSpec((1, 64, 1152), lambda j, info: (jnp.maximum(info[7 + start + j] - 4, 0), 0, 0))
    shapes = [jax.ShapeDtypeStruct((512, 1024), F4)]
    if last:
        shapes = [jax.ShapeDtypeStruct((512, 512), F4), jax.ShapeDtypeStruct((512, 512), BF)]
    blocks = blocks[start : start + 3]
    operands = [info, *blocks, *pieces, tokens, gains] + ([] if first else [before])
    return pl.pallas_call(
        lambda *refs: gram_kernel(first, last, start, *refs),
        grid_spec=pltpu.PrefetchScalarGridSpec(
            num_scalar_prefetch=1,
            grid=(steps,),
            in_specs=[whole(b.shape) for b in blocks]
            + [by_z, by_z, low, high, low, high, whole((16, 8, 128)), whole((16, 1536))]
            + ([] if first else [whole((512, 1024))]),
            out_specs=[whole(o.shape) for o in shapes],
            scratch_shapes=([pltpu.VMEM((512, 1024), F4)] if last else [])
            + [
                pltpu.VMEM((256, 1536), BF),
                pltpu.VMEM((1024, 256), BF),
                pltpu.VMEM((1024, 128), F4),
                pltpu.VMEM((1024, 1536), BF),
            ],
        ),
        out_shape=shapes,
        input_output_aliases={} if first or last else {len(operands) - 1: 0},
        compiler_params=pltpu.CompilerParams(dimension_semantics=("arbitrary",), vmem_limit_bytes=VMEM),
        cost_estimate=pl.CostEstimate(flops=steps * 2**31, bytes_accessed=6 * 2**20, transcendentals=0),
        name="gram" + str(i),
    )(*operands)


def local(bank, calib_ids, norm_gains, proj_slabs):
    p = lax.axis_index("mp")
    s = lax.axis_index("shard")
    y, xh, c = p // 4, p // 2 % 2, p % 2
    z, xl = s // 2, s % 2
    info = jnp.stack([p, s, xl, y, xh, c, z] + [(z + k) % 8 for k in ORDER]).astype(jnp.int32)
    weights = proj_slabs[0]

    tie = lax.optimization_barrier
    piece, bank_cols = prepare(info, bank, calib_ids)
    own, weights_other = tie((swap_z(piece), shift(weights, xl=1)))
    both = jnp.concatenate([weights, weights_other], 0)
    xp, yp, core = shift(own[:4], xh=1), shift(own[4:], yp=1), shift(own, c=1)
    tokens = lax.all_to_all(address(info, own, norm_gains), "mp", 0, 0, tiled=True)
    blocks = ring(bank_cols)
    xp, yp, core, tokens = tie((xp, yp, core, tokens))
    pieces = [own, core, xp, yp, shift(xp, c=1), shift(yp, c=1)]
    gains = jnp.concatenate([tokens[:, 16:20], tokens[:, 8:16]], 1).reshape(16, 1536)
    tokens = tokens[:, 0:8]

    partial_out, calib, diag = project(info, pieces, norm_gains, both)
    partial_out, info, *blocks = tie((partial_out, info, *blocks))
    (acc,) = gram_call(0, info, blocks, pieces, tokens, gains, None)
    partial_out, acc = tie((swap_z(partial_out), acc))
    model_out = jnp.sum(partial_out.astype(F4), 0).astype(BF)
    model_out, info = tie((jnp.broadcast_to(model_out[None], (8, 64, 512)), info))
    (acc,) = gram_call(1, info, blocks, pieces, tokens, gains, acc)
    model_out, acc = tie((swap_z(model_out), acc))

    numer = numer_call(info, calib, model_out.reshape(512, 512), diag, both)
    numer, info = tie((numer, info))
    near, far = gram_call(2, info, blocks, pieces, tokens, gains, acc)
    numer, near = tie((lax.all_to_all(numer, AXES, 0, 0, tiled=True, axis_index_groups=XLO_GROUPS), near))
    numer = jnp.sum(numer.astype(F4), 0).astype(BF)
    numer = lax.all_to_all(jnp.broadcast_to(numer[None], (16, 32, 512)), "mp", 0, 0, tiled=True)
    numer = numer.reshape(512, 512).astype(F4)

    gram = near + shift(far, xl=1).astype(F4)
    on_diag = (p == s) & (
        lax.broadcasted_iota(jnp.int32, (512, 512), 0) == lax.broadcasted_iota(jnp.int32, (512, 512), 1)
    )
    merged_gram = gram * jnp.where(on_diag, 1.0 / 1024, ALPHA / 1024)

    return (merged_gram, numer)


def solution(mesh):
    placed = (P("shard", None), P("mp", "shard"), P("mp", None), P("mp", "shard", None))
    return jax.shard_map(
        local,
        mesh=mesh,
        in_specs=placed,
        out_specs=(P("mp", "shard"), P("shard", None)),
        check_vma=False,
    )
```

```python
import jax
import jax.numpy as jnp
from jax import lax
from jax.experimental import pallas as pl
from jax.experimental.pallas import tpu as pltpu
from jax.sharding import PartitionSpec as P

ALPHA = 0.9
EPSILON = 1e-05
BF = jnp.bfloat16
F4 = jnp.float32
VMEM = 60 * 2**20
AXES = ("mp", "shard")
Z_GROUPS = [[z * 2 + xl for z in range(8)] for xl in range(2)]
XLO_GROUPS = [[p * 16 + z * 2 + xl for p in range(16) for xl in range(2)] for z in range(8)]


def shift(x, yp=0, xh=0, c=0, z=0, xl=0):
    pairs = []
    for p in range(16):
        for s in range(16):
            py, pxh, pc = p // 4, p // 2 % 2, p % 2
            sz, sxl = s // 2, s % 2
            tp = (py ^ yp) * 4 + (pxh ^ xh) * 2 + (pc ^ c)
            ts = (sz + z) % 8 * 2 + (sxl ^ xl)
            pairs.append((p * 16 + s, tp * 16 + ts))
    return lax.ppermute(x, AXES, pairs)


def swap_z(x):
    return lax.all_to_all(x, "shard", 0, 0, tiled=True, axis_index_groups=Z_GROUPS)


def dot(a, b):
    return jnp.dot(a, b, preferred_element_type=F4)


def contract_rows(a, b):
    return lax.dot_general(a, b, (((0,), (0,)), ((), ())), preferred_element_type=F4)


def quarter(info, other_core, other_pair, high):
    y, xh, c = info[3], info[4], info[5]
    pair = y % 2 if high else xh
    return pl.multiple_of((c ^ other_core) * 64 + (pair ^ other_pair) * 128, 64)


def prepare_kernel(info, bank, ids, piece_out, cols_out, total, pick):
    zz = pl.program_id(0)
    p, s, xl = info[0], info[1], info[2]

    @pl.when(zz == 0)
    def _():
        i0 = lax.broadcasted_iota(jnp.int32, (64, 64), 0)
        i1 = lax.broadcasted_iota(jnp.int32, (64, 64), 1)
        row_ids = (ids[...] - s * 256).astype(F4)
        row_ids = jnp.sum(jnp.where(i0 == i1, row_ids, 0.0), axis=1, keepdims=True)
        lane = lax.broadcasted_iota(jnp.int32, (64, 256), 1).astype(F4)
        pick[...] = jnp.where(row_ids == lane, 1.0, 0.0).astype(BF)
        total[...] = jnp.zeros_like(total)

    own_row = jnp.where(info[6] < 4, quarter(info, 0, 0, False), quarter(info, 0, 0, True))
    own_row = pl.multiple_of(own_row, 64)
    for half in range(2):
        got = dot(pick[...], bank[:, half * 1024 : half * 1024 + 1024])
        got = got * got
        total[...] += sum(got[:, i * 128 : i * 128 + 128] for i in range(8))
        for j in range(2):
            at = pl.multiple_of(half * 1024 + (xl ^ j) * 512, 512)
            piece_out[zz * 2 + half, :, j * 512 : j * 512 + 512] = bank[pl.ds(own_row, 64), pl.ds(at, 512)]

    @pl.when(zz == p // 4)
    def _():
        cols_out[...] = bank[:, pl.ds(pl.multiple_of(p % 4 * 512, 512), 512)]

    @pl.when(zz == 3)
    def _():
        scale = lax.rsqrt(jnp.sum(total[...], axis=1, keepdims=True) / 8192 + EPSILON)
        i0 = lax.broadcasted_iota(jnp.int32, (64, 64), 0)
        i1 = lax.broadcasted_iota(jnp.int32, (64, 64), 1)
        scale = jnp.sum(jnp.where(i0 == i1, scale, 0.0), axis=0, keepdims=True)
        hi = scale.astype(BF).astype(F4)
        mid = (scale - hi).astype(BF).astype(F4)
        low = scale - hi - mid
        first = jnp.concatenate([(ids[...] - s * 256).astype(F4), hi], 1)
        second = jnp.concatenate([mid, low], 1)
        row = lax.broadcasted_iota(jnp.int32, (64, 128), 0)
        extra = jnp.where(row == 0, first, jnp.where(row == 1, second, 0.0)).astype(BF)
        for to in range(8):
            piece_out[to, :, 1024:1152] = extra


def prepare(info, bank, ids):
    whole = lambda shape: pl.BlockSpec(shape, lambda i, info: (0,) * len(shape))
    return pl.pallas_call(
        prepare_kernel,
        grid_spec=pltpu.PrefetchScalarGridSpec(
            num_scalar_prefetch=1,
            grid=(4,),
            in_specs=[pl.BlockSpec((256, 2048), lambda i, info: (0, i)), whole((1, 64))],
            out_specs=[whole((8, 64, 1152)), whole((256, 512))],
            scratch_shapes=[pltpu.VMEM((64, 128), F4), pltpu.VMEM((64, 256), BF)],
        ),
        out_shape=[jax.ShapeDtypeStruct((8, 64, 1152), BF), jax.ShapeDtypeStruct((256, 512), BF)],
        compiler_params=pltpu.CompilerParams(dimension_semantics=("arbitrary",), vmem_limit_bytes=VMEM),
        cost_estimate=pl.CostEstimate(flops=2**28, bytes_accessed=5 * 2**20, transcendentals=64),
        name="prepare",
    )(info, bank, ids)


def address_kernel(info, extra, gains, out):
    z, xl = info[6], info[2]
    tokens = []
    for i in range(8):
        e = extra[i].astype(F4)
        scale = e[0:1, 64:128] + e[1:2, 0:64] + e[1:2, 64:128]
        tokens.append(jnp.concatenate([e[0:1, 0:64], scale], 1))
    tokens = jnp.concatenate(tokens, 0)

    def rows(b):
        g = gains[:, pl.ds(b, 512)]
        return [g[:, j * 128 : j * 128 + 128] for j in range(4)]

    mine = rows(pl.multiple_of((z * 2 + xl) * 512, 512)) + rows(pl.multiple_of((z * 2 + 1 - xl) * 512, 512))
    mine = jnp.concatenate(mine, 0)
    for q in range(16):
        out[q, 0:8] = tokens
        out[q, 8:16] = mine
        out[q, 16:24] = jnp.concatenate(rows(q * 512) * 2, 0)


def address(info, pieces, gains):
    whole = lambda shape: pl.BlockSpec(shape, lambda i, info: (0,) * len(shape))
    return pl.pallas_call(
        address_kernel,
        grid_spec=pltpu.PrefetchScalarGridSpec(
            num_scalar_prefetch=1,
            grid=(1,),
            in_specs=[pl.BlockSpec((8, 16, 128), lambda i, info: (0, 0, 8)), whole((1, 8192))],
            out_specs=whole((16, 24, 128)),
        ),
        out_shape=jax.ShapeDtypeStruct((16, 24, 128), F4),
        cost_estimate=pl.CostEstimate(flops=2**20, bytes_accessed=2**18, transcendentals=0),
        name="address",
    )(info, pieces, gains)


def fill(info, table, i, cols, high, own, core, pair, both):
    for j, src in enumerate((own, core, pair, both)):
        table[pl.ds(quarter(info, j % 2, j // 2, high), 64), cols] = src[i, :, 0:1024]


def project_kernel(
    info, own, core, xp, yp, xc, yc, gains, weights, part_out, calib_out, diag_out, table, calib
):
    zz = pl.program_id(0)
    xl, z = info[2], info[6]
    lane = lax.broadcasted_iota(jnp.int32, (64, 256), 1).astype(F4)
    for i in range(2):

        @pl.when(zz < 2)
        def _():
            fill(info, table.at[i], i, slice(0, 1024), False, own, core, xp, xc)

        @pl.when(zz >= 2)
        def _():
            fill(info, table.at[i], i, slice(0, 1024), True, own, core, yp, yc)

        extra = own[i, 0:16, 1024:1152].astype(F4)[0:8]
        extra = jnp.concatenate([extra] * 16, 0).T
        column = extra[0:64, 0:1]
        scale = extra[64:128, 0:1] + extra[0:64, 1:2] + extra[64:128, 1:2]
        pick = jnp.where(column == lane, 1.0, 0.0).astype(BF)
        rows = pl.ds(pl.multiple_of(zz * 128 + i * 64, 64), 64)
        for j in range(2):
            cols = slice(j * 512, j * 512 + 512)
            g = gains[:, pl.ds(pl.multiple_of((z * 2 + (xl ^ j)) * 512, 512), 512)]
            calib[rows, cols] = (dot(pick, table[i, :, cols]) * scale * g).astype(BF)

    @pl.when(zz == 3)
    def _():
        calib_out[...] = calib[...]
        part = dot(calib[...], weights[...]).astype(BF)
        for to in range(8):
            part_out[to] = part[to * 64 : to * 64 + 64]
        whole = calib[...].astype(F4)
        diag_out[...] = jnp.sum(whole * whole, axis=0, keepdims=True)


def project(info, pieces, gains, weights):
    whole = lambda shape: pl.BlockSpec(shape, lambda i, info: (0,) * len(shape))
    by_z = pl.BlockSpec((2, 64, 1152), lambda i, info: (i, 0, 0))
    low = pl.BlockSpec((2, 64, 1152), lambda i, info: (jnp.minimum(i, 1), 0, 0))
    high = pl.BlockSpec((2, 64, 1152), lambda i, info: (jnp.maximum(i - 2, 0), 0, 0))
    return pl.pallas_call(
        project_kernel,
        grid_spec=pltpu.PrefetchScalarGridSpec(
            num_scalar_prefetch=1,
            grid=(4,),
            in_specs=[by_z, by_z, low, high, low, high, whole((1, 8192)), whole((1024, 512))],
            out_specs=[whole((8, 64, 512)), whole((512, 1024)), whole((1, 1024))],
            scratch_shapes=[pltpu.VMEM((2, 256, 1024), BF), pltpu.VMEM((512, 1024), BF)],
        ),
        out_shape=[
            jax.ShapeDtypeStruct((8, 64, 512), BF),
            jax.ShapeDtypeStruct((512, 1024), BF),
            jax.ShapeDtypeStruct((1, 1024), F4),
        ],
        compiler_params=pltpu.CompilerParams(dimension_semantics=("arbitrary",), vmem_limit_bytes=20 * 2**20),
        cost_estimate=pl.CostEstimate(flops=2**30, bytes_accessed=8 * 2**20, transcendentals=0),
        name="project",
    )(info, *pieces, gains, weights)


def numer_kernel(info, calib, model_out, diag, weights, out):
    xl = info[2]
    ratio = lax.broadcasted_iota(jnp.int32, (512, 512), 0) == lax.broadcasted_iota(jnp.int32, (512, 512), 1)
    for j in range(2):
        cols = slice(j * 512, j * 512 + 512)
        d = diag[:, cols] * ((1.0 - ALPHA) / 1024)
        d = jnp.sum(jnp.where(ratio, d, 0.0), axis=1, keepdims=True)
        got = contract_rows(calib[:, cols], model_out[...]) * (ALPHA / 1024)
        got = got + d * weights[cols, :].astype(F4)
        got = got.astype(BF)
        for q in range(16):
            out[q * 2 + (xl ^ j)] = got[q * 32 : q * 32 + 32]


def numer_call(info, calib, model_out, diag, weights):
    return pl.pallas_call(
        numer_kernel,
        in_specs=[pl.BlockSpec(memory_space=pltpu.SMEM)] + [pl.BlockSpec(memory_space=pltpu.VMEM)] * 4,
        out_specs=pl.BlockSpec(memory_space=pltpu.VMEM),
        out_shape=jax.ShapeDtypeStruct((32, 32, 512), BF),
        compiler_params=pltpu.CompilerParams(vmem_limit_bytes=VMEM),
        cost_estimate=pl.CostEstimate(flops=2**29, bytes_accessed=4 * 2**20, transcendentals=0),
        name="numer",
    )(info, calib, model_out, diag, weights)


ORDER = (0, 7, 1, 6, 2, 5, 3, 4)
STEPS = (3, 3, 2)


def gram_kernel(first, last, start, info, *refs):
    refs = list(refs)
    blocks = [refs.pop(0) for _ in range(3)]
    own, core, xp, yp, xc, yc, tokens, gains = [refs.pop(0) for _ in range(8)]
    if not first:
        before = refs.pop(0)
    if last:
        near, far = refs.pop(0), refs.pop(0)
    acc, table, pick, scale, calib = refs
    step = pl.program_id(0)
    at = info[7 + start + step]

    @pl.when(step == 0)
    def _():
        acc[...] = jnp.zeros_like(acc) if first else before[...]

    for i in range(2 if last else 3):

        @pl.when(step == i)
        def _(i=i):
            if last and i == 1:
                table[0:128, 0:512] = blocks[1][...]
                table[128:256, 0:512] = blocks[2][...]
            else:
                table[:, 0:512] = blocks[i][...]

    @pl.when(at < 4)
    def _():
        fill(info, table, 0, slice(512, 1536), False, own, core, xp, xc)

    @pl.when(at >= 4)
    def _():
        fill(info, table, 0, slice(512, 1536), True, own, core, yp, yc)

    lane = lax.broadcasted_iota(jnp.int32, (64, 256), 1).astype(F4)
    z_row = lax.broadcasted_iota(jnp.int32, (16, 8, 128), 1)
    token = jnp.sum(jnp.where(z_row == at, tokens[...], 0.0), axis=1)
    token = jnp.concatenate([token, jnp.zeros((112, 128), F4)], 0).T
    for m in range(16):
        part = slice(m * 64, m * 64 + 64)
        pick[part, :] = jnp.where(token[0:64, m : m + 1] == lane, 1.0, 0.0).astype(BF)
        scale[part, :] = jnp.broadcast_to(token[64:128, m : m + 1], (64, 128))

    for n in range(6):
        cols = slice(n * 256, n * 256 + 256)
        got = dot(pick[...], table[:, cols])
        for m in range(16):
            part = slice(m * 64, m * 64 + 64)
            r = scale[part, :]
            r = jnp.concatenate([r, r], 1)
            g = gains[m : m + 1, cols]
            calib[part, cols] = (got[part] * r * g).astype(BF)
    acc[...] += contract_rows(calib[:, 0:512], calib[:, 512:1536])

    if last:

        @pl.when(step == STEPS[-1] - 1)
        def _():
            near[...] = acc[:, 0:512]
            far[...] = acc[:, 512:1024].astype(BF)


def gram_call(i, info, blocks, pieces, tokens, gains, before):
    first, last = i == 0, i == len(STEPS) - 1
    start, steps = sum(STEPS[:i]), STEPS[i]
    whole = lambda shape: pl.BlockSpec(shape, lambda j, info: (0,) * len(shape))
    by_z = pl.BlockSpec((1, 64, 1152), lambda j, info: (info[7 + start + j], 0, 0))
    low = pl.BlockSpec((1, 64, 1152), lambda j, info: (jnp.minimum(info[7 + start + j], 3), 0, 0))
    high = pl.BlockSpec((1, 64, 1152), lambda j, info: (jnp.maximum(info[7 + start + j] - 4, 0), 0, 0))
    shapes = [jax.ShapeDtypeStruct((512, 1024), F4)]
    if last:
        shapes = [jax.ShapeDtypeStruct((512, 512), F4), jax.ShapeDtypeStruct((512, 512), BF)]
    operands = [info, *blocks, *pieces, tokens, gains] + ([] if first else [before])
    return pl.pallas_call(
        lambda *refs: gram_kernel(first, last, start, *refs),
        grid_spec=pltpu.PrefetchScalarGridSpec(
            num_scalar_prefetch=1,
            grid=(steps,),
            in_specs=[whole(b.shape) for b in blocks]
            + [by_z, by_z, low, high, low, high, whole((16, 8, 128)), whole((16, 1536))]
            + ([] if first else [whole((512, 1024))]),
            out_specs=[whole(o.shape) for o in shapes],
            scratch_shapes=([pltpu.VMEM((512, 1024), F4)] if last else [])
            + [
                pltpu.VMEM((256, 1536), BF),
                pltpu.VMEM((1024, 256), BF),
                pltpu.VMEM((1024, 128), F4),
                pltpu.VMEM((1024, 1536), BF),
            ],
        ),
        out_shape=shapes,
        input_output_aliases={} if first or last else {len(operands) - 1: 0},
        compiler_params=pltpu.CompilerParams(dimension_semantics=("arbitrary",), vmem_limit_bytes=VMEM),
        cost_estimate=pl.CostEstimate(flops=steps * 2**31, bytes_accessed=6 * 2**20, transcendentals=0),
        name="gram" + str(i),
    )(*operands)


def local(bank, calib_ids, norm_gains, proj_slabs):
    p = lax.axis_index("mp")
    s = lax.axis_index("shard")
    y, xh, c = p // 4, p // 2 % 2, p % 2
    z, xl = s // 2, s % 2
    info = jnp.stack([p, s, xl, y, xh, c, z] + [(z + k) % 8 for k in ORDER]).astype(jnp.int32)
    weights = proj_slabs[0]

    tie = lax.optimization_barrier
    piece, bank_cols = prepare(info, bank, calib_ids)
    own, both = tie((swap_z(piece), jnp.concatenate([weights, shift(weights, xl=1)], 0)))
    xp, yp, core = shift(own[:4], xh=1), shift(own[4:], yp=1), shift(own, c=1)
    tokens = lax.all_to_all(address(info, own, norm_gains), "mp", 0, 0, tiled=True)
    u1, d1 = shift(bank_cols, z=1), shift(bank_cols, z=-1)
    xp, yp, core, tokens, u1, d1 = tie((xp, yp, core, tokens, u1, d1))
    pieces = [own, core, xp, yp, shift(xp, c=1), shift(yp, c=1)]
    gains = jnp.concatenate([tokens[:, 16:20], tokens[:, 8:16]], 1).reshape(16, 1536)
    tokens = tokens[:, 0:8]

    partial_out, calib, diag = project(info, pieces, norm_gains, both)
    u2, d2 = shift(u1, z=1), shift(d1, z=-1)
    partial_out, info, u2, d2 = tie((partial_out, info, u2, d2))
    (acc,) = gram_call(0, info, [bank_cols, u1, d1], pieces, tokens, gains, None)
    u3, d3 = shift(u2, z=1), shift(d2, z=-1)
    partial_out, acc, u3, d3 = tie((swap_z(partial_out), acc, u3, d3))
    model_out = jnp.sum(partial_out.astype(F4), 0).astype(BF)
    model_out, info = tie((jnp.broadcast_to(model_out[None], (8, 64, 512)), info))
    (acc,) = gram_call(1, info, [u2, d2, u3], pieces, tokens, gains, acc)
    far = [shift(u3[:128], z=1), shift(d3[128:], z=-1)]
    model_out, acc, *far = tie((swap_z(model_out), acc, *far))

    numer = numer_call(info, calib, model_out.reshape(512, 512), diag, both)
    numer, info = tie((numer, info))
    near, far = gram_call(2, info, [d3, *far], pieces, tokens, gains, acc)
    numer, near = tie((lax.all_to_all(numer, AXES, 0, 0, tiled=True, axis_index_groups=XLO_GROUPS), near))
    numer = jnp.sum(numer.astype(F4), 0).astype(BF)
    numer = lax.all_to_all(jnp.broadcast_to(numer[None], (16, 32, 512)), "mp", 0, 0, tiled=True)
    numer = numer.reshape(512, 512).astype(F4)

    gram = near + shift(far, xl=1).astype(F4)
    on_diag = (p == s) & (
        lax.broadcasted_iota(jnp.int32, (512, 512), 0) == lax.broadcasted_iota(jnp.int32, (512, 512), 1)
    )
    merged_gram = gram * jnp.where(on_diag, 1.0 / 1024, ALPHA / 1024)

    return (merged_gram, numer)


def solution(mesh):
    placed = (P("shard", None), P("mp", "shard"), P("mp", None), P("mp", "shard", None))
    return jax.shard_map(
        local,
        mesh=mesh,
        in_specs=placed,
        out_specs=(P("mp", "shard"), P("shard", None)),
        check_vma=False,
    )
```

```python
import jax
import jax.numpy as jnp
from jax import lax
from jax.experimental import pallas as pl
from jax.experimental.pallas import tpu as pltpu
from jax.sharding import PartitionSpec as P

ALPHA = 0.9
EPSILON = 1e-05
BF = jnp.bfloat16
F4 = jnp.float32
VMEM = 60 * 2**20
AXES = ("mp", "shard")
Z_GROUPS = [[z * 2 + xl for z in range(8)] for xl in range(2)]
XLO_GROUPS = [[p * 16 + z * 2 + xl for p in range(16) for xl in range(2)] for z in range(8)]


def shift(x, yp=0, xh=0, c=0, z=0, xl=0):
    pairs = []
    for p in range(16):
        for s in range(16):
            py, pxh, pc = p // 4, p // 2 % 2, p % 2
            sz, sxl = s // 2, s % 2
            tp = (py ^ yp) * 4 + (pxh ^ xh) * 2 + (pc ^ c)
            ts = (sz + z) % 8 * 2 + (sxl ^ xl)
            pairs.append((p * 16 + s, tp * 16 + ts))
    return lax.ppermute(x, AXES, pairs)


def swap_z(x):
    return lax.all_to_all(x, "shard", 0, 0, tiled=True, axis_index_groups=Z_GROUPS)


def dot(a, b):
    return jnp.dot(a, b, preferred_element_type=F4)


def contract_rows(a, b):
    return lax.dot_general(a, b, (((0,), (0,)), ((), ())), preferred_element_type=F4)


def quarter(info, other_core, other_pair, high):
    y, xh, c = info[3], info[4], info[5]
    pair = y % 2 if high else xh
    return pl.multiple_of((c ^ other_core) * 64 + (pair ^ other_pair) * 128, 64)


def prepare_kernel(info, bank, ids, piece_out, cols_out, total, pick):
    zz = pl.program_id(0)
    p, s, xl = info[0], info[1], info[2]

    @pl.when(zz == 0)
    def _():
        i0 = lax.broadcasted_iota(jnp.int32, (64, 64), 0)
        i1 = lax.broadcasted_iota(jnp.int32, (64, 64), 1)
        row_ids = (ids[...] - s * 256).astype(F4)
        row_ids = jnp.sum(jnp.where(i0 == i1, row_ids, 0.0), axis=1, keepdims=True)
        lane = lax.broadcasted_iota(jnp.int32, (64, 256), 1).astype(F4)
        pick[...] = jnp.where(row_ids == lane, 1.0, 0.0).astype(BF)
        total[...] = jnp.zeros_like(total)

    own_row = jnp.where(info[6] < 4, quarter(info, 0, 0, False), quarter(info, 0, 0, True))
    own_row = pl.multiple_of(own_row, 64)
    for half in range(2):
        got = dot(pick[...], bank[:, half * 1024 : half * 1024 + 1024])
        got = got * got
        total[...] += sum(got[:, i * 128 : i * 128 + 128] for i in range(8))
        for j in range(2):
            at = pl.multiple_of(half * 1024 + (xl ^ j) * 512, 512)
            piece_out[zz * 2 + half, :, j * 512 : j * 512 + 512] = bank[pl.ds(own_row, 64), pl.ds(at, 512)]

    @pl.when(zz == p // 4)
    def _():
        cols_out[...] = bank[:, pl.ds(pl.multiple_of(p % 4 * 512, 512), 512)]

    @pl.when(zz == 3)
    def _():
        scale = lax.rsqrt(jnp.sum(total[...], axis=1, keepdims=True) / 8192 + EPSILON)
        i0 = lax.broadcasted_iota(jnp.int32, (64, 64), 0)
        i1 = lax.broadcasted_iota(jnp.int32, (64, 64), 1)
        scale = jnp.sum(jnp.where(i0 == i1, scale, 0.0), axis=0, keepdims=True)
        hi = scale.astype(BF).astype(F4)
        mid = (scale - hi).astype(BF).astype(F4)
        low = scale - hi - mid
        first = jnp.concatenate([(ids[...] - s * 256).astype(F4), hi], 1)
        second = jnp.concatenate([mid, low], 1)
        row = lax.broadcasted_iota(jnp.int32, (64, 128), 0)
        extra = jnp.where(row == 0, first, jnp.where(row == 1, second, 0.0)).astype(BF)
        for to in range(8):
            piece_out[to, :, 1024:1152] = extra


def prepare(info, bank, ids):
    whole = lambda shape: pl.BlockSpec(shape, lambda i, info: (0,) * len(shape))
    return pl.pallas_call(
        prepare_kernel,
        grid_spec=pltpu.PrefetchScalarGridSpec(
            num_scalar_prefetch=1,
            grid=(4,),
            in_specs=[pl.BlockSpec((256, 2048), lambda i, info: (0, i)), whole((1, 64))],
            out_specs=[whole((8, 64, 1152)), whole((256, 512))],
            scratch_shapes=[pltpu.VMEM((64, 128), F4), pltpu.VMEM((64, 256), BF)],
        ),
        out_shape=[jax.ShapeDtypeStruct((8, 64, 1152), BF), jax.ShapeDtypeStruct((256, 512), BF)],
        compiler_params=pltpu.CompilerParams(dimension_semantics=("arbitrary",), vmem_limit_bytes=VMEM),
        cost_estimate=pl.CostEstimate(flops=2**28, bytes_accessed=5 * 2**20, transcendentals=64),
        name="prepare",
    )(info, bank, ids)


def address_kernel(info, extra, gains, out):
    z, xl = info[6], info[2]
    tokens = []
    for i in range(8):
        e = extra[i].astype(F4)
        scale = e[0:1, 64:128] + e[1:2, 0:64] + e[1:2, 64:128]
        tokens.append(jnp.concatenate([e[0:1, 0:64], scale], 1))
    tokens = jnp.concatenate(tokens, 0)

    def rows(b):
        g = gains[:, pl.ds(b, 512)]
        return [g[:, j * 128 : j * 128 + 128] for j in range(4)]

    mine = rows(pl.multiple_of((z * 2 + xl) * 512, 512)) + rows(pl.multiple_of((z * 2 + 1 - xl) * 512, 512))
    mine = jnp.concatenate(mine, 0)
    for q in range(16):
        out[q, 0:8] = tokens
        out[q, 8:16] = mine
        out[q, 16:24] = jnp.concatenate(rows(q * 512) * 2, 0)


def address(info, pieces, gains):
    whole = lambda shape: pl.BlockSpec(shape, lambda i, info: (0,) * len(shape))
    return pl.pallas_call(
        address_kernel,
        grid_spec=pltpu.PrefetchScalarGridSpec(
            num_scalar_prefetch=1,
            grid=(1,),
            in_specs=[pl.BlockSpec((8, 16, 128), lambda i, info: (0, 0, 8)), whole((1, 8192))],
            out_specs=whole((16, 24, 128)),
        ),
        out_shape=jax.ShapeDtypeStruct((16, 24, 128), F4),
        cost_estimate=pl.CostEstimate(flops=2**20, bytes_accessed=2**18, transcendentals=0),
        name="address",
    )(info, pieces, gains)


def fill(info, table, i, cols, high, own, core, pair, both):
    for j, src in enumerate((own, core, pair, both)):
        table[pl.ds(quarter(info, j % 2, j // 2, high), 64), cols] = src[i, :, 0:1024]


def project_kernel(
    info, own, core, xp, yp, xc, yc, gains, weights, part_out, calib_out, diag_out, table, calib
):
    zz = pl.program_id(0)
    xl, z = info[2], info[6]
    lane = lax.broadcasted_iota(jnp.int32, (64, 256), 1).astype(F4)
    for i in range(2):

        @pl.when(zz < 2)
        def _():
            fill(info, table.at[i], i, slice(0, 1024), False, own, core, xp, xc)

        @pl.when(zz >= 2)
        def _():
            fill(info, table.at[i], i, slice(0, 1024), True, own, core, yp, yc)

        extra = own[i, 0:16, 1024:1152].astype(F4)[0:8]
        extra = jnp.concatenate([extra] * 16, 0).T
        column = extra[0:64, 0:1]
        scale = extra[64:128, 0:1] + extra[0:64, 1:2] + extra[64:128, 1:2]
        pick = jnp.where(column == lane, 1.0, 0.0).astype(BF)
        rows = pl.ds(pl.multiple_of(zz * 128 + i * 64, 64), 64)
        for j in range(2):
            cols = slice(j * 512, j * 512 + 512)
            g = gains[:, pl.ds(pl.multiple_of((z * 2 + (xl ^ j)) * 512, 512), 512)]
            calib[rows, cols] = (dot(pick, table[i, :, cols]) * scale * g).astype(BF)

    @pl.when(zz == 3)
    def _():
        calib_out[...] = calib[...]
        part = dot(calib[...], weights[...]).astype(BF)
        for to in range(8):
            part_out[to] = part[to * 64 : to * 64 + 64]
        whole = calib[...].astype(F4)
        diag_out[...] = jnp.sum(whole * whole, axis=0, keepdims=True)


def project(info, pieces, gains, weights):
    whole = lambda shape: pl.BlockSpec(shape, lambda i, info: (0,) * len(shape))
    by_z = pl.BlockSpec((2, 64, 1152), lambda i, info: (i, 0, 0))
    low = pl.BlockSpec((2, 64, 1152), lambda i, info: (jnp.minimum(i, 1), 0, 0))
    high = pl.BlockSpec((2, 64, 1152), lambda i, info: (jnp.maximum(i - 2, 0), 0, 0))
    return pl.pallas_call(
        project_kernel,
        grid_spec=pltpu.PrefetchScalarGridSpec(
            num_scalar_prefetch=1,
            grid=(4,),
            in_specs=[by_z, by_z, low, high, low, high, whole((1, 8192)), whole((1024, 512))],
            out_specs=[whole((8, 64, 512)), whole((512, 1024)), whole((1, 1024))],
            scratch_shapes=[pltpu.VMEM((2, 256, 1024), BF), pltpu.VMEM((512, 1024), BF)],
        ),
        out_shape=[
            jax.ShapeDtypeStruct((8, 64, 512), BF),
            jax.ShapeDtypeStruct((512, 1024), BF),
            jax.ShapeDtypeStruct((1, 1024), F4),
        ],
        compiler_params=pltpu.CompilerParams(dimension_semantics=("arbitrary",), vmem_limit_bytes=20 * 2**20),
        cost_estimate=pl.CostEstimate(flops=2**30, bytes_accessed=8 * 2**20, transcendentals=0),
        name="project",
    )(info, *pieces, gains, weights)


def numer_kernel(info, calib, model_out, diag, weights, out):
    xl = info[2]
    ratio = lax.broadcasted_iota(jnp.int32, (512, 512), 0) == lax.broadcasted_iota(jnp.int32, (512, 512), 1)
    for j in range(2):
        cols = slice(j * 512, j * 512 + 512)
        d = diag[:, cols] * ((1.0 - ALPHA) / 1024)
        d = jnp.sum(jnp.where(ratio, d, 0.0), axis=1, keepdims=True)
        got = contract_rows(calib[:, cols], model_out[...]) * (ALPHA / 1024)
        got = got + d * weights[cols, :].astype(F4)
        got = got.astype(BF)
        for q in range(16):
            out[q * 2 + (xl ^ j)] = got[q * 32 : q * 32 + 32]


def numer_call(info, calib, model_out, diag, weights):
    return pl.pallas_call(
        numer_kernel,
        in_specs=[pl.BlockSpec(memory_space=pltpu.SMEM)] + [pl.BlockSpec(memory_space=pltpu.VMEM)] * 4,
        out_specs=pl.BlockSpec(memory_space=pltpu.VMEM),
        out_shape=jax.ShapeDtypeStruct((32, 32, 512), BF),
        compiler_params=pltpu.CompilerParams(vmem_limit_bytes=VMEM),
        cost_estimate=pl.CostEstimate(flops=2**29, bytes_accessed=4 * 2**20, transcendentals=0),
        name="numer",
    )(info, calib, model_out, diag, weights)


ORDER = (0, 7, 1, 6, 2, 5, 3, 4)
STEPS = (3, 3, 2)


def gram_kernel(first, last, start, info, *refs):
    refs = list(refs)
    blocks = [refs.pop(0) for _ in range(3)]
    own, core, xp, yp, xc, yc, tokens, gains = [refs.pop(0) for _ in range(8)]
    if not first:
        before = refs.pop(0)
    if last:
        near, far = refs.pop(0), refs.pop(0)
    acc, table, pick, scale, calib = refs
    step = pl.program_id(0)
    at = info[7 + start + step]

    @pl.when(step == 0)
    def _():
        acc[...] = jnp.zeros_like(acc) if first else before[...]

    for i in range(2 if last else 3):

        @pl.when(step == i)
        def _(i=i):
            if last and i == 1:
                table[0:128, 0:512] = blocks[1][...]
                table[128:256, 0:512] = blocks[2][...]
            else:
                table[:, 0:512] = blocks[i][...]

    @pl.when(at < 4)
    def _():
        fill(info, table, 0, slice(512, 1536), False, own, core, xp, xc)

    @pl.when(at >= 4)
    def _():
        fill(info, table, 0, slice(512, 1536), True, own, core, yp, yc)

    lane = lax.broadcasted_iota(jnp.int32, (64, 256), 1).astype(F4)
    z_row = lax.broadcasted_iota(jnp.int32, (16, 8, 128), 1)
    token = jnp.sum(jnp.where(z_row == at, tokens[...], 0.0), axis=1)
    token = jnp.concatenate([token, jnp.zeros((112, 128), F4)], 0).T
    for m in range(16):
        part = slice(m * 64, m * 64 + 64)
        pick[part, :] = jnp.where(token[0:64, m : m + 1] == lane, 1.0, 0.0).astype(BF)
        scale[part, :] = jnp.broadcast_to(token[64:128, m : m + 1], (64, 128))

    for n in range(6):
        cols = slice(n * 256, n * 256 + 256)
        got = dot(pick[...], table[:, cols])
        for m in range(16):
            part = slice(m * 64, m * 64 + 64)
            r = scale[part, :]
            r = jnp.concatenate([r, r], 1)
            g = gains[m : m + 1, cols]
            calib[part, cols] = (got[part] * r * g).astype(BF)
    acc[...] += contract_rows(calib[:, 0:512], calib[:, 512:1536])

    if last:

        @pl.when(step == STEPS[-1] - 1)
        def _():
            near[...] = acc[:, 0:512]
            far[...] = acc[:, 512:1024].astype(BF)


def gram_call(i, info, blocks, pieces, tokens, gains, before):
    first, last = i == 0, i == len(STEPS) - 1
    start, steps = sum(STEPS[:i]), STEPS[i]
    whole = lambda shape: pl.BlockSpec(shape, lambda j, info: (0,) * len(shape))
    by_z = pl.BlockSpec((1, 64, 1152), lambda j, info: (info[7 + start + j], 0, 0))
    low = pl.BlockSpec((1, 64, 1152), lambda j, info: (jnp.minimum(info[7 + start + j], 3), 0, 0))
    high = pl.BlockSpec((1, 64, 1152), lambda j, info: (jnp.maximum(info[7 + start + j] - 4, 0), 0, 0))
    shapes = [jax.ShapeDtypeStruct((512, 1024), F4)]
    if last:
        shapes = [jax.ShapeDtypeStruct((512, 512), F4), jax.ShapeDtypeStruct((512, 512), BF)]
    operands = [info, *blocks, *pieces, tokens, gains] + ([] if first else [before])
    return pl.pallas_call(
        lambda *refs: gram_kernel(first, last, start, *refs),
        grid_spec=pltpu.PrefetchScalarGridSpec(
            num_scalar_prefetch=1,
            grid=(steps,),
            in_specs=[whole(b.shape) for b in blocks]
            + [by_z, by_z, low, high, low, high, whole((16, 8, 128)), whole((16, 1536))]
            + ([] if first else [whole((512, 1024))]),
            out_specs=[whole(o.shape) for o in shapes],
            scratch_shapes=([pltpu.VMEM((512, 1024), F4)] if last else [])
            + [
                pltpu.VMEM((256, 1536), BF),
                pltpu.VMEM((1024, 256), BF),
                pltpu.VMEM((1024, 128), F4),
                pltpu.VMEM((1024, 1536), BF),
            ],
        ),
        out_shape=shapes,
        input_output_aliases={} if first or last else {len(operands) - 1: 0},
        compiler_params=pltpu.CompilerParams(dimension_semantics=("arbitrary",), vmem_limit_bytes=VMEM),
        cost_estimate=pl.CostEstimate(flops=steps * 2**31, bytes_accessed=6 * 2**20, transcendentals=0),
        name="gram" + str(i),
    )(*operands)


def local(bank, calib_ids, norm_gains, proj_slabs):
    p = lax.axis_index("mp")
    s = lax.axis_index("shard")
    y, xh, c = p // 4, p // 2 % 2, p % 2
    z, xl = s // 2, s % 2
    info = jnp.stack([p, s, xl, y, xh, c, z] + [(z + k) % 8 for k in ORDER]).astype(jnp.int32)
    weights = proj_slabs[0]

    tie = lax.optimization_barrier
    piece, bank_cols = prepare(info, bank, calib_ids)
    own, both = tie((swap_z(piece), jnp.concatenate([weights, shift(weights, xl=1)], 0)))
    xp, yp, core = shift(own[:4], xh=1), shift(own[4:], yp=1), shift(own, c=1)
    tokens = lax.all_to_all(address(info, own, norm_gains), "mp", 0, 0, tiled=True)
    u1, d1 = shift(bank_cols, z=1), shift(bank_cols, z=-1)
    xp, yp, core, tokens, u1, d1 = tie((xp, yp, core, tokens, u1, d1))
    gains = jnp.concatenate([tokens[:, 16:20], tokens[:, 8:16]], 1).reshape(16, 1536)
    xc, yc, gains, tokens = tie((shift(xp, c=1), shift(yp, c=1), gains, tokens[:, 0:8]))
    pieces = [own, core, xp, yp, xc, yc]

    partial_out, calib, diag = project(info, pieces, norm_gains, both)
    u2, d2 = shift(u1, z=1), shift(d1, z=-1)
    partial_out, info, u2, d2 = tie((partial_out, info, u2, d2))
    (acc,) = gram_call(0, info, [bank_cols, u1, d1], pieces, tokens, gains, None)
    u3, d3 = shift(u2, z=1), shift(d2, z=-1)
    partial_out, acc = tie((swap_z(partial_out), acc))
    model_out = jnp.sum(partial_out.astype(F4), 0).astype(BF)
    model_out, info, u3, d3 = tie((jnp.broadcast_to(model_out[None], (8, 64, 512)), info, u3, d3))
    (acc,) = gram_call(1, info, [u2, d2, u3], pieces, tokens, gains, acc)
    far = [shift(u3[:128], z=1), shift(d3[128:], z=-1)]
    model_out, acc, *far = tie((swap_z(model_out), acc, *far))

    numer = numer_call(info, calib, model_out.reshape(512, 512), diag, both)
    numer, info = tie((numer, info))
    near, far = gram_call(2, info, [d3, *far], pieces, tokens, gains, acc)
    numer, near = tie((lax.all_to_all(numer, AXES, 0, 0, tiled=True, axis_index_groups=XLO_GROUPS), near))
    numer = jnp.sum(numer.astype(F4), 0).astype(BF)
    numer = lax.all_to_all(jnp.broadcast_to(numer[None], (16, 32, 512)), "mp", 0, 0, tiled=True)
    numer = numer.reshape(512, 512).astype(F4)

    gram = near + shift(far, xl=1).astype(F4)
    on_diag = (p == s) & (
        lax.broadcasted_iota(jnp.int32, (512, 512), 0) == lax.broadcasted_iota(jnp.int32, (512, 512), 1)
    )
    merged_gram = gram * jnp.where(on_diag, 1.0 / 1024, ALPHA / 1024)

    return (merged_gram, numer)


def solution(mesh):
    placed = (P("shard", None), P("mp", "shard"), P("mp", None), P("mp", "shard", None))
    return jax.shard_map(
        local,
        mesh=mesh,
        in_specs=placed,
        out_specs=(P("mp", "shard"), P("shard", None)),
        check_vma=False,
    )
```

```python
import jax
import jax.numpy as jnp
from jax import lax
from jax.experimental import pallas as pl
from jax.experimental.pallas import tpu as pltpu
from jax.sharding import PartitionSpec as P

ALPHA = 0.9
EPSILON = 1e-05
BF = jnp.bfloat16
F4 = jnp.float32
VMEM = 60 * 2**20
AXES = ("mp", "shard")
Z_GROUPS = [[z * 2 + xl for z in range(8)] for xl in range(2)]
CORE_GROUPS = [[q * 2 + c for q in range(8)] for c in range(2)]
XLO_GROUPS = [[p * 16 + z * 2 + xl for p in range(16) for xl in range(2)] for z in range(8)]


def shift(x, y=0, xh=0, c=0, z=0, xl=0):
    pairs = []
    for p in range(16):
        for s in range(16):
            py, pxh, pc = p // 4, p // 2 % 2, p % 2
            sz, sxl = s // 2, s % 2
            tp = (py + y) % 4 * 4 + (pxh ^ xh) * 2 + (pc ^ c)
            ts = (sz + z) % 8 * 2 + (sxl ^ xl)
            pairs.append((p * 16 + s, tp * 16 + ts))
    return lax.ppermute(x, AXES, pairs)


def swap_z(x):
    return lax.all_to_all(x, "shard", 0, 0, tiled=True, axis_index_groups=Z_GROUPS)


def dot(a, b):
    return jnp.dot(a, b, preferred_element_type=F4)


def contract_rows(a, b):
    return lax.dot_general(a, b, (((0,), (0,)), ((), ())), preferred_element_type=F4)


def gather(sent, w, x):
    sent, other = lax.optimization_barrier((sent, shift(w, xl=1)))
    own = lax.all_to_all(sent, "mp", 0, 0, tiled=True, axis_index_groups=CORE_GROUPS)
    z = [x]
    u = d = x
    for _ in range(3):
        u, d = shift(u, z=1), shift(d, z=-1)
        z += [u, d]
    z += [shift(u[:128], z=1), shift(d[128:], z=-1)]
    both = jnp.concatenate([w, other], 0)
    own, both, *z = lax.optimization_barrier((own.reshape(8, 8, 16, 1152), both, *z))
    return own, shift(own, c=1), both, z


def prepare_kernel(info, bank, ids, piece_out, cols_out, total, pick):
    zz = pl.program_id(0)
    p, s, xl = info[0], info[1], info[2]

    @pl.when(zz == 0)
    def _():
        i0 = lax.broadcasted_iota(jnp.int32, (64, 64), 0)
        i1 = lax.broadcasted_iota(jnp.int32, (64, 64), 1)
        row_ids = (ids[...] - s * 256).astype(F4)
        row_ids = jnp.sum(jnp.where(i0 == i1, row_ids, 0.0), axis=1, keepdims=True)
        lane = lax.broadcasted_iota(jnp.int32, (64, 256), 1).astype(F4)
        pick[...] = jnp.where(row_ids == lane, 1.0, 0.0).astype(BF)
        total[...] = jnp.zeros_like(total)

    own_row = pl.multiple_of(p * 16, 16)
    for half in range(2):
        got = dot(pick[...], bank[:, half * 1024 : half * 1024 + 1024])
        got = got * got
        total[...] += sum(got[:, i * 128 : i * 128 + 128] for i in range(8))
        for j in range(2):
            at = pl.multiple_of(half * 1024 + (xl ^ j) * 512, 512)
            piece_out[zz * 2 + half, :, j * 512 : j * 512 + 512] = bank[pl.ds(own_row, 16), pl.ds(at, 512)]

    @pl.when(zz == p // 4)
    def _():
        cols_out[...] = bank[:, pl.ds(pl.multiple_of(p % 4 * 512, 512), 512)]

    @pl.when(zz == 3)
    def _():
        scale = lax.rsqrt(jnp.sum(total[...], axis=1, keepdims=True) / 8192 + EPSILON)
        i0 = lax.broadcasted_iota(jnp.int32, (64, 64), 0)
        i1 = lax.broadcasted_iota(jnp.int32, (64, 64), 1)
        scale = jnp.sum(jnp.where(i0 == i1, scale, 0.0), axis=0, keepdims=True)
        hi = scale.astype(BF).astype(F4)
        mid = (scale - hi).astype(BF).astype(F4)
        low = scale - hi - mid
        first = jnp.concatenate([(ids[...] - s * 256).astype(F4), hi], 1)
        second = jnp.concatenate([mid, low], 1)
        row = lax.broadcasted_iota(jnp.int32, (16, 128), 0)
        extra = jnp.where(row == 0, first, jnp.where(row == 1, second, 0.0)).astype(BF)
        for to in range(8):
            piece_out[to, :, 1024:1152] = extra


def prepare(info, bank, ids):
    whole = lambda shape: pl.BlockSpec(shape, lambda i, info: (0,) * len(shape))
    return pl.pallas_call(
        prepare_kernel,
        grid_spec=pltpu.PrefetchScalarGridSpec(
            num_scalar_prefetch=1,
            grid=(4,),
            in_specs=[pl.BlockSpec((256, 2048), lambda i, info: (0, i)), whole((1, 64))],
            out_specs=[whole((8, 16, 1152)), whole((256, 512))],
            scratch_shapes=[pltpu.VMEM((64, 128), F4), pltpu.VMEM((64, 256), BF)],
        ),
        out_shape=[jax.ShapeDtypeStruct((8, 16, 1152), BF), jax.ShapeDtypeStruct((256, 512), BF)],
        compiler_params=pltpu.CompilerParams(dimension_semantics=("arbitrary",), vmem_limit_bytes=VMEM),
        cost_estimate=pl.CostEstimate(flops=2**28, bytes_accessed=5 * 2**20, transcendentals=64),
        name="prepare",
    )(info, bank, ids)


def address_kernel(info, piece, gains, out):
    z, xl = info[6], info[2]
    for q in range(8):
        out[q * 8 : q * 8 + 8] = piece[...]
        for i, b in enumerate((2 * q, 2 * q + 1, z * 2 + xl, z * 2 + (1 - xl))):
            at = b * 512 if i < 2 else pl.multiple_of(b * 512, 512)
            g = gains[:, pl.ds(at, 512)]
            g = jnp.concatenate([g[:, j * 128 : j * 128 + 128] for j in range(4)], 0)
            hi = g.astype(BF).astype(F4)
            top = piece[i, :, 1024:1152].astype(F4)[0:8]
            out[q * 8 + i, :, 1024:1152] = jnp.concatenate([top, hi, g - hi], 0).astype(BF)


def address(info, piece, gains):
    return pl.pallas_call(
        address_kernel,
        in_specs=[pl.BlockSpec(memory_space=pltpu.SMEM)] + [pl.BlockSpec(memory_space=pltpu.VMEM)] * 2,
        out_specs=pl.BlockSpec(memory_space=pltpu.VMEM),
        out_shape=jax.ShapeDtypeStruct((64, 16, 1152), BF),
        compiler_params=pltpu.CompilerParams(vmem_limit_bytes=VMEM),
        cost_estimate=pl.CostEstimate(flops=2**20, bytes_accessed=3 * 2**20, transcendentals=0),
        name="address",
    )(info, piece, gains)


def token_columns(tiles):
    stacked = jnp.concatenate([t.astype(F4)[0:8] for t in tiles], 0).T
    out = []
    for m in range(16):
        first, second = stacked[:, m * 8 : m * 8 + 1], stacked[:, m * 8 + 1 : m * 8 + 2]
        out.append((first[0:64], first[64:128] + second[0:64] + second[64:128]))
    return out


def project_kernel(info, own_s, other_s, gains, weights, part_out, calib_out, diag_out, table, calib):
    zz = pl.program_id(0)
    xl, z = info[2], info[6]
    lane = lax.broadcasted_iota(jnp.int32, (64, 256), 1).astype(F4)
    for i in range(2):
        for core in range(2):
            src = own_s if core == 0 else other_s
            for slot in range(8):
                m = slot_model(info, core, slot)
                table[i, pl.ds(pl.multiple_of(m * 16, 16), 16), :] = src[slot, i, :, 0:1024]
        extra = own_s[info[3] * 2 + info[4], i, :, 1024:1152]
        column, scale = token_columns([extra] * 16)[0]
        pick = jnp.where(column == lane, 1.0, 0.0).astype(BF)
        rows = pl.ds(pl.multiple_of(zz * 128 + i * 64, 64), 64)
        for j in range(2):
            cols = slice(j * 512, j * 512 + 512)
            g = gains[:, pl.ds(pl.multiple_of((z * 2 + (xl ^ j)) * 512, 512), 512)]
            calib[rows, cols] = (dot(pick, table[i, :, cols]) * scale * g).astype(BF)

    @pl.when(zz == 3)
    def _():
        calib_out[...] = calib[...]
        part = dot(calib[...], weights[...]).astype(BF)
        for to in range(8):
            part_out[to] = part[to * 64 : to * 64 + 64]
        whole = calib[...].astype(F4)
        diag_out[...] = jnp.sum(whole * whole, axis=0, keepdims=True)


def project(info, own_s, other_s, gains, weights):
    whole = lambda shape: pl.BlockSpec(shape, lambda i, info: (0,) * len(shape))
    by_z = pl.BlockSpec((8, 2, 16, 1152), lambda i, info: (0, i, 0, 0))
    return pl.pallas_call(
        project_kernel,
        grid_spec=pltpu.PrefetchScalarGridSpec(
            num_scalar_prefetch=1,
            grid=(4,),
            in_specs=[by_z, by_z, whole((1, 8192)), whole((1024, 512))],
            out_specs=[whole((8, 64, 512)), whole((512, 1024)), whole((1, 1024))],
            scratch_shapes=[pltpu.VMEM((2, 256, 1024), BF), pltpu.VMEM((512, 1024), BF)],
        ),
        out_shape=[
            jax.ShapeDtypeStruct((8, 64, 512), BF),
            jax.ShapeDtypeStruct((512, 1024), BF),
            jax.ShapeDtypeStruct((1, 1024), F4),
        ],
        compiler_params=pltpu.CompilerParams(dimension_semantics=("arbitrary",), vmem_limit_bytes=VMEM),
        cost_estimate=pl.CostEstimate(flops=2**30, bytes_accessed=8 * 2**20, transcendentals=0),
        name="project",
    )(info, own_s, other_s, gains, weights)


def numer_kernel(info, calib, model_out, diag, weights, out):
    xl = info[2]
    ratio = lax.broadcasted_iota(jnp.int32, (512, 512), 0) == lax.broadcasted_iota(jnp.int32, (512, 512), 1)
    for j in range(2):
        cols = slice(j * 512, j * 512 + 512)
        d = diag[:, cols] * ((1.0 - ALPHA) / 1024)
        d = jnp.sum(jnp.where(ratio, d, 0.0), axis=1, keepdims=True)
        got = contract_rows(calib[:, cols], model_out[...]) * (ALPHA / 1024)
        got = got + d * weights[cols, :].astype(F4)
        got = got.astype(BF)
        for q in range(16):
            out[q * 2 + (xl ^ j)] = got[q * 32 : q * 32 + 32]


def numer_call(info, calib, model_out, diag, weights):
    return pl.pallas_call(
        numer_kernel,
        in_specs=[pl.BlockSpec(memory_space=pltpu.SMEM)] + [pl.BlockSpec(memory_space=pltpu.VMEM)] * 4,
        out_specs=pl.BlockSpec(memory_space=pltpu.VMEM),
        out_shape=jax.ShapeDtypeStruct((32, 32, 512), BF),
        compiler_params=pltpu.CompilerParams(vmem_limit_bytes=VMEM),
        cost_estimate=pl.CostEstimate(flops=2**29, bytes_accessed=4 * 2**20, transcendentals=0),
        name="numer",
    )(info, calib, model_out, diag, weights)


ORDER = (0, 7, 1, 6, 2, 5, 3, 4)
STEPS = (3, 3, 2)


def slot_model(info, core, slot):
    return slot * 2 + (info[5] ^ core)


def gram_kernel(first, last, info, *refs):
    refs = list(refs)
    blocks = [refs.pop(0) for _ in range(3)]
    own_s, other_s = refs.pop(0), refs.pop(0)
    if first:
        own_g, other_g = refs.pop(0), refs.pop(0)
    else:
        gains, before = refs.pop(0), refs.pop(0)
    if last:
        near, far = refs.pop(0), refs.pop(0)
    else:
        acc = refs.pop(0)
    if first:
        gains = refs.pop(0)
    if last:
        acc = refs.pop(0)
    table, pick, scale, calib = refs
    step = pl.program_id(0)

    @pl.when(step == 0)
    def _():
        if not first:
            acc[...] = before[...]
        else:
            acc[...] = jnp.zeros_like(acc)
            for core in range(2):
                src = own_g if core == 0 else other_g
                for slot in range(8):
                    m = slot_model(info, core, slot)
                    row = []
                    for b in (info[5], 2, 3):
                        tile = src[slot, b].astype(F4)
                        tile = tile[8:12] + tile[12:16]
                        row += [tile[i : i + 1] for i in range(4)]
                    gains[pl.ds(m, 1), :] = jnp.concatenate(row, 1)

    for i in range(2 if last else 3):

        @pl.when(step == i)
        def _(i=i):
            if last and i == 1:
                table[0:128, 0:512] = blocks[1][...]
                table[128:256, 0:512] = blocks[2][...]
            else:
                table[:, 0:512] = blocks[i][...]

    lane = lax.broadcasted_iota(jnp.int32, (64, 256), 1).astype(F4)
    models, tiles = [], []
    for core in range(2):
        src = own_s if core == 0 else other_s
        for slot in range(8):
            m = slot_model(info, core, slot)
            models.append(m)
            table[pl.ds(pl.multiple_of(m * 16, 16), 16), 512:1536] = src[slot, 0, :, 0:1024]
            tiles.append(src[slot, 0, :, 1024:1152])
    for m, (column, value) in enumerate(token_columns(tiles)):
        part = slice(m * 64, m * 64 + 64)
        pick[part, :] = jnp.where(column == lane, 1.0, 0.0).astype(BF)
        scale[part, :] = jnp.broadcast_to(value, (64, 128))

    for n in range(6):
        cols = slice(n * 256, n * 256 + 256)
        got = dot(pick[...], table[:, cols])
        for m in range(16):
            part = slice(m * 64, m * 64 + 64)
            r = scale[part, :]
            r = jnp.concatenate([r, r], 1)
            g = gains[pl.ds(models[m], 1), cols]
            calib[part, cols] = (got[part] * r * g).astype(BF)
    acc[...] += contract_rows(calib[:, 0:512], calib[:, 512:1536])

    if last:

        @pl.when(step == STEPS[-1] - 1)
        def _():
            near[...] = acc[:, 0:512]
            far[...] = acc[:, 512:1024].astype(BF)


def gram_call(i, info, blocks, own_s, other_s, gains, before):
    first, last = i == 0, i == len(STEPS) - 1
    start, steps = sum(STEPS[:i]), STEPS[i]
    whole = lambda shape: pl.BlockSpec(shape, lambda j, info: (0,) * len(shape))
    by_z = pl.BlockSpec((8, 1, 16, 1152), lambda j, info: (0, info[7 + start + j], 0, 0))
    gain_view = pl.BlockSpec((8, 8, 16, 128), lambda j, info: (0, 0, 0, 8))
    shapes = [jax.ShapeDtypeStruct((512, 1024), F4)]
    if last:
        shapes = [jax.ShapeDtypeStruct((512, 512), F4), jax.ShapeDtypeStruct((512, 512), BF)]
    if first:
        shapes.append(jax.ShapeDtypeStruct((16, 1536), F4))
    extra = [own_s, other_s] if first else [gains, before]
    extra_specs = [gain_view, gain_view] if first else [whole((16, 1536)), whole((512, 1024))]
    blocks = blocks[start : start + 3]
    operands = [info, *blocks, own_s, other_s, *extra]
    return pl.pallas_call(
        lambda *refs: gram_kernel(first, last, *refs),
        grid_spec=pltpu.PrefetchScalarGridSpec(
            num_scalar_prefetch=1,
            grid=(steps,),
            in_specs=[whole(b.shape) for b in blocks] + [by_z, by_z] + extra_specs,
            out_specs=[whole(o.shape) for o in shapes],
            scratch_shapes=([pltpu.VMEM((512, 1024), F4)] if last else [])
            + [
                pltpu.VMEM((256, 1536), BF),
                pltpu.VMEM((1024, 256), BF),
                pltpu.VMEM((1024, 128), F4),
                pltpu.VMEM((1024, 1536), BF),
            ],
        ),
        out_shape=shapes,
        input_output_aliases={} if first or last else {len(operands) - 1: 0},
        compiler_params=pltpu.CompilerParams(dimension_semantics=("arbitrary",), vmem_limit_bytes=VMEM),
        cost_estimate=pl.CostEstimate(flops=steps * 2**31, bytes_accessed=6 * 2**20, transcendentals=0),
        name="gram" + str(i),
    )(*operands)


def local(bank, calib_ids, norm_gains, proj_slabs):
    p = lax.axis_index("mp")
    s = lax.axis_index("shard")
    y, xh, c = p // 4, p // 2 % 2, p % 2
    z, xl = s // 2, s % 2
    info = jnp.stack([p, s, xl, y, xh, c, z] + [(z + k) % 8 for k in ORDER]).astype(jnp.int32)
    weights = proj_slabs[0]

    piece, bank_cols = prepare(info, bank, calib_ids)
    sent = address(info, swap_z(piece), norm_gains)
    own_s, other_s, both, blocks = gather(sent, weights, bank_cols)

    partial_out, calib, diag = project(info, own_s, other_s, norm_gains, both)
    tie = lax.optimization_barrier
    partial_out, info = tie((partial_out, info))
    acc, gains = gram_call(0, info, blocks, own_s, other_s, None, None)
    partial_out, gains = tie((swap_z(partial_out), gains))
    model_out = jnp.sum(partial_out.astype(F4), 0).astype(BF)
    model_out, info = tie((jnp.broadcast_to(model_out[None], (8, 64, 512)), info))
    (acc,) = gram_call(1, info, blocks, own_s, other_s, gains, acc)
    model_out, acc = tie((swap_z(model_out), acc))

    numer = numer_call(info, calib, model_out.reshape(512, 512), diag, both)
    numer, info = tie((numer, info))
    near, far = gram_call(2, info, blocks, own_s, other_s, gains, acc)
    numer, near = tie((lax.all_to_all(numer, AXES, 0, 0, tiled=True, axis_index_groups=XLO_GROUPS), near))
    numer = jnp.sum(numer.astype(F4), 0).astype(BF)
    numer = lax.all_to_all(jnp.broadcast_to(numer[None], (16, 32, 512)), "mp", 0, 0, tiled=True)
    numer = numer.reshape(512, 512).astype(F4)

    gram = near + shift(far, xl=1).astype(F4)
    on_diag = (p == s) & (
        lax.broadcasted_iota(jnp.int32, (512, 512), 0) == lax.broadcasted_iota(jnp.int32, (512, 512), 1)
    )
    merged_gram = gram * jnp.where(on_diag, 1.0 / 1024, ALPHA / 1024)

    return (merged_gram, numer)


def solution(mesh):
    placed = (P("shard", None), P("mp", "shard"), P("mp", None), P("mp", "shard", None))
    return jax.shard_map(
        local,
        mesh=mesh,
        in_specs=placed,
        out_specs=(P("mp", "shard"), P("shard", None)),
        check_vma=False,
    )
```

```python
import jax
import jax.numpy as jnp
from jax import lax
from jax.experimental import pallas as pl
from jax.experimental.pallas import tpu as pltpu
from jax.sharding import PartitionSpec as P

ALPHA = 0.9
EPSILON = 1e-05
BF = jnp.bfloat16
F4 = jnp.float32
VMEM = 60 * 2**20
AXES = ("mp", "shard")
Z_GROUPS = [[z * 2 + xl for z in range(8)] for xl in range(2)]
CORE_GROUPS = [[q * 2 + c for q in range(8)] for c in range(2)]
XLO_GROUPS = [[p * 16 + z * 2 + xl for p in range(16) for xl in range(2)] for z in range(8)]


def shift(x, y=0, xh=0, c=0, z=0, xl=0):
    pairs = []
    for p in range(16):
        for s in range(16):
            py, pxh, pc = p // 4, p // 2 % 2, p % 2
            sz, sxl = s // 2, s % 2
            tp = (py + y) % 4 * 4 + (pxh ^ xh) * 2 + (pc ^ c)
            ts = (sz + z) % 8 * 2 + (sxl ^ xl)
            pairs.append((p * 16 + s, tp * 16 + ts))
    return lax.ppermute(x, AXES, pairs)


def swap_z(x):
    return lax.all_to_all(x, "shard", 0, 0, tiled=True, axis_index_groups=Z_GROUPS)


def dot(a, b):
    return jnp.dot(a, b, preferred_element_type=F4)


def contract_rows(a, b):
    return lax.dot_general(a, b, (((0,), (0,)), ((), ())), preferred_element_type=F4)


def gather(sent, w, x):
    u, d = shift(x, z=1), shift(x, z=-1)
    sent, other, u, d = lax.optimization_barrier((sent, shift(w, xl=1), u, d))
    own = lax.all_to_all(sent, "mp", 0, 0, tiled=True, axis_index_groups=CORE_GROUPS)
    z = [x, u, d]
    for _ in range(2):
        u, d = shift(u, z=1), shift(d, z=-1)
        z += [u, d]
    z += [shift(u[:128], z=1), shift(d[128:], z=-1)]
    both = jnp.concatenate([w, other], 0)
    own, both, *z = lax.optimization_barrier((own.reshape(8, 8, 16, 1152), both, *z))
    return own, shift(own, c=1), both, z


def prepare_kernel(info, bank, ids, piece_out, cols_out, total, pick):
    zz = pl.program_id(0)
    p, s, xl = info[0], info[1], info[2]

    @pl.when(zz == 0)
    def _():
        i0 = lax.broadcasted_iota(jnp.int32, (64, 64), 0)
        i1 = lax.broadcasted_iota(jnp.int32, (64, 64), 1)
        row_ids = (ids[...] - s * 256).astype(F4)
        row_ids = jnp.sum(jnp.where(i0 == i1, row_ids, 0.0), axis=1, keepdims=True)
        lane = lax.broadcasted_iota(jnp.int32, (64, 256), 1).astype(F4)
        pick[...] = jnp.where(row_ids == lane, 1.0, 0.0).astype(BF)
        total[...] = jnp.zeros_like(total)

    own_row = pl.multiple_of(p * 16, 16)
    for half in range(2):
        got = dot(pick[...], bank[:, half * 1024 : half * 1024 + 1024])
        got = got * got
        total[...] += sum(got[:, i * 128 : i * 128 + 128] for i in range(8))
        for j in range(2):
            at = pl.multiple_of(half * 1024 + (xl ^ j) * 512, 512)
            piece_out[zz * 2 + half, :, j * 512 : j * 512 + 512] = bank[pl.ds(own_row, 16), pl.ds(at, 512)]

    @pl.when(zz == p // 4)
    def _():
        cols_out[...] = bank[:, pl.ds(pl.multiple_of(p % 4 * 512, 512), 512)]

    @pl.when(zz == 3)
    def _():
        scale = lax.rsqrt(jnp.sum(total[...], axis=1, keepdims=True) / 8192 + EPSILON)
        i0 = lax.broadcasted_iota(jnp.int32, (64, 64), 0)
        i1 = lax.broadcasted_iota(jnp.int32, (64, 64), 1)
        scale = jnp.sum(jnp.where(i0 == i1, scale, 0.0), axis=0, keepdims=True)
        hi = scale.astype(BF).astype(F4)
        mid = (scale - hi).astype(BF).astype(F4)
        low = scale - hi - mid
        first = jnp.concatenate([(ids[...] - s * 256).astype(F4), hi], 1)
        second = jnp.concatenate([mid, low], 1)
        row = lax.broadcasted_iota(jnp.int32, (16, 128), 0)
        extra = jnp.where(row == 0, first, jnp.where(row == 1, second, 0.0)).astype(BF)
        for to in range(8):
            piece_out[to, :, 1024:1152] = extra


def prepare(info, bank, ids):
    whole = lambda shape: pl.BlockSpec(shape, lambda i, info: (0,) * len(shape))
    return pl.pallas_call(
        prepare_kernel,
        grid_spec=pltpu.PrefetchScalarGridSpec(
            num_scalar_prefetch=1,
            grid=(4,),
            in_specs=[pl.BlockSpec((256, 2048), lambda i, info: (0, i)), whole((1, 64))],
            out_specs=[whole((8, 16, 1152)), whole((256, 512))],
            scratch_shapes=[pltpu.VMEM((64, 128), F4), pltpu.VMEM((64, 256), BF)],
        ),
        out_shape=[jax.ShapeDtypeStruct((8, 16, 1152), BF), jax.ShapeDtypeStruct((256, 512), BF)],
        compiler_params=pltpu.CompilerParams(dimension_semantics=("arbitrary",), vmem_limit_bytes=VMEM),
        cost_estimate=pl.CostEstimate(flops=2**28, bytes_accessed=5 * 2**20, transcendentals=64),
        name="prepare",
    )(info, bank, ids)


def address_kernel(info, piece, gains, out):
    z, xl = info[6], info[2]
    for q in range(8):
        out[q * 8 : q * 8 + 8] = piece[...]
        for i, b in enumerate((2 * q, 2 * q + 1, z * 2 + xl, z * 2 + (1 - xl))):
            at = b * 512 if i < 2 else pl.multiple_of(b * 512, 512)
            g = gains[:, pl.ds(at, 512)]
            g = jnp.concatenate([g[:, j * 128 : j * 128 + 128] for j in range(4)], 0)
            hi = g.astype(BF).astype(F4)
            top = piece[i, :, 1024:1152].astype(F4)[0:8]
            out[q * 8 + i, :, 1024:1152] = jnp.concatenate([top, hi, g - hi], 0).astype(BF)


def address(info, piece, gains):
    return pl.pallas_call(
        address_kernel,
        in_specs=[pl.BlockSpec(memory_space=pltpu.SMEM)] + [pl.BlockSpec(memory_space=pltpu.VMEM)] * 2,
        out_specs=pl.BlockSpec(memory_space=pltpu.VMEM),
        out_shape=jax.ShapeDtypeStruct((64, 16, 1152), BF),
        compiler_params=pltpu.CompilerParams(vmem_limit_bytes=VMEM),
        cost_estimate=pl.CostEstimate(flops=2**20, bytes_accessed=3 * 2**20, transcendentals=0),
        name="address",
    )(info, piece, gains)


def token_columns(tiles):
    stacked = jnp.concatenate([t.astype(F4)[0:8] for t in tiles], 0).T
    out = []
    for m in range(16):
        first, second = stacked[:, m * 8 : m * 8 + 1], stacked[:, m * 8 + 1 : m * 8 + 2]
        out.append((first[0:64], first[64:128] + second[0:64] + second[64:128]))
    return out


def project_kernel(info, own_s, other_s, gains, weights, part_out, calib_out, diag_out, table, calib):
    zz = pl.program_id(0)
    xl, z = info[2], info[6]
    lane = lax.broadcasted_iota(jnp.int32, (64, 256), 1).astype(F4)
    for i in range(2):
        for core in range(2):
            src = own_s if core == 0 else other_s
            for slot in range(8):
                m = slot_model(info, core, slot)
                table[i, pl.ds(pl.multiple_of(m * 16, 16), 16), :] = src[slot, i, :, 0:1024]
        extra = own_s[info[3] * 2 + info[4], i, :, 1024:1152]
        column, scale = token_columns([extra] * 16)[0]
        pick = jnp.where(column == lane, 1.0, 0.0).astype(BF)
        rows = pl.ds(pl.multiple_of(zz * 128 + i * 64, 64), 64)
        for j in range(2):
            cols = slice(j * 512, j * 512 + 512)
            g = gains[:, pl.ds(pl.multiple_of((z * 2 + (xl ^ j)) * 512, 512), 512)]
            calib[rows, cols] = (dot(pick, table[i, :, cols]) * scale * g).astype(BF)

    @pl.when(zz == 3)
    def _():
        calib_out[...] = calib[...]
        part = dot(calib[...], weights[...]).astype(BF)
        for to in range(8):
            part_out[to] = part[to * 64 : to * 64 + 64]
        whole = calib[...].astype(F4)
        diag_out[...] = jnp.sum(whole * whole, axis=0, keepdims=True)


def project(info, own_s, other_s, gains, weights):
    whole = lambda shape: pl.BlockSpec(shape, lambda i, info: (0,) * len(shape))
    by_z = pl.BlockSpec((8, 2, 16, 1152), lambda i, info: (0, i, 0, 0))
    return pl.pallas_call(
        project_kernel,
        grid_spec=pltpu.PrefetchScalarGridSpec(
            num_scalar_prefetch=1,
            grid=(4,),
            in_specs=[by_z, by_z, whole((1, 8192)), whole((1024, 512))],
            out_specs=[whole((8, 64, 512)), whole((512, 1024)), whole((1, 1024))],
            scratch_shapes=[pltpu.VMEM((2, 256, 1024), BF), pltpu.VMEM((512, 1024), BF)],
        ),
        out_shape=[
            jax.ShapeDtypeStruct((8, 64, 512), BF),
            jax.ShapeDtypeStruct((512, 1024), BF),
            jax.ShapeDtypeStruct((1, 1024), F4),
        ],
        compiler_params=pltpu.CompilerParams(dimension_semantics=("arbitrary",), vmem_limit_bytes=VMEM),
        cost_estimate=pl.CostEstimate(flops=2**30, bytes_accessed=8 * 2**20, transcendentals=0),
        name="project",
    )(info, own_s, other_s, gains, weights)


def numer_kernel(info, calib, model_out, diag, weights, out):
    xl = info[2]
    ratio = lax.broadcasted_iota(jnp.int32, (512, 512), 0) == lax.broadcasted_iota(jnp.int32, (512, 512), 1)
    for j in range(2):
        cols = slice(j * 512, j * 512 + 512)
        d = diag[:, cols] * ((1.0 - ALPHA) / 1024)
        d = jnp.sum(jnp.where(ratio, d, 0.0), axis=1, keepdims=True)
        got = contract_rows(calib[:, cols], model_out[...]) * (ALPHA / 1024)
        got = got + d * weights[cols, :].astype(F4)
        got = got.astype(BF)
        for q in range(16):
            out[q * 2 + (xl ^ j)] = got[q * 32 : q * 32 + 32]


def numer_call(info, calib, model_out, diag, weights):
    return pl.pallas_call(
        numer_kernel,
        in_specs=[pl.BlockSpec(memory_space=pltpu.SMEM)] + [pl.BlockSpec(memory_space=pltpu.VMEM)] * 4,
        out_specs=pl.BlockSpec(memory_space=pltpu.VMEM),
        out_shape=jax.ShapeDtypeStruct((32, 32, 512), BF),
        compiler_params=pltpu.CompilerParams(vmem_limit_bytes=VMEM),
        cost_estimate=pl.CostEstimate(flops=2**29, bytes_accessed=4 * 2**20, transcendentals=0),
        name="numer",
    )(info, calib, model_out, diag, weights)


ORDER = (0, 7, 1, 6, 2, 5, 3, 4)
STEPS = (3, 3, 2)


def slot_model(info, core, slot):
    return slot * 2 + (info[5] ^ core)


def gram_kernel(first, last, info, *refs):
    refs = list(refs)
    blocks = [refs.pop(0) for _ in range(3)]
    own_s, other_s = refs.pop(0), refs.pop(0)
    if first:
        own_g, other_g = refs.pop(0), refs.pop(0)
    else:
        gains, before = refs.pop(0), refs.pop(0)
    if last:
        near, far = refs.pop(0), refs.pop(0)
    else:
        acc = refs.pop(0)
    if first:
        gains = refs.pop(0)
    if last:
        acc = refs.pop(0)
    table, pick, scale, calib = refs
    step = pl.program_id(0)

    @pl.when(step == 0)
    def _():
        if not first:
            acc[...] = before[...]
        else:
            acc[...] = jnp.zeros_like(acc)
            for core in range(2):
                src = own_g if core == 0 else other_g
                for slot in range(8):
                    m = slot_model(info, core, slot)
                    row = []
                    for b in (info[5], 2, 3):
                        tile = src[slot, b].astype(F4)
                        tile = tile[8:12] + tile[12:16]
                        row += [tile[i : i + 1] for i in range(4)]
                    gains[pl.ds(m, 1), :] = jnp.concatenate(row, 1)

    for i in range(2 if last else 3):

        @pl.when(step == i)
        def _(i=i):
            if last and i == 1:
                table[0:128, 0:512] = blocks[1][...]
                table[128:256, 0:512] = blocks[2][...]
            else:
                table[:, 0:512] = blocks[i][...]

    lane = lax.broadcasted_iota(jnp.int32, (64, 256), 1).astype(F4)
    models, tiles = [], []
    for core in range(2):
        src = own_s if core == 0 else other_s
        for slot in range(8):
            m = slot_model(info, core, slot)
            models.append(m)
            table[pl.ds(pl.multiple_of(m * 16, 16), 16), 512:1536] = src[slot, 0, :, 0:1024]
            tiles.append(src[slot, 0, :, 1024:1152])
    for m, (column, value) in enumerate(token_columns(tiles)):
        part = slice(m * 64, m * 64 + 64)
        pick[part, :] = jnp.where(column == lane, 1.0, 0.0).astype(BF)
        scale[part, :] = jnp.broadcast_to(value, (64, 128))

    for n in range(6):
        cols = slice(n * 256, n * 256 + 256)
        got = dot(pick[...], table[:, cols])
        for m in range(16):
            part = slice(m * 64, m * 64 + 64)
            r = scale[part, :]
            r = jnp.concatenate([r, r], 1)
            g = gains[pl.ds(models[m], 1), cols]
            calib[part, cols] = (got[part] * r * g).astype(BF)
    acc[...] += contract_rows(calib[:, 0:512], calib[:, 512:1536])

    if last:

        @pl.when(step == STEPS[-1] - 1)
        def _():
            near[...] = acc[:, 0:512]
            far[...] = acc[:, 512:1024].astype(BF)


def gram_call(i, info, blocks, own_s, other_s, gains, before):
    first, last = i == 0, i == len(STEPS) - 1
    start, steps = sum(STEPS[:i]), STEPS[i]
    whole = lambda shape: pl.BlockSpec(shape, lambda j, info: (0,) * len(shape))
    by_z = pl.BlockSpec((8, 1, 16, 1152), lambda j, info: (0, info[7 + start + j], 0, 0))
    gain_view = pl.BlockSpec((8, 8, 16, 128), lambda j, info: (0, 0, 0, 8))
    shapes = [jax.ShapeDtypeStruct((512, 1024), F4)]
    if last:
        shapes = [jax.ShapeDtypeStruct((512, 512), F4), jax.ShapeDtypeStruct((512, 512), BF)]
    if first:
        shapes.append(jax.ShapeDtypeStruct((16, 1536), F4))
    extra = [own_s, other_s] if first else [gains, before]
    extra_specs = [gain_view, gain_view] if first else [whole((16, 1536)), whole((512, 1024))]
    blocks = blocks[start : start + 3]
    operands = [info, *blocks, own_s, other_s, *extra]
    return pl.pallas_call(
        lambda *refs: gram_kernel(first, last, *refs),
        grid_spec=pltpu.PrefetchScalarGridSpec(
            num_scalar_prefetch=1,
            grid=(steps,),
            in_specs=[whole(b.shape) for b in blocks] + [by_z, by_z] + extra_specs,
            out_specs=[whole(o.shape) for o in shapes],
            scratch_shapes=([pltpu.VMEM((512, 1024), F4)] if last else [])
            + [
                pltpu.VMEM((256, 1536), BF),
                pltpu.VMEM((1024, 256), BF),
                pltpu.VMEM((1024, 128), F4),
                pltpu.VMEM((1024, 1536), BF),
            ],
        ),
        out_shape=shapes,
        input_output_aliases={} if first or last else {len(operands) - 1: 0},
        compiler_params=pltpu.CompilerParams(dimension_semantics=("arbitrary",), vmem_limit_bytes=VMEM),
        cost_estimate=pl.CostEstimate(flops=steps * 2**31, bytes_accessed=6 * 2**20, transcendentals=0),
        name="gram" + str(i),
    )(*operands)


def local(bank, calib_ids, norm_gains, proj_slabs):
    p = lax.axis_index("mp")
    s = lax.axis_index("shard")
    y, xh, c = p // 4, p // 2 % 2, p % 2
    z, xl = s // 2, s % 2
    info = jnp.stack([p, s, xl, y, xh, c, z] + [(z + k) % 8 for k in ORDER]).astype(jnp.int32)
    weights = proj_slabs[0]

    piece, bank_cols = prepare(info, bank, calib_ids)
    sent = address(info, swap_z(piece), norm_gains)
    own_s, other_s, both, blocks = gather(sent, weights, bank_cols)

    partial_out, calib, diag = project(info, own_s, other_s, norm_gains, both)
    tie = lax.optimization_barrier
    partial_out, info = tie((partial_out, info))
    acc, gains = gram_call(0, info, blocks, own_s, other_s, None, None)
    partial_out, gains = tie((swap_z(partial_out), gains))
    model_out = jnp.sum(partial_out.astype(F4), 0).astype(BF)
    model_out, info = tie((jnp.broadcast_to(model_out[None], (8, 64, 512)), info))
    (acc,) = gram_call(1, info, blocks, own_s, other_s, gains, acc)
    model_out, acc = tie((swap_z(model_out), acc))

    numer = numer_call(info, calib, model_out.reshape(512, 512), diag, both)
    numer, info = tie((numer, info))
    near, far = gram_call(2, info, blocks, own_s, other_s, gains, acc)
    numer, near = tie((lax.all_to_all(numer, AXES, 0, 0, tiled=True, axis_index_groups=XLO_GROUPS), near))
    numer = jnp.sum(numer.astype(F4), 0).astype(BF)
    numer = lax.all_to_all(jnp.broadcast_to(numer[None], (16, 32, 512)), "mp", 0, 0, tiled=True)
    numer = numer.reshape(512, 512).astype(F4)

    gram = near + shift(far, xl=1).astype(F4)
    on_diag = (p == s) & (
        lax.broadcasted_iota(jnp.int32, (512, 512), 0) == lax.broadcasted_iota(jnp.int32, (512, 512), 1)
    )
    merged_gram = gram * jnp.where(on_diag, 1.0 / 1024, ALPHA / 1024)

    return (merged_gram, numer)


def solution(mesh):
    placed = (P("shard", None), P("mp", "shard"), P("mp", None), P("mp", "shard", None))
    return jax.shard_map(
        local,
        mesh=mesh,
        in_specs=placed,
        out_specs=(P("mp", "shard"), P("shard", None)),
        check_vma=False,
    )
```

```python
import jax
import jax.numpy as jnp
from jax import lax
from jax.experimental import pallas as pl
from jax.experimental.pallas import tpu as pltpu
from jax.sharding import PartitionSpec as P

ALPHA = 0.9
EPSILON = 1e-05
BF = jnp.bfloat16
F4 = jnp.float32
VMEM = 60 * 2**20
AXES = ("mp", "shard")
Z_GROUPS = [[z * 2 + xl for z in range(8)] for xl in range(2)]
CORE_GROUPS = [[q * 2 + c for q in range(8)] for c in range(2)]
XLO_GROUPS = [[p * 16 + z * 2 + xl for p in range(16) for xl in range(2)] for z in range(8)]


def shift(x, y=0, xh=0, c=0, z=0, xl=0):
    pairs = []
    for p in range(16):
        for s in range(16):
            py, pxh, pc = p // 4, p // 2 % 2, p % 2
            sz, sxl = s // 2, s % 2
            tp = (py + y) % 4 * 4 + (pxh ^ xh) * 2 + (pc ^ c)
            ts = (sz + z) % 8 * 2 + (sxl ^ xl)
            pairs.append((p * 16 + s, tp * 16 + ts))
    return lax.ppermute(x, AXES, pairs)


def swap_z(x):
    return lax.all_to_all(x, "shard", 0, 0, tiled=True, axis_index_groups=Z_GROUPS)


def dot(a, b):
    return jnp.dot(a, b, preferred_element_type=F4)


def contract_rows(a, b):
    return lax.dot_general(a, b, (((0,), (0,)), ((), ())), preferred_element_type=F4)


def gather(sent, w, x):
    u, d = shift(x, z=1), shift(x, z=-1)
    sent, other, u, d = lax.optimization_barrier((sent, shift(w, xl=1), u, d))
    own = lax.all_to_all(sent, "mp", 0, 0, tiled=True, axis_index_groups=CORE_GROUPS)
    z = [x, u, d]
    for _ in range(2):
        u, d = shift(u, z=1), shift(d, z=-1)
        z += [u, d]
    z += [shift(u[:128], z=1), shift(d[128:], z=-1)]
    both = jnp.concatenate([w, other], 0)
    own, both, *z = lax.optimization_barrier((own.reshape(8, 8, 16, 1152), both, *z))
    return own, shift(own, c=1), both, z


def prepare_kernel(info, bank, ids, piece_out, cols_out, total, pick):
    zz = pl.program_id(0)
    p, s, xl = info[0], info[1], info[2]

    @pl.when(zz == 0)
    def _():
        i0 = lax.broadcasted_iota(jnp.int32, (64, 64), 0)
        i1 = lax.broadcasted_iota(jnp.int32, (64, 64), 1)
        row_ids = (ids[...] - s * 256).astype(F4)
        row_ids = jnp.sum(jnp.where(i0 == i1, row_ids, 0.0), axis=1, keepdims=True)
        lane = lax.broadcasted_iota(jnp.int32, (64, 256), 1).astype(F4)
        pick[...] = jnp.where(row_ids == lane, 1.0, 0.0).astype(BF)
        total[...] = jnp.zeros_like(total)

    own_row = pl.multiple_of(p * 16, 16)
    for half in range(2):
        got = dot(pick[...], bank[:, half * 1024 : half * 1024 + 1024])
        got = got * got
        total[...] += sum(got[:, i * 128 : i * 128 + 128] for i in range(8))
        for j in range(2):
            at = pl.multiple_of(half * 1024 + (xl ^ j) * 512, 512)
            piece_out[zz * 2 + half, :, j * 512 : j * 512 + 512] = bank[pl.ds(own_row, 16), pl.ds(at, 512)]

    @pl.when(zz == p // 4)
    def _():
        cols_out[...] = bank[:, pl.ds(pl.multiple_of(p % 4 * 512, 512), 512)]

    @pl.when(zz == 3)
    def _():
        scale = lax.rsqrt(jnp.sum(total[...], axis=1, keepdims=True) / 8192 + EPSILON)
        i0 = lax.broadcasted_iota(jnp.int32, (64, 64), 0)
        i1 = lax.broadcasted_iota(jnp.int32, (64, 64), 1)
        scale = jnp.sum(jnp.where(i0 == i1, scale, 0.0), axis=0, keepdims=True)
        hi = scale.astype(BF).astype(F4)
        mid = (scale - hi).astype(BF).astype(F4)
        low = scale - hi - mid
        first = jnp.concatenate([(ids[...] - s * 256).astype(F4), hi], 1)
        second = jnp.concatenate([mid, low], 1)
        row = lax.broadcasted_iota(jnp.int32, (16, 128), 0)
        extra = jnp.where(row == 0, first, jnp.where(row == 1, second, 0.0)).astype(BF)
        for to in range(8):
            piece_out[to, :, 1024:1152] = extra


def prepare(info, bank, ids):
    whole = lambda shape: pl.BlockSpec(shape, lambda i, info: (0,) * len(shape))
    return pl.pallas_call(
        prepare_kernel,
        grid_spec=pltpu.PrefetchScalarGridSpec(
            num_scalar_prefetch=1,
            grid=(4,),
            in_specs=[pl.BlockSpec((256, 2048), lambda i, info: (0, i)), whole((1, 64))],
            out_specs=[whole((8, 16, 1152)), whole((256, 512))],
            scratch_shapes=[pltpu.VMEM((64, 128), F4), pltpu.VMEM((64, 256), BF)],
        ),
        out_shape=[jax.ShapeDtypeStruct((8, 16, 1152), BF), jax.ShapeDtypeStruct((256, 512), BF)],
        compiler_params=pltpu.CompilerParams(dimension_semantics=("arbitrary",), vmem_limit_bytes=VMEM),
        cost_estimate=pl.CostEstimate(flops=2**28, bytes_accessed=5 * 2**20, transcendentals=64),
        name="prepare",
    )(info, bank, ids)


def address_kernel(info, piece, gains, out):
    z, xl = info[6], info[2]
    for q in range(8):
        out[q * 8 : q * 8 + 8] = piece[...]
        for i, b in enumerate((2 * q, 2 * q + 1, z * 2 + xl, z * 2 + (1 - xl))):
            at = b * 512 if i < 2 else pl.multiple_of(b * 512, 512)
            g = gains[:, pl.ds(at, 512)]
            g = jnp.concatenate([g[:, j * 128 : j * 128 + 128] for j in range(4)], 0)
            hi = g.astype(BF).astype(F4)
            top = piece[i, :, 1024:1152].astype(F4)[0:8]
            out[q * 8 + i, :, 1024:1152] = jnp.concatenate([top, hi, g - hi], 0).astype(BF)


def address(info, piece, gains):
    return pl.pallas_call(
        address_kernel,
        in_specs=[pl.BlockSpec(memory_space=pltpu.SMEM)] + [pl.BlockSpec(memory_space=pltpu.VMEM)] * 2,
        out_specs=pl.BlockSpec(memory_space=pltpu.VMEM),
        out_shape=jax.ShapeDtypeStruct((64, 16, 1152), BF),
        compiler_params=pltpu.CompilerParams(vmem_limit_bytes=16 * 2**20),
        cost_estimate=pl.CostEstimate(flops=2**20, bytes_accessed=3 * 2**20, transcendentals=0),
        name="address",
    )(info, piece, gains)


def token_columns(tiles):
    stacked = jnp.concatenate([t.astype(F4)[0:8] for t in tiles], 0).T
    out = []
    for m in range(16):
        first, second = stacked[:, m * 8 : m * 8 + 1], stacked[:, m * 8 + 1 : m * 8 + 2]
        out.append((first[0:64], first[64:128] + second[0:64] + second[64:128]))
    return out


def project_kernel(info, own_s, other_s, gains, weights, part_out, calib_out, diag_out, table, calib):
    zz = pl.program_id(0)
    xl, z = info[2], info[6]
    lane = lax.broadcasted_iota(jnp.int32, (64, 256), 1).astype(F4)
    for i in range(2):
        for core in range(2):
            src = own_s if core == 0 else other_s
            for slot in range(8):
                m = slot_model(info, core, slot)
                table[i, pl.ds(pl.multiple_of(m * 16, 16), 16), :] = src[slot, i, :, 0:1024]
        extra = own_s[info[3] * 2 + info[4], i, :, 1024:1152]
        column, scale = token_columns([extra] * 16)[0]
        pick = jnp.where(column == lane, 1.0, 0.0).astype(BF)
        rows = pl.ds(pl.multiple_of(zz * 128 + i * 64, 64), 64)
        for j in range(2):
            cols = slice(j * 512, j * 512 + 512)
            g = gains[:, pl.ds(pl.multiple_of((z * 2 + (xl ^ j)) * 512, 512), 512)]
            calib[rows, cols] = (dot(pick, table[i, :, cols]) * scale * g).astype(BF)

    @pl.when(zz == 3)
    def _():
        calib_out[...] = calib[...]
        part = dot(calib[...], weights[...]).astype(BF)
        for to in range(8):
            part_out[to] = part[to * 64 : to * 64 + 64]
        whole = calib[...].astype(F4)
        diag_out[...] = jnp.sum(whole * whole, axis=0, keepdims=True)


def project(info, own_s, other_s, gains, weights):
    whole = lambda shape: pl.BlockSpec(shape, lambda i, info: (0,) * len(shape))
    by_z = pl.BlockSpec((8, 2, 16, 1152), lambda i, info: (0, i, 0, 0))
    return pl.pallas_call(
        project_kernel,
        grid_spec=pltpu.PrefetchScalarGridSpec(
            num_scalar_prefetch=1,
            grid=(4,),
            in_specs=[by_z, by_z, whole((1, 8192)), whole((1024, 512))],
            out_specs=[whole((8, 64, 512)), whole((512, 1024)), whole((1, 1024))],
            scratch_shapes=[pltpu.VMEM((2, 256, 1024), BF), pltpu.VMEM((512, 1024), BF)],
        ),
        out_shape=[
            jax.ShapeDtypeStruct((8, 64, 512), BF),
            jax.ShapeDtypeStruct((512, 1024), BF),
            jax.ShapeDtypeStruct((1, 1024), F4),
        ],
        compiler_params=pltpu.CompilerParams(dimension_semantics=("arbitrary",), vmem_limit_bytes=VMEM),
        cost_estimate=pl.CostEstimate(flops=2**30, bytes_accessed=8 * 2**20, transcendentals=0),
        name="project",
    )(info, own_s, other_s, gains, weights)


def numer_kernel(info, calib, model_out, diag, weights, out):
    i = pl.program_id(0)
    side = info[2] ^ (i // 2)
    on = lax.broadcasted_iota(jnp.int32, (256, 256), 0) == lax.broadcasted_iota(jnp.int32, (256, 256), 1)
    d = jnp.sum(jnp.where(on, diag[...] * ((1.0 - ALPHA) / 1024), 0.0), axis=1, keepdims=True)
    got = contract_rows(calib[...], model_out[...]) * (ALPHA / 1024) + d * weights[...].astype(F4)
    got = got.astype(BF)
    for q in range(8):
        out[(i % 2 * 8 + q) * 2 + side] = got[q * 32 : q * 32 + 32]


def numer_call(info, calib, model_out, diag, weights):
    return pl.pallas_call(
        numer_kernel,
        grid_spec=pltpu.PrefetchScalarGridSpec(
            num_scalar_prefetch=1,
            grid=(4,),
            in_specs=[
                pl.BlockSpec((512, 256), lambda i, info: (0, i)),
                pl.BlockSpec((512, 512), lambda i, info: (0, 0)),
                pl.BlockSpec((1, 256), lambda i, info: (0, i)),
                pl.BlockSpec((256, 512), lambda i, info: (i, 0)),
            ],
            out_specs=pl.BlockSpec((32, 32, 512), lambda i, info: (0, 0, 0)),
        ),
        out_shape=jax.ShapeDtypeStruct((32, 32, 512), BF),
        compiler_params=pltpu.CompilerParams(dimension_semantics=("arbitrary",), vmem_limit_bytes=16 * 2**20),
        cost_estimate=pl.CostEstimate(flops=2**29, bytes_accessed=4 * 2**20, transcendentals=0),
        name="numer",
    )(info, calib, model_out, diag, weights)


ORDER = (0, 7, 1, 6, 2, 5, 3, 4)
STEPS = (3, 3, 2)


def slot_model(info, core, slot):
    return slot * 2 + (info[5] ^ core)


def gram_kernel(first, last, info, *refs):
    refs = list(refs)
    blocks = [refs.pop(0) for _ in range(3)]
    own_s, other_s = refs.pop(0), refs.pop(0)
    if first:
        own_g, other_g = refs.pop(0), refs.pop(0)
    else:
        gains, before = refs.pop(0), refs.pop(0)
    if last:
        near, far = refs.pop(0), refs.pop(0)
    else:
        acc = refs.pop(0)
    if first:
        gains = refs.pop(0)
    if last:
        acc = refs.pop(0)
    table, pick, scale, calib = refs
    step = pl.program_id(0)

    @pl.when(step == 0)
    def _():
        if not first:
            acc[...] = before[...]
        else:
            acc[...] = jnp.zeros_like(acc)
            for core in range(2):
                src = own_g if core == 0 else other_g
                for slot in range(8):
                    m = slot_model(info, core, slot)
                    row = []
                    for b in (info[5], 2, 3):
                        tile = src[slot, b].astype(F4)
                        tile = tile[8:12] + tile[12:16]
                        row += [tile[i : i + 1] for i in range(4)]
                    gains[pl.ds(m, 1), :] = jnp.concatenate(row, 1)

    for i in range(2 if last else 3):

        @pl.when(step == i)
        def _(i=i):
            if last and i == 1:
                table[0:128, 0:512] = blocks[1][...]
                table[128:256, 0:512] = blocks[2][...]
            else:
                table[:, 0:512] = blocks[i][...]

    lane = lax.broadcasted_iota(jnp.int32, (64, 256), 1).astype(F4)
    models, tiles = [], []
    for core in range(2):
        src = own_s if core == 0 else other_s
        for slot in range(8):
            m = slot_model(info, core, slot)
            models.append(m)
            table[pl.ds(pl.multiple_of(m * 16, 16), 16), 512:1536] = src[slot, 0, :, 0:1024]
            tiles.append(src[slot, 0, :, 1024:1152])
    for m, (column, value) in enumerate(token_columns(tiles)):
        part = slice(m * 64, m * 64 + 64)
        pick[part, :] = jnp.where(column == lane, 1.0, 0.0).astype(BF)
        scale[part, :] = jnp.broadcast_to(value, (64, 128))

    for n in range(6):
        cols = slice(n * 256, n * 256 + 256)
        got = dot(pick[...], table[:, cols])
        for m in range(16):
            part = slice(m * 64, m * 64 + 64)
            r = scale[part, :]
            r = jnp.concatenate([r, r], 1)
            g = gains[pl.ds(models[m], 1), cols]
            calib[part, cols] = (got[part] * r * g).astype(BF)
    acc[...] += contract_rows(calib[:, 0:512], calib[:, 512:1536])

    if last:

        @pl.when(step == STEPS[-1] - 1)
        def _():
            near[...] = acc[:, 0:512]
            far[...] = acc[:, 512:1024].astype(BF)


def gram_call(i, info, blocks, own_s, other_s, gains, before):
    first, last = i == 0, i == len(STEPS) - 1
    start, steps = sum(STEPS[:i]), STEPS[i]
    whole = lambda shape: pl.BlockSpec(shape, lambda j, info: (0,) * len(shape))
    by_z = pl.BlockSpec((8, 1, 16, 1152), lambda j, info: (0, info[7 + start + j], 0, 0))
    gain_view = pl.BlockSpec((8, 8, 16, 128), lambda j, info: (0, 0, 0, 8))
    shapes = [jax.ShapeDtypeStruct((512, 1024), F4)]
    if last:
        shapes = [jax.ShapeDtypeStruct((512, 512), F4), jax.ShapeDtypeStruct((512, 512), BF)]
    if first:
        shapes.append(jax.ShapeDtypeStruct((16, 1536), F4))
    extra = [own_s, other_s] if first else [gains, before]
    extra_specs = [gain_view, gain_view] if first else [whole((16, 1536)), whole((512, 1024))]
    blocks = blocks[start : start + 3]
    operands = [info, *blocks, own_s, other_s, *extra]
    return pl.pallas_call(
        lambda *refs: gram_kernel(first, last, *refs),
        grid_spec=pltpu.PrefetchScalarGridSpec(
            num_scalar_prefetch=1,
            grid=(steps,),
            in_specs=[whole(b.shape) for b in blocks] + [by_z, by_z] + extra_specs,
            out_specs=[whole(o.shape) for o in shapes],
            scratch_shapes=([pltpu.VMEM((512, 1024), F4)] if last else [])
            + [
                pltpu.VMEM((256, 1536), BF),
                pltpu.VMEM((1024, 256), BF),
                pltpu.VMEM((1024, 128), F4),
                pltpu.VMEM((1024, 1536), BF),
            ],
        ),
        out_shape=shapes,
        input_output_aliases={} if first or last else {len(operands) - 1: 0},
        compiler_params=pltpu.CompilerParams(dimension_semantics=("arbitrary",), vmem_limit_bytes=VMEM),
        cost_estimate=pl.CostEstimate(flops=steps * 2**31, bytes_accessed=6 * 2**20, transcendentals=0),
        name="gram" + str(i),
    )(*operands)


def local(bank, calib_ids, norm_gains, proj_slabs):
    p = lax.axis_index("mp")
    s = lax.axis_index("shard")
    y, xh, c = p // 4, p // 2 % 2, p % 2
    z, xl = s // 2, s % 2
    info = jnp.stack([p, s, xl, y, xh, c, z] + [(z + k) % 8 for k in ORDER]).astype(jnp.int32)
    weights = proj_slabs[0]

    piece, bank_cols = prepare(info, bank, calib_ids)
    sent = address(info, swap_z(piece), norm_gains)
    own_s, other_s, both, blocks = gather(sent, weights, bank_cols)

    partial_out, calib, diag = project(info, own_s, other_s, norm_gains, both)
    tie = lax.optimization_barrier
    partial_out, info = tie((partial_out, info))
    acc, gains = gram_call(0, info, blocks, own_s, other_s, None, None)
    partial_out, gains = tie((swap_z(partial_out), gains))
    model_out = jnp.sum(partial_out.astype(F4), 0).astype(BF)
    model_out, info = tie((jnp.broadcast_to(model_out[None], (8, 64, 512)), info))
    (acc,) = gram_call(1, info, blocks, own_s, other_s, gains, acc)
    model_out, acc = tie((swap_z(model_out), acc))

    numer = numer_call(info, calib, model_out.reshape(512, 512), diag, both)
    numer, info = tie((numer, info))
    near, far = gram_call(2, info, blocks, own_s, other_s, gains, acc)
    numer, near = tie((lax.all_to_all(numer, AXES, 0, 0, tiled=True, axis_index_groups=XLO_GROUPS), near))
    numer = jnp.sum(numer.astype(F4), 0).astype(BF)
    numer = lax.all_to_all(jnp.broadcast_to(numer[None], (16, 32, 512)), "mp", 0, 0, tiled=True)
    numer = numer.reshape(512, 512).astype(F4)

    gram = near + shift(far, xl=1).astype(F4)
    on_diag = (p == s) & (
        lax.broadcasted_iota(jnp.int32, (512, 512), 0) == lax.broadcasted_iota(jnp.int32, (512, 512), 1)
    )
    merged_gram = gram * jnp.where(on_diag, 1.0 / 1024, ALPHA / 1024)

    return (merged_gram, numer)


def solution(mesh):
    placed = (P("shard", None), P("mp", "shard"), P("mp", None), P("mp", "shard", None))
    return jax.shard_map(
        local,
        mesh=mesh,
        in_specs=placed,
        out_specs=(P("mp", "shard"), P("shard", None)),
        check_vma=False,
    )
```
